512 devices in a mesh: gx: 16 (over y, core), gy: 32 (over z, x).
Axes of the slice: x: 4, y: 8, z: 8, core: 2. Of those that a mesh axis runs over, the one named last changes fastest.
Arguments:
- inputs: bfloat16 [256, 4, 2304], P('gy', None, 'gx'), may hold values from -8 to 8
- cache_pool: bfloat16 [2, 64, 4096, 1024], P(None, 'gx', 'gy'), may hold values from -6 to 6
- lengths: int32 [32], P('gy'), may hold values from 1 to 32768, as said below
- block_table: int32 [32, 33], P('gy'), may hold values from -1 to 63, as said below
- parents: int32 [3, 256], P(None, 'gy'), may hold values from 0 to 7
- norm_gains: float32 [4, 2304], P(None, 'gx'), may hold values from -0.5 to 1
- w_query: bfloat16 [2304, 2048], P('gx', 'gy'), may hold values from -0.125 to 0.125
- w_key: bfloat16 [2304, 1024], P('gx', 'gy'), may hold values from -0.125 to 0.125
- w_value: bfloat16 [2304, 1024], P('gx', 'gy'), may hold values from -0.125 to 0.125
- w_out: bfloat16 [2048, 2304], P('gy', 'gx'), may hold values from -1 to 1
- w_gate: bfloat16 [2304, 9216], P('gx', 'gy'), may hold values from -0.125 to 0.125
- w_up: bfloat16 [2304, 9216], P('gx', 'gy'), may hold values from -0.125 to 0.125
- w_down: bfloat16 [9216, 2304], P('gy', 'gx'), may hold values from -1 to 1
Outputs:
- outputs: bfloat16 [256, 4, 2304], P('gy', None, 'gx')
The draws below stay inside these ranges and needn't reach their ends.
Inputs may be any that keep to these rules, and one draw needn't show every extreme that they name: `lengths`: a group's beams share its prompt length. block_table[g, j] is the slot, numbered over the index of gy that holds group g as gx index times 4 plus the device's slot, of page first(g) + j of the group, for j up to (lengths[g] - 1) // 128 - first(g), and -1 beyond; no slot is named twice; a device holds at most 4 pages, and some device holds 4. Beam b at step s + 1 continues beam parents[s, b] of its own group, numbered within the group.
All inputs are finite; a program needn't handle non-finite values.
Results may differ from the reference program's by a relative error of at most 0.015.
Values may be sent and summed in bfloat16 or wider, within the bound.
A program may use at most 64 MiB of HBM per device.

```python
import math
import jax
import jax.numpy as jnp
from jax import lax

D = 2304
FF = 9216
HEADS = 8
KV_HEADS = 4
HEAD_DIM = 256
WINDOW = 4096
MAXLEN = 32768
PAGE = 128
BEAM = 8
STEPS = 4
GROUPS_DEV = 1
GROUPS = 32
BEAMS = 256
PAGES_MAX = 33
SLOTS = 4
POOL_SLOTS = 64
Q_WIDTH = 2048
KV_WIDTH = 1024
N_GY = 32


def permute_slots(key_item):
    return jax.random.permutation(key_item, POOL_SLOTS)


def group_layout(key):
    key_one = jax.random.fold_in(key, 101)
    key_two = jax.random.fold_in(key, 102)
    key_three = jax.random.fold_in(key, 103)
    key_four = jax.random.fold_in(key, 104)
    key_five = jax.random.fold_in(key, 105)
    key_six = jax.random.fold_in(key, 106)
    shifts = jax.random.randint(key_one, (GROUPS,), 0, 8)
    top_lengths = jnp.right_shift(jnp.full((GROUPS,), MAXLEN, jnp.int32), shifts)
    half_tops = top_lengths // 2
    offsets = jax.random.randint(key_two, (GROUPS,), 0, half_tops)
    group_lengths = half_tops + offsets
    longest = jax.random.randint(key_three, (), 0, GROUPS)
    second = (longest + 1 + jax.random.randint(key_four, (), 0, GROUPS - 1)) % GROUPS
    group_ids = jnp.arange(GROUPS, dtype=jnp.int32)
    group_lengths = jnp.where(group_ids == longest, MAXLEN, group_lengths)
    group_lengths = jnp.where(group_ids == second, MAXLEN - PAGE // 2, group_lengths)
    first_page = jnp.maximum(group_lengths - WINDOW + 1, 0) // PAGE
    last_page = (group_lengths - 1) // PAGE
    page_counts = last_page - first_page + 1
    column_count = GROUPS // GROUPS_DEV
    per_column = page_counts.reshape(column_count, GROUPS_DEV)
    first_flat = jnp.cumsum(per_column, axis=1) - per_column
    rank_rows = jax.vmap(permute_slots)(jax.random.split(key_five, column_count)).astype(jnp.int32)
    hot_device = jax.random.randint(key_six, (column_count, 1), 0, POOL_SLOTS // SLOTS)
    owner_dev = jnp.arange(POOL_SLOTS, dtype=jnp.int32) // SLOTS
    slot_scores = rank_rows + POOL_SLOTS * (owner_dev[None, :] != hot_device).astype(jnp.int32)
    slot_order = jnp.argsort(slot_scores, axis=1, stable=True).astype(jnp.int32)
    flat_index = first_flat.reshape(GROUPS, 1) + jnp.arange(PAGES_MAX, dtype=jnp.int32)[None, :]
    column_ids = group_ids // GROUPS_DEV
    picked = slot_order[column_ids[:, None], jnp.minimum(flat_index, POOL_SLOTS - 1)]
    block_rows = jnp.where(jnp.arange(PAGES_MAX, dtype=jnp.int32)[None, :] < page_counts[:, None], picked, -1)
    return (group_lengths.astype(jnp.int32), block_rows.astype(jnp.int32))


def draw_lengths(key, part):
    return group_layout(key)[0]


def draw_block_table(key, part):
    return group_layout(key)[1]


def common_direction(key):
    return jax.random.normal(jax.random.fold_in(key, 301), (D,), jnp.float32)


def draw_inputs(key, part):
    column_frac = jnp.arange(D, dtype=jnp.float32) / D
    direction = common_direction(key)
    loadings = jax.random.normal(jax.random.fold_in(key, 10), (BEAMS, STEPS, 1), jnp.float32)
    base_draw = jax.random.normal(jax.random.fold_in(key, 9), (BEAMS, STEPS, D), jnp.float32)
    mixed_draw = base_draw * math.sqrt(0.7) + loadings * direction * math.sqrt(0.3)
    values = mixed_draw * jnp.exp(column_frac * math.log(3.0)) / 1.7
    return jnp.clip(values, -8.0, 8.0).astype(jnp.bfloat16)


def draw_w_out(key, part):
    column_frac = jnp.arange(D, dtype=jnp.float32) / D
    direction = common_direction(key)
    loadings = jax.random.normal(jax.random.fold_in(key, 23), (Q_WIDTH, 1), jnp.float32)
    base_draw = jax.random.normal(jax.random.fold_in(key, 22), (Q_WIDTH, D), jnp.float32)
    mixed_draw = base_draw * math.sqrt(0.7) + loadings * direction * math.sqrt(0.3)
    values = mixed_draw * jnp.exp(column_frac * math.log(3.0)) / 1.9
    return jnp.clip(values * (1.0 / math.sqrt(Q_WIDTH)), -1.0, 1.0).astype(jnp.bfloat16)


def draw_w_down(key, part):
    column_frac = jnp.arange(D, dtype=jnp.float32) / D
    direction = jax.random.normal(jax.random.fold_in(key, 302), (D,), jnp.float32)
    loadings = jax.random.normal(jax.random.fold_in(key, 33), (FF, 1), jnp.float32)
    base_draw = jax.random.normal(jax.random.fold_in(key, 32), (FF, D), jnp.float32)
    mixed_draw = base_draw * math.sqrt(0.7) + loadings * direction * math.sqrt(0.3)
    values = mixed_draw * jnp.exp(column_frac * math.log(3.0)) / 1.9
    return jnp.clip(values * (1.0 / math.sqrt(FF)), -1.0, 1.0).astype(jnp.bfloat16)


def with_ends(entries, stream_key, least, high):
    place = [jax.random.randint(jax.random.fold_in(stream_key, axis), (), 0, length) for axis, length in enumerate(entries.shape)]
    widest = entries.shape.index(max(entries.shape))
    next_to = place[:widest] + [(place[widest] + 1) % entries.shape[widest]] + place[widest + 1:]
    return entries.at[tuple(place)].set(least).at[tuple(next_to)].set(high)


def block_levels(key, dims, pieces, least, largest):
    def one(dim, parts):
        heights = jax.random.uniform(jax.random.fold_in(jax.random.fold_in(key, 6), dim), (parts,), jnp.float32, least / len(pieces), largest / len(pieces))
        return jnp.repeat(jnp.exp(heights), dims[dim] // parts).reshape((-1,) + (1,) * (len(dims) - dim - 1))

    loudness = one(*pieces[0])
    for cut in pieces[1:]:
        loudness = loudness * one(*cut)
    return loudness


def noise(rng, dims, scale, most, cuts=(), held_as=jnp.bfloat16):
    entries = scale * jax.random.normal(rng, dims, jnp.float32)
    if cuts:
        entries = entries * block_levels(rng, dims, cuts, -0.22, 0.18)
    return jnp.clip(entries, -most, most).astype(held_as)


def setup_inputs(seed: int = 0) -> dict:
    key_of = jax.random.split(jax.random.key(seed), 14)
    return {
        "inputs": draw_inputs(jax.random.fold_in(key_of[13], 71), 0),
        "cache_pool": noise(key_of[1], (2, POOL_SLOTS, N_GY * PAGE, KV_WIDTH), 1.0, 6.0, ((1, 16), (2, 32))),
        "lengths": draw_lengths(jax.random.fold_in(key_of[13], 71), 0),
        "block_table": draw_block_table(jax.random.fold_in(key_of[13], 71), 0),
        "parents": with_ends(jax.random.randint(key_of[4], (STEPS - 1, BEAMS), 0, BEAM), jax.random.fold_in(key_of[4], 1), 0, BEAM - 1).astype(jnp.int32),
        "norm_gains": jnp.clip(-0.5 + 1.5 * jax.random.uniform(key_of[5], (4, D), jnp.float32) ** block_levels(key_of[5], (4, D), ((1, 16),), -0.2, 0.2), -0.5, 1.0),
        "w_query": noise(key_of[6], (D, Q_WIDTH), D ** -0.5, 0.125, ((0, 16), (1, 32))),
        "w_key": noise(key_of[7], (D, KV_WIDTH), D ** -0.5, 0.125, ((0, 16), (1, 32))),
        "w_value": noise(key_of[8], (D, KV_WIDTH), D ** -0.5, 0.125, ((0, 16), (1, 32))),
        "w_out": draw_w_out(jax.random.fold_in(key_of[13], 71), 0),
        "w_gate": noise(key_of[10], (D, FF), D ** -0.5, 0.125, ((0, 16), (1, 32))),
        "w_up": noise(key_of[11], (D, FF), D ** -0.5, 0.125, ((0, 16), (1, 32))),
        "w_down": draw_w_down(jax.random.fold_in(key_of[13], 71), 0),
    }


EPSILON = 1e-06
SOFT_CAP = 50.0
ROPE_BASE = 10000.0

def row_scale(values):
    return lax.rsqrt(lax.optimization_barrier(jnp.mean(values * values, axis=-1, keepdims=True)) + EPSILON)

def rotate(values, positions):
    half_width = values.shape[-1] // 2
    inverse_freq = ROPE_BASE ** (-jnp.arange(half_width, dtype=jnp.float32) * 2.0 / values.shape[-1])
    angles = positions[..., None].astype(jnp.float32) * inverse_freq
    cosine = jnp.cos(angles)[..., None, :]
    sine_part = jnp.sin(angles)[..., None, :]
    first_half = values[..., :half_width]
    second_half = values[..., half_width:]
    return jnp.concatenate([first_half * cosine - second_half * sine_part, second_half * cosine + first_half * sine_part], axis=-1)

def ancestry(parents, beam_count, group_size, steps_count):
    beam_ids = jnp.arange(beam_count, dtype=jnp.int32)
    group_base = beam_ids // group_size * group_size
    table_rows = []
    for moment in range(steps_count):
        current = beam_ids
        chain_list = [beam_ids] * steps_count
        for earlier in range(moment, 0, -1):
            current = group_base + jnp.take(parents[earlier - 1], current)
            chain_list[earlier - 1] = current
        table_rows.append(jnp.stack(chain_list))
    return jnp.stack(table_rows)

def tail_terms(grouped, key_steps, value_steps, ancestors):
    steps_count = grouped.shape[1]
    step_ids = jnp.arange(steps_count, dtype=jnp.int32)
    tail_keys = key_steps[ancestors, step_ids[None, :, None]]
    tail_values = value_steps[ancestors, step_ids[None, :, None]]
    scores = jnp.einsum('bskgd,sjbkd->bskgj', grouped.astype(jnp.float32), tail_keys.astype(jnp.float32))
    allowed = step_ids[None, :] <= step_ids[:, None]
    weights = jnp.where(allowed[None, :, None, None, :], jnp.exp(SOFT_CAP * jnp.tanh(scores / SOFT_CAP)), 0.0)
    rounded = lax.optimization_barrier(weights.astype(jnp.bfloat16)).astype(jnp.float32)
    numerator = jnp.einsum('bskgj,sjbkd->bskgd', rounded, tail_values.astype(jnp.float32))
    return (numerator, lax.optimization_barrier(jnp.sum(weights, axis=-1)))

def reference(inputs, cache_pool, lengths, block_table, parents, norm_gains, w_query, w_key, w_value, w_out, w_gate, w_up, w_down):
    x_wide = inputs.astype(jnp.float32)
    gain_rows = 1.0 + norm_gains.astype(jnp.float32)
    normed = (x_wide * row_scale(x_wide) * gain_rows[0]).astype(jnp.bfloat16)
    matrix_rows = normed.reshape(BEAMS * STEPS, D)
    query_raw = jnp.dot(matrix_rows, w_query, preferred_element_type=jnp.float32).reshape(BEAMS, STEPS, HEADS, HEAD_DIM)
    key_raw = jnp.dot(matrix_rows, w_key, preferred_element_type=jnp.float32).reshape(BEAMS, STEPS, KV_HEADS, HEAD_DIM)
    value_raw = jnp.dot(matrix_rows, w_value, preferred_element_type=jnp.float32).reshape(BEAMS, STEPS, KV_HEADS, HEAD_DIM)
    beam_lengths = jnp.repeat(lengths, BEAM)
    positions = beam_lengths[:, None] + jnp.arange(STEPS, dtype=jnp.int32)[None, :]
    queries = (rotate(query_raw, positions) * HEAD_DIM ** (-0.5)).astype(jnp.bfloat16)
    key_steps = rotate(key_raw, positions).astype(jnp.bfloat16)
    value_steps = value_raw.astype(jnp.bfloat16)
    grouped = queries.reshape(BEAMS, STEPS, KV_HEADS, HEADS // KV_HEADS, HEAD_DIM)
    ancestors = ancestry(parents, BEAMS, BEAM, STEPS)
    tail_num, tail_den = tail_terms(grouped, key_steps, value_steps, ancestors)
    group_queries = grouped.reshape(GROUPS, BEAM, STEPS, KV_HEADS, HEADS // KV_HEADS, HEAD_DIM)

    def one_group(operands):
        group_query, length, slot_list, column = operands
        column_pool = lax.dynamic_slice_in_dim(cache_pool, (column * PAGE).astype(jnp.int32), PAGE, 2)
        valid_page = slot_list >= 0
        page_rows = jnp.take(column_pool, jnp.maximum(slot_list, 0), axis=1)
        key_rows = page_rows[0].reshape(PAGES_MAX * PAGE, KV_HEADS, HEAD_DIM)
        value_rows = page_rows[1].reshape(PAGES_MAX * PAGE, KV_HEADS, HEAD_DIM)
        first_page = jnp.maximum(length - WINDOW + 1, 0) // PAGE
        key_positions = ((first_page + jnp.arange(PAGES_MAX, dtype=jnp.int32))[:, None] * PAGE + jnp.arange(PAGE, dtype=jnp.int32)[None, :]).reshape(-1)
        page_valid = jnp.repeat(valid_page, PAGE)
        lower_bound = length + jnp.arange(STEPS, dtype=jnp.int32) - WINDOW + 1
        visible = page_valid[None, :] & (key_positions[None, :] < length) & (key_positions[None, :] >= lower_bound[:, None])
        scores = jnp.einsum('bskgd,tkd->bskgt', group_query.astype(jnp.float32), key_rows.astype(jnp.float32))
        weights = jnp.where(visible[None, :, None, None, :], jnp.exp(SOFT_CAP * jnp.tanh(scores / SOFT_CAP)), 0.0)
        rounded = lax.optimization_barrier(weights.astype(jnp.bfloat16)).astype(jnp.float32)
        numerator = jnp.einsum('bskgt,tkd->bskgd', rounded, value_rows.astype(jnp.float32))
        return (numerator, lax.optimization_barrier(jnp.sum(weights, axis=-1)))
    columns = jnp.arange(GROUPS, dtype=jnp.int32) // GROUPS_DEV
    prefix_num, prefix_den = lax.map(one_group, (group_queries, lengths, block_table, columns))
    numerator = prefix_num.reshape(BEAMS, STEPS, KV_HEADS, HEADS // KV_HEADS, HEAD_DIM) + tail_num
    denominator = prefix_den.reshape(BEAMS, STEPS, KV_HEADS, HEADS // KV_HEADS) + tail_den
    attended = (numerator / denominator[..., None]).astype(jnp.bfloat16).reshape(BEAMS * STEPS, HEADS * HEAD_DIM)
    attn_full = jnp.dot(attended, w_out, preferred_element_type=jnp.float32).reshape(BEAMS, STEPS, D)
    mixed_full = x_wide + attn_full * row_scale(attn_full) * gain_rows[1]
    ff_input = (mixed_full * row_scale(mixed_full) * gain_rows[2]).astype(jnp.bfloat16).reshape(BEAMS * STEPS, D)
    gate_part = jnp.dot(ff_input, w_gate, preferred_element_type=jnp.float32)
    up_part = jnp.dot(ff_input, w_up, preferred_element_type=jnp.float32)
    hidden = (jax.nn.gelu(gate_part, approximate=True) * up_part).astype(jnp.bfloat16)
    down_full = jnp.dot(hidden, w_down, preferred_element_type=jnp.float32).reshape(BEAMS, STEPS, D)
    return (mixed_full + down_full * row_scale(down_full) * gain_rows[3]).astype(jnp.bfloat16)
```

```python
import functools
import math

import jax
import jax.numpy as jnp
from jax import lax
from jax.experimental import pallas as pl
from jax.experimental.pallas import tpu as pltpu
from jax.sharding import PartitionSpec as P

MESH = pl.DeviceIdType.MESH
F32 = jnp.float32
BF16 = jnp.bfloat16

HEAD_DIM = 256
WINDOW = 4096
PAGE = 128
BEAM = 8
STEPS = 4
ROWS = BEAM * STEPS
EPSILON = 1e-06
SOFT_CAP = 50.0
ROPE_BASE = 10000.0
MAIN = 128
REST = 16

QKV_ROWS = 144
A_ROWS = 160
OUT_AT = 0
OUT_REST_AT = 64
GATE_AT = 80
DOWN_AT = 800
DOWN_REST_AT = 1088
F_ROWS = 1136
CUT = 576


def capped(scores):
    return jnp.exp(SOFT_CAP * jnp.tanh(scores * (1.0 / SOFT_CAP)))


def gelu(v):
    return 0.5 * v * (1.0 + jnp.tanh(math.sqrt(2.0 / math.pi) * (v + 0.044715 * (v * v * v))))


def dot(a, b):
    return jnp.dot(a, b, preferred_element_type=F32)


def dot_nt(a, b):
    return lax.dot_general(a, b, (((1,), (1,)), ((), ())), preferred_element_type=F32)


def layer_kernel(
    nx, ny, width,
    x_ref, wa_ref, wf_ref, cache_ref, trig_ref, table_ref, length_ref, parents_ref,
    out_ref,
    wa_all, wf_all, gain_main, gain_rest, x_in, x_own, row_out, row_all, ff_all, norm_in,
    qkv_out, qkv_in, cache, num_out, num_in, part_out, part_in, down_in, last_out, last_in,
    mixed, sums,
    cache_sem, own_sem, wa_send, wa_recv, wa_core_send, ring_send, ring_recv, wa_core_recv, wf_core_send, wf_core_recv,
    x_send, x_recv, row_send, row_recv, qkv_send, qkv_recv, num_send, num_recv,
    part_send, part_recv, ff_send, ff_recv, down_send, down_recv, last_send, last_recv,
):
    ys = nx // 2
    zs = ny // 4
    heads = ny // 4
    kv_heads = ny // 8
    tiles = nx + nx // 8 if nx >= 8 else nx + 1
    rest_tiles = tiles - nx
    blocks = 8
    i = lax.axis_index("gx")
    j = lax.axis_index("gy")
    y, c = i // 2, i % 2
    sibling = i + 1 - 2 * c
    piece = c * ys + y
    zj, xj = j // 4, j % 4
    chunk = 2 * ((zj + 2 * xj) % ys) + xj % 2
    half = xj // 2

    def group_of(part):
        x_r = 2 * part + c
        return ((y + 8 * ys - 2 * x_r) % ys) * 4 + x_r

    def owner_of(core, block):
        return 4 * block + 2 * core + block % 2 if zs == 8 else block

    if zs == 8:
        is_owner = (xj // 2 == c) & (xj % 2 == zj % 2)
        my_block = zj
    else:
        is_owner = j >= 0
        my_block = j

    def remote(src, dst, send_sem, recv_sem, tx, ty):
        return pltpu.make_async_remote_copy(
            src_ref=src, dst_ref=dst, send_sem=send_sem, recv_sem=recv_sem,
            device_id=(tx, ty), device_id_type=MESH,
        )

    def put(src, dst, send_sem, recv_sem, tx, ty):
        own = (tx == i) & (ty == j)

        @pl.when(jnp.logical_not(own))
        def _():
            remote(src, dst, send_sem, recv_sem, tx, ty).start()

        @pl.when(own)
        def _():
            pltpu.make_async_copy(src, dst, recv_sem).start()

    def take(ref, sem):
        pltpu.make_async_copy(ref, ref, sem).wait()

    def take_sent(ref, count, sem, own):
        @pl.when(own)
        def _():
            take(ref.at[pl.ds(0, count - 1)], sem)

        @pl.when(jnp.logical_not(own))
        def _():
            take(ref.at[pl.ds(0, count)], sem)

    cache_copy = pltpu.make_async_copy(cache_ref, cache, cache_sem)
    cache_copy.start()
    core_of_chunk = chunk % 2
    for q in range(4):
        put(x_ref.at[q], x_in.at[piece], x_send, x_recv, chunk, owner_of(core_of_chunk, half * 4 + q))
    for step in range(1, ys):
        remote(wa_ref, wa_all.at[c, y], wa_send, wa_recv, 2 * ((y + step) % ys) + c, j).start()
    pltpu.make_async_copy(wa_ref, wa_all.at[c, y], wa_recv).start()

    right = 2 * ((y + 1) % ys) + c
    left = 2 * ((y + ys - 1) % ys) + c
    last_step = ys // 2

    def ring_refs(step):
        from_left = (y + ys - (step - 1)) % ys
        from_right = (y + (step - 1)) % ys
        return from_left, from_right

    def ring_start(step):
        a, b = ring_refs(step)
        src_a = wf_ref if step == 1 else wf_all.at[c, a]
        src_b = wf_ref if step == 1 else wf_all.at[c, b]
        dst_a, dst_b = wf_all.at[c, a], wf_all.at[c, b]
        if step == last_step:
            src_a, dst_a = src_a.at[pl.ds(0, CUT)], dst_a.at[pl.ds(0, CUT)]
            src_b, dst_b = src_b.at[pl.ds(CUT, F_ROWS - CUT)], dst_b.at[pl.ds(CUT, F_ROWS - CUT)]
        remote(src_a, dst_a, ring_send.at[2 * step - 2], ring_recv.at[2 * step - 2], right, j).start()
        remote(src_b, dst_b, ring_send.at[2 * step - 1], ring_recv.at[2 * step - 1], left, j).start()

    def to_sibling(k):
        remote(wf_all.at[c, k], wf_all.at[c, k], wf_core_send, wf_core_recv, sibling, j).start()

    def ring_take(step):
        a = (y + ys - step) % ys
        b = (y + step) % ys
        ref_a, ref_b = wf_all.at[c, a], wf_all.at[c, b]
        if step == last_step:
            take(ref_a.at[pl.ds(0, CUT)], ring_recv.at[2 * step - 2])
            take(ref_b.at[pl.ds(CUT, F_ROWS - CUT)], ring_recv.at[2 * step - 1])
            to_sibling(a)
        else:
            take(ref_a, ring_recv.at[2 * step - 2])
            take(ref_b, ring_recv.at[2 * step - 1])
            ring_start(step + 1)
            to_sibling(a)
            to_sibling(b)

    ring_start(1)
    remote(wf_ref, wf_all.at[c, y], wf_core_send, wf_core_recv, sibling, j).start()
    own_copy = pltpu.make_async_copy(wf_ref, wf_all.at[c, y], own_sem)
    own_copy.start()

    def rest_sum(pieces):
        out = []
        for t in range(rest_tiles):
            total = None
            for k in range(min(8, nx)):
                v = pieces[8 * t + k]
                v = pltpu.roll(v, REST * k, 1) if k else v
                total = v if total is None else total + v
            out.append(total)
        return out

    def spread(which, dst_all, send_sem, recv_sem):
        @pl.loop(1, ny)
        def _(step):
            remote(row_out.at[which], dst_all.at[my_block], send_sem, recv_sem, i, (j + step) % ny).start()

        pltpu.make_async_copy(row_out.at[which], dst_all.at[my_block], recv_sem).start()

    @pl.when(is_owner)
    def _():
        take(x_in, x_recv)
        rests = []
        for p in range(nx):
            v = x_in[p].astype(F32)
            x_own[:, MAIN * p:MAIN * (p + 1)] = v[:, 0:MAIN]
            rests.append(v[:, MAIN:2 * MAIN])
        for t, v in enumerate(rest_sum(rests)):
            x_own[:, MAIN * (nx + t):MAIN * (nx + t + 1)] = v
        row_out[0] = x_own[...].astype(BF16)
        spread(0, row_all, row_send, row_recv)

    take(wa_all.at[c], wa_recv)
    remote(wa_all.at[c], wa_all.at[c], wa_core_send, wa_core_recv, sibling, j).start()
    take(wa_all.at[1 - c], wa_core_recv)
    rests = []
    for p in range(nx):
        v = wa_all[p // ys, p % ys, QKV_ROWS:A_ROWS, :].astype(F32)
        v = v[0:8] + v[8:16]
        gain_main[p] = v
        rests.append(v)
    for t, v in enumerate(rest_sum(rests)):
        gain_rest[t] = v

    def gain(which, t):
        if t < nx:
            return gain_main[t, which:which + 1, :]
        return gain_rest[t - nx, 4 + which:5 + which, :]

    if last_step > 1:
        ring_take(1)

    take(row_all, row_recv)

    def chunk_tile(ref, t):
        at = slice(MAIN * t, MAIN * (t + 1))
        return jnp.concatenate([ref[k, :, at].astype(F32) for k in range(blocks)], axis=0)

    total = None
    for t in range(tiles):
        v = chunk_tile(row_all, t)
        total = v * v if total is None else total + v * v
    scale = lax.rsqrt(jnp.sum(total, axis=1, keepdims=True) / width + EPSILON)
    for t in range(tiles):
        v = chunk_tile(row_all, t)
        norm_in[:, MAIN * t:MAIN * (t + 1)] = (v * scale * gain(0, t)).astype(BF16)
    main_w = wa_all[:, :, 0:MAIN, :].reshape(nx * MAIN, 128)
    rest_w = wa_all[:, :, MAIN:QKV_ROWS, :].reshape(nx * REST, 128)
    qkv = dot(norm_in[:, 0:nx * MAIN], main_w) + dot(norm_in[:, nx * MAIN:nx * MAIN + nx * REST], rest_w)
    qkv = qkv.astype(BF16)
    qkv_out[0] = qkv[0:ROWS]
    qkv_out[1] = qkv[ROWS:2 * ROWS]

    for part in range(2):
        group = group_of(part)

        @pl.loop(0, nx)
        def _(step):
            put(qkv_out.at[part], qkv_in.at[j], qkv_send, qkv_recv, (i + step) % nx, group)

    if last_step > 2:
        ring_take(2)

    row = lax.broadcasted_iota(jnp.int32, (ROWS, 1), 0)
    row_step, row_beam = row & 3, jnp.right_shift(row, 2)
    length = length_ref[...]
    first_page = jnp.right_shift(jnp.maximum(length - (WINDOW - 1), 0), 7).astype(F32)
    length_wide = length.astype(F32)
    page_iota = lax.broadcasted_iota(jnp.int32, table_ref.shape, 1).astype(F32)
    lane = lax.broadcasted_iota(jnp.int32, (ROWS, PAGE), 1)
    lane_wide = lane.astype(F32)
    lowest = row_step.astype(F32) - (WINDOW - 1)
    masks = []
    for slot in range(4):
        match = table_ref[...] == i * 4 + slot
        page = jnp.sum(jnp.where(match, page_iota, 0.0), axis=1, keepdims=True)
        used = jnp.sum(jnp.where(match, 1.0, 0.0), axis=1, keepdims=True)
        start = jnp.where(used > 0.5, (first_page + page) * PAGE - length_wide, 1.0)
        place = start + lane_wide
        mask = jnp.where((place < 0.0) & (place >= lowest), 1.0, 0.0)
        masks.append(jnp.concatenate([mask, mask], axis=0) > 0.5)
    key_lane = lax.broadcasted_iota(jnp.int32, (ROWS, ROWS), 1)
    key_step, key_beam = key_lane & 3, jnp.right_shift(key_lane, 2)
    beam_lane = lax.broadcasted_iota(jnp.int32, (ROWS, BEAM), 1)
    current = row_beam
    tail = jnp.zeros((ROWS, ROWS), F32)
    for at in range(STEPS - 1, -1, -1):
        hit = (key_step == at) & (row_step >= at) & (key_beam == current)
        tail = jnp.where(hit, 1.0, tail)
        if at:
            chosen = jnp.where(beam_lane == current, parents_ref[at - 1:at, :].astype(F32), 0.0)
            parent = jnp.sum(chosen, axis=1, keepdims=True).astype(jnp.int32)
            current = jnp.where(row_step >= at, parent, current)
    tail = jnp.where(i == 0, tail, 0.0)
    tail_mask = jnp.concatenate([tail, tail], axis=0) > 0.5

    cosine, sine = trig_ref[0], trig_ref[1]
    cache_copy.wait()
    take(qkv_in, qkv_recv)

    def quarter(source, at, parts):
        span = 128 // parts
        total = None
        for m in range(parts):
            v = qkv_in[source + m].astype(F32)
            shift = (span * m - at) % 128
            v = pltpu.roll(v, shift, 1) if shift else v
            total = v if total is None else jnp.where(lane >= span * m, v, total)
        return total

    def rotated(u, w):
        return u * cosine - w * sine, w * cosine + u * sine

    def wide(u, w):
        return jnp.concatenate([u, w], axis=1)

    for h in range(kv_heads):
        qs = []
        for g in range(2):
            base = 4 * (2 * h + g)
            u, w = rotated(quarter(base, 0, 2), quarter(base + 2, 0, 2))
            qs.append(wide(u, w) * HEAD_DIM ** -0.5)
        query = jnp.concatenate(qs, axis=0).astype(BF16)
        key = wide(*rotated(quarter(8 * h, 64, 4), quarter(8 * h + 4, 64, 4))).astype(BF16)
        value = wide(quarter(8 * h, 96, 4), quarter(8 * h + 4, 96, 4)).astype(BF16)
        weights = jnp.where(tail_mask, capped(dot_nt(query, key)), 0.0)
        den = jnp.sum(weights, axis=1, keepdims=True)
        num = dot(weights.astype(BF16), value)
        for slot in range(4):
            at = slice(HEAD_DIM * h, HEAD_DIM * (h + 1))
            weights = jnp.where(masks[slot], capped(dot_nt(query, cache[0, slot, :, at])), 0.0)
            den = den + jnp.sum(weights, axis=1, keepdims=True)
            num = num + dot(weights.astype(BF16), cache[1, slot, :, at])
        den_high = den.astype(BF16).astype(F32)
        den_low = den - den_high
        for g in range(2):
            rows = slice(ROWS * g, ROWS * (g + 1))
            both = jnp.where(lane < 96, den_high[rows], den_low[rows])
            for t in range(2):
                v = num[rows, 128 * t:128 * (t + 1)]
                base = 4 * (2 * h + g) + 2 * t
                num_out[base] = jnp.where(lane < 64, v, both).astype(BF16)
                num_out[base + 1] = jnp.where(lane < 64, pltpu.roll(v, 64, 1), both).astype(BF16)

    @pl.loop(0, ny)
    def _(step):
        to = (j + step) % ny
        put(num_out.at[to], num_in.at[half, piece], num_send, num_recv, chunk, to)

    for step in range(3, last_step):
        ring_take(step)
    own_copy.wait()

    take(num_in, num_recv)
    attended = []
    for part in range(2):
        total = None
        for p in range(nx):
            v = num_in[part, p].astype(F32)
            total = v if total is None else total + v
        attended.append(total[:, 0:64] / (total[:, 64:65] + total[:, 96:97]))
    attended = jnp.concatenate(attended, axis=0).astype(BF16)
    ring_take(last_step)
    take(wf_all.at[1 - c], wf_core_recv)

    def put_partial(which, t, v):
        for k in range(blocks):
            part_out[which, k, :, MAIN * t:MAIN * (t + 1)] = v[8 * k:8 * (k + 1)].astype(BF16)

    def put_rest(which, v):
        if v.shape[1] < 128:
            v = jnp.concatenate([v, jnp.zeros((v.shape[0], 128 - v.shape[1]), F32)], axis=1)
        for t in range(rest_tiles):
            put_partial(which, nx + t, v[:, 128 * t:128 * (t + 1)])

    for p in range(nx):
        put_partial(0, p, dot(attended, wf_all[p // ys, p % ys, OUT_AT:OUT_REST_AT, :]))
    rest_w = wf_all[:, :, OUT_REST_AT:GATE_AT, :].reshape(nx * REST, 128)
    put_rest(0, dot_nt(attended, rest_w[:, 0:64]))

    def send_partial(which, dst_all, send_sem, recv_sem):
        @pl.loop(0, blocks)
        def _(k):
            put(part_out.at[which, k], dst_all.at[j], send_sem, recv_sem, i, owner_of(c, k))

    def add_up(ref, t):
        total = None
        for s in range(ny):
            v = ref[s, :, MAIN * t:MAIN * (t + 1)].astype(F32)
            total = v if total is None else total + v
        return total

    def add_rows(ref):
        square = None
        for t in range(tiles):
            v = add_up(ref, t)
            sums[:, MAIN * t:MAIN * (t + 1)] = v
            square = v * v if square is None else square + v * v
        return lax.rsqrt(jnp.sum(square, axis=1, keepdims=True) / width + EPSILON)

    send_partial(0, part_in, part_send, part_recv)

    @pl.when(is_owner)
    def _():
        take(part_in, part_recv)
        scale = add_rows(part_in)
        square = None
        for t in range(tiles):
            at = slice(MAIN * t, MAIN * (t + 1))
            v = x_own[:, at] + sums[:, at] * scale * gain(1, t)
            mixed[:, at] = v
            square = v * v if square is None else square + v * v
        scale = lax.rsqrt(jnp.sum(square, axis=1, keepdims=True) / width + EPSILON)
        for t in range(tiles):
            at = slice(MAIN * t, MAIN * (t + 1))
            row_out[1, :, at] = (mixed[:, at] * scale * gain(2, t)).astype(BF16)

        spread(1, ff_all, ff_send, ff_recv)

    take(ff_all, ff_recv)
    for t in range(tiles):
        norm_in[:, MAIN * t:MAIN * (t + 1)] = chunk_tile(ff_all, t).astype(BF16)
    main_x = norm_in[:, 0:nx * MAIN]
    rest_x = norm_in[:, nx * MAIN:nx * MAIN + nx * REST]

    def ff_part(n):
        at = GATE_AT + 144 * n
        main_w = wf_all[:, :, at:at + MAIN, :].reshape(nx * MAIN, 128)
        rest_w = wf_all[:, :, at + MAIN:at + 144, :].reshape(nx * REST, 128)
        return dot(main_x, main_w) + dot(rest_x, rest_w)

    hidden = [(gelu(ff_part(n)) * ff_part(n + 2)).astype(BF16) for n in range(2)]
    both = ff_part(4)
    narrow = gelu(both) * pltpu.roll(both, 96, 1)
    lane_chunk = lax.broadcasted_iota(jnp.int32, narrow.shape, 1)
    hidden.append(jnp.where(lane_chunk < 32, narrow, 0.0).astype(BF16))
    first_hidden = jnp.concatenate(hidden[0:2], axis=1)
    for p in range(nx):
        w = wf_all.at[p // ys, p % ys]
        v = dot(first_hidden, w[DOWN_AT:DOWN_AT + 256, :])
        v = v + dot(hidden[2][:, 0:32], w[DOWN_AT + 256:DOWN_REST_AT, :])
        put_partial(1, p, v)
    v = None
    for n in range(3):
        at = DOWN_REST_AT + REST * n
        rest_w = wf_all[:, :, at:at + REST, :].reshape(nx * REST, 128)
        term = dot_nt(hidden[n], rest_w)
        v = term if v is None else v + term
    put_rest(1, v)
    send_partial(1, down_in, down_send, down_recv)

    @pl.when(is_owner)
    def _():
        take(down_in, down_recv)
        scale = add_rows(down_in)

        def result(t):
            at = slice(MAIN * t, MAIN * (t + 1))
            return mixed[:, at] + sums[:, at] * scale * gain(3, t)

        for p in range(nx):
            v = result(nx + p // 8)
            shift = (128 - REST * (p % 8)) % 128
            v = pltpu.roll(v, shift, 1) if shift else v
            last_out[p] = jnp.concatenate([result(p), v], axis=1).astype(BF16)
        group = group_of(my_block // 4)

        @pl.loop(0, nx)
        def _(p):
            to = 2 * (p % ys) + p // ys
            put(last_out.at[p], last_in.at[my_block % 4], last_send, last_recv, to, group)

    take(last_in, last_recv)
    out_ref[...] = last_in[...]

    home = chunk == i
    take_sent(x_in, 4, x_send, home & is_owner & (my_block // 4 == half))
    if ys > 1:
        take(wa_all.at[c, pl.ds(0, ys - 1)], wa_send)
    take(wa_all.at[c], wa_core_send)
    for step in range(1, last_step + 1):
        for side in range(2):
            rows = pl.ds(0, F_ROWS) if step < last_step else pl.ds(CUT * side, F_ROWS - CUT if side else CUT)
            take(wf_all.at[0, 0, rows], ring_send.at[2 * step - 2 + side])
    take(wf_all.at[c], wf_core_send)
    take_sent(qkv_in, ny, qkv_send, home)
    take_sent(num_out, ny, num_send, home)
    take_sent(row_all, blocks, part_send, is_owner)
    take_sent(ff_all, blocks, down_send, is_owner)

    @pl.when(is_owner)
    def _():
        take(part_in.at[pl.ds(0, ny - 1)], row_send)
        take(down_in.at[pl.ds(0, ny - 1)], ff_send)
        take_sent(x_in, nx, last_send, home & (my_block // 4 == half))


def body(
    inputs, cache_pool, lengths, block_table, parents, norm_gains,
    w_query, w_key, w_value, w_out, w_gate, w_up, w_down, *, nx, ny,
):
    columns = inputs.shape[2]
    tiles = nx + max(nx // 8, 1)
    rest_tiles = tiles - nx
    span = tiles * MAIN
    ys = nx // 2
    last_step = ys // 2

    x = jnp.pad(inputs.reshape(ROWS // 8, 8, columns), ((0, 0), (0, 0), (0, 256 - columns)))
    gains = 1.0 + norm_gains
    gains = jnp.concatenate([gains[:, 0:MAIN], jnp.pad(gains[:, MAIN:], ((0, 0), (0, MAIN - REST)))], axis=0)
    high = lax.reduce_precision(gains, 8, 7)
    qkv_weights = jnp.concatenate([w_query, w_key, w_value], axis=1)
    wa = jnp.concatenate([qkv_weights, high.astype(BF16), (gains - high).astype(BF16)], axis=0)
    narrow = jnp.pad(jnp.concatenate([w_gate[:, 256:], w_up[:, 256:]], axis=1), ((0, 0), (0, 64)))
    out_rest = jnp.pad(w_out[:, MAIN:].T, ((0, 0), (0, 64)))
    down_rest = jnp.pad(w_down[:, MAIN:].T, ((0, 0), (0, 96)))
    wf = jnp.concatenate(
        [w_out[:, 0:MAIN], out_rest]
        + [w_gate[:, 0:128], w_gate[:, 128:256], w_up[:, 0:128], w_up[:, 128:256], narrow]
        + [w_down[:, 0:MAIN]] + [down_rest[:, 128 * n:128 * (n + 1)] for n in range(3)],
        axis=0,
    )
    frequency = ROPE_BASE ** (-jnp.arange(128, dtype=F32) * 2.0 / HEAD_DIM)
    positions = lengths[0] + jnp.arange(STEPS, dtype=jnp.int32)
    angles = positions[:, None].astype(F32) * frequency
    trig = jnp.tile(jnp.stack([jnp.cos(angles), jnp.sin(angles)]), (1, BEAM, 1))

    vmem = pl.BlockSpec(memory_space=pltpu.VMEM)
    dma = pltpu.SemaphoreType.DMA
    out = pl.pallas_call(
        functools.partial(layer_kernel, nx, ny, nx * columns),
        name="layer",
        out_shape=jax.ShapeDtypeStruct((4, 8, 256), BF16),
        in_specs=[vmem, vmem, vmem, pl.BlockSpec(memory_space=pl.ANY), vmem, vmem, vmem, vmem],
        out_specs=vmem,
        scratch_shapes=[
            pltpu.VMEM((2, ys, A_ROWS, 128), BF16),
            pltpu.VMEM((2, ys, F_ROWS, 128), BF16),
            pltpu.VMEM((nx, 8, 128), F32),
            pltpu.VMEM((rest_tiles, 8, 128), F32),
            pltpu.VMEM((nx, 8, 256), BF16),
            pltpu.VMEM((8, span), F32),
            pltpu.VMEM((2, 8, span), BF16),
            pltpu.VMEM((8, 8, span), BF16),
            pltpu.VMEM((8, 8, span), BF16),
            pltpu.VMEM((64, span), BF16),
            pltpu.VMEM((2, ROWS, 128), BF16),
            pltpu.VMEM((ny, ROWS, 128), BF16),
            pltpu.VMEM(cache_pool.shape, BF16),
            pltpu.VMEM((ny, ROWS, 128), BF16),
            pltpu.VMEM((2, nx, ROWS, 128), BF16),
            pltpu.VMEM((2, 8, 8, span), BF16),
            pltpu.VMEM((ny, 8, span), BF16),
            pltpu.VMEM((ny, 8, span), BF16),
            pltpu.VMEM((nx, 8, 256), BF16),
            pltpu.VMEM((4, 8, 256), BF16),
            pltpu.VMEM((8, span), F32),
            pltpu.VMEM((8, span), F32),
        ]
        + [dma(())] * 5
        + [dma((2 * last_step,)), dma((2 * last_step,))]
        + [dma(())] * 19,
        compiler_params=pltpu.CompilerParams(has_side_effects=True, vmem_limit_bytes=40 << 20),
    )(x, wa, wf, cache_pool, trig, block_table, lengths.reshape(1, 1), parents)
    return out[:, :, 0:columns].reshape(inputs.shape)


def solution(mesh):
    return jax.shard_map(
        functools.partial(body, nx=mesh.shape["gx"], ny=mesh.shape["gy"]),
        mesh=mesh,
        in_specs=(
            P("gy", None, "gx"),
            P(None, "gx", "gy", None),
            P("gy"),
            P("gy", None),
            P(None, "gy"),
            P(None, "gx"),
            P("gx", "gy"),
            P("gx", "gy"),
            P("gx", "gy"),
            P("gy", "gx"),
            P("gx", "gy"),
            P("gx", "gy"),
            P("gy", "gx"),
        ),
        out_specs=P("gy", None, "gx"),
        check_vma=False,
    )
```

```python
import functools
import math

import jax
import jax.numpy as jnp
from jax import lax
from jax.experimental import pallas as pl
from jax.experimental.pallas import tpu as pltpu
from jax.sharding import PartitionSpec as P

MESH = pl.DeviceIdType.MESH
F32 = jnp.float32
BF16 = jnp.bfloat16

HEAD_DIM = 256
WINDOW = 4096
PAGE = 128
BEAM = 8
STEPS = 4
ROWS = BEAM * STEPS
EPSILON = 1e-06
SOFT_CAP = 50.0
ROPE_BASE = 10000.0
MAIN = 128
REST = 16

QKV_ROWS = 144
A_ROWS = 160
OUT_AT = 0
OUT_REST_AT = 64
GATE_AT = 80
NARROW_AT = 656
DOWN_AT = 800
F_ROWS = 1088
CUT = 544
DEN_ROWS = 40


def capped(scores):
    return jnp.exp(SOFT_CAP * jnp.tanh(scores * (1.0 / SOFT_CAP)))


def gelu(v):
    return 0.5 * v * (1.0 + jnp.tanh(math.sqrt(2.0 / math.pi) * (v + 0.044715 * (v * v * v))))


def dot(a, b):
    return jnp.dot(a, b, preferred_element_type=F32)


def dot_nt(a, b):
    return lax.dot_general(a, b, (((1,), (1,)), ((), ())), preferred_element_type=F32)


def layer_kernel(
    nx, ny, width,
    inputs_ref, cache_ref, length_ref, table_ref, parents_ref, gains_ref,
    wq_ref, wk_ref, wv_ref, wo_ref, wg_ref, wu_ref, wd_ref, trig_ref,
    out_ref,
    inputs_vm, cache, table_vm, parents_vm, gains_vm,
    wq_vm, wk_vm, wv_vm, wo_vm, wg_vm, wu_vm, wd_vm,
    wa_all, wf_all, gain_main, gain_rest, x_out, x_in, x_own, row_all, ff_all, norm_in,
    qkv_out, qkv_in, num_out, num_in, att_out, att_in, part_out, part_in, down_in, last_out, last_in,
    mixed, sums,
    load_sem, wa_send, wa_recv, wa_core_send, wa_core_recv, ring_send, ring_recv, wf_core_send, wf_core_recv,
    x_send, x_recv, row_a_send, row_a_recv, row_b_send, row_b_recv, qkv_send, qkv_recv, num_send, num_recv,
    att_send, att_recv, part_send, part_recv, ff_a_send, ff_a_recv, ff_b_send, ff_b_recv,
    down_send, down_recv, last_send, last_recv,
):
    ys = nx // 2
    zs = ny // 4
    kv_heads = ny // 8
    tiles = nx + nx // 8 if nx >= 8 else nx + 1
    rest_tiles = tiles - nx
    blocks = 8
    row_blocks = blocks // zs
    i = lax.axis_index("gx")
    j = lax.axis_index("gy")
    y, c = i // 2, i % 2
    sibling = i + 1 - 2 * c
    piece = c * ys + y
    zj, xj = j // 4, j % 4
    chunk = 2 * ((zj + 2 * xj) % ys) + xj % 2
    half = xj // 2

    def group_of(part):
        x_r = 2 * part + c
        return ((y + 8 * ys - 2 * x_r) % ys) * 4 + x_r

    def owner_of(core, block):
        return 4 * block + 2 * core + block % 2 if zs == 8 else block

    if zs == 8:
        is_owner = (xj // 2 == c) & (xj % 2 == zj % 2)
        my_block = zj
    else:
        is_owner = j >= 0
        my_block = j

    def remote(src, dst, send_sem, recv_sem, tx, ty):
        return pltpu.make_async_remote_copy(
            src_ref=src, dst_ref=dst, send_sem=send_sem, recv_sem=recv_sem,
            device_id=(tx, ty), device_id_type=MESH,
        )

    def put(src, dst, send_sem, recv_sem, tx, ty):
        own = (tx == i) & (ty == j)

        @pl.when(jnp.logical_not(own))
        def _():
            remote(src, dst, send_sem, recv_sem, tx, ty).start()

        @pl.when(own)
        def _():
            pltpu.make_async_copy(src, dst, recv_sem).start()

    def take(ref, sem):
        pltpu.make_async_copy(ref, ref, sem).wait()

    def take_sent(ref, count, sem, own):
        @pl.when(own)
        def _():
            take(ref.at[pl.ds(0, count - 1)], sem)

        @pl.when(jnp.logical_not(own))
        def _():
            take(ref.at[pl.ds(0, count)], sem)

    loads = [
        pltpu.make_async_copy(src, dst, load_sem.at[k])
        for k, (src, dst) in enumerate([
            (inputs_ref, inputs_vm), (wq_ref, wq_vm), (wk_ref, wk_vm), (wv_ref, wv_vm), (gains_ref, gains_vm),
            (wo_ref, wo_vm), (wg_ref, wg_vm), (wu_ref, wu_vm), (wd_ref, wd_vm),
            (table_ref, table_vm), (parents_ref, parents_vm), (cache_ref, cache),
        ])
    ]
    for load in loads:
        load.start()

    home = chunk == i
    own_rows = home & is_owner & (my_block // 4 == half)
    barrier = pltpu.get_barrier_semaphore()

    def hello(tx, ty):
        pl.semaphore_signal(barrier, inc=1, device_id=(tx, ty), device_id_type=MESH)

    for step in range(1, ys):
        hello(2 * ((y + step) % ys) + c, j)
    hello(sibling, j)
    for step in range(1, zs):
        hello(i, 4 * ((zj + step) % zs) + xj)
    for step in range(1, 4):
        if zs == 8:
            @pl.when((2 * c + zj % 2) == (xj + step) % 4)
            def _():
                hello(i, 4 * zj + (xj + step) % 4)
        else:
            hello(i, 4 * zj + (xj + step) % 4)

    @pl.when(is_owner)
    def _():
        group = group_of(my_block // 4)

        @pl.loop(0, nx)
        def _(to):
            @pl.when(jnp.logical_not((to == i) & (group == j)))
            def _():
                hello(to, group)

    waits = ys + (zs - 1) + 4
    waits = waits + jnp.where(is_owner, 3, 0) - jnp.where(own_rows, 1, 0)

    loads[0].wait()
    for q in range(4):
        v = jnp.concatenate([inputs_vm[2 * q].astype(F32), inputs_vm[2 * q + 1].astype(F32)], axis=0)
        v = jnp.concatenate([v, jnp.zeros((8, MAIN - REST), F32)], axis=1)
        x_out[q] = v.astype(BF16)
    pl.semaphore_wait(barrier, waits)
    core_of_chunk = chunk % 2
    for q in range(4):
        put(x_out.at[q], x_in.at[piece], x_send, x_recv, chunk, owner_of(core_of_chunk, half * 4 + q))
    for load in loads[1:5]:
        load.wait()
    v = jnp.concatenate([wq_vm[...].astype(F32), wk_vm[...].astype(F32), wv_vm[...].astype(F32)], axis=0)
    wa_all[c, y, 0:MAIN, :] = v[:, 0:MAIN].T.astype(BF16)
    v = jnp.concatenate([v[:, MAIN:], jnp.zeros((128, MAIN - REST), F32)], axis=1).T
    wa_all[c, y, MAIN:QKV_ROWS, :] = v[0:REST].astype(BF16)
    v = 1.0 + gains_vm[...]
    v = jnp.concatenate([v, jnp.zeros((4, MAIN - REST), F32)], axis=1)
    v = jnp.concatenate([v[:, 0:MAIN], v[:, MAIN:]], axis=0)
    high = v.astype(BF16).astype(F32)
    wa_all[c, y, QKV_ROWS:A_ROWS, :] = jnp.concatenate([high, v - high], axis=0).astype(BF16)
    for step in range(1, ys):
        remote(wa_all.at[c, y], wa_all.at[c, y], wa_send, wa_recv, 2 * ((y + step) % ys) + c, j).start()

    right = 2 * ((y + 1) % ys) + c
    left = 2 * ((y + ys - 1) % ys) + c
    last_step = ys // 2

    def ring_refs(step):
        from_left = (y + ys - (step - 1)) % ys
        from_right = (y + (step - 1)) % ys
        return from_left, from_right

    def ring_start(step):
        a, b = ring_refs(step)
        src_a, src_b = wf_all.at[c, a], wf_all.at[c, b]
        if step == last_step:
            src_a, src_b = src_a.at[pl.ds(0, CUT)], src_b.at[pl.ds(CUT, F_ROWS - CUT)]
        remote(src_a, src_a, ring_send.at[2 * step - 2], ring_recv.at[2 * step - 2], right, j).start()
        remote(src_b, src_b, ring_send.at[2 * step - 1], ring_recv.at[2 * step - 1], left, j).start()

    def to_sibling(k):
        remote(wf_all.at[c, k], wf_all.at[c, k], wf_core_send, wf_core_recv, sibling, j).start()

    def ring_take(step):
        a = (y + ys - step) % ys
        b = (y + step) % ys
        ref_a, ref_b = wf_all.at[c, a], wf_all.at[c, b]
        if step == last_step:
            take(ref_a.at[pl.ds(0, CUT)], ring_recv.at[2 * step - 2])
            take(ref_b.at[pl.ds(CUT, F_ROWS - CUT)], ring_recv.at[2 * step - 1])
            to_sibling(a)
        else:
            take(ref_a, ring_recv.at[2 * step - 2])
            take(ref_b, ring_recv.at[2 * step - 1])
            ring_start(step + 1)
            to_sibling(a)
            to_sibling(b)

    def rest_sum(pieces):
        out = []
        for t in range(rest_tiles):
            total = None
            for k in range(min(8, nx)):
                v = pieces[8 * t + k]
                v = pltpu.roll(v, REST * k, 1) if k else v
                total = v if total is None else total + v
            out.append(total)
        return out

    def spread(ref, send_sem, recv_sem):
        for step in range(1, 4):
            src = ref.at[my_block]
            remote(src, src, send_sem, recv_sem, i, 4 * zj + (xj + step) % 4).start()

    def spread_in(ref, recv_sem):
        @pl.when(jnp.logical_not(is_owner))
        def _():
            take(ref.at[pl.ds(0, row_blocks)], recv_sem)

        if row_blocks > 1:
            @pl.when(is_owner)
            def _():
                take(ref.at[pl.ds(0, row_blocks - 1)], recv_sem)

    def spread_out(ref, send_sem, recv_sem):
        src = ref.at[pl.ds(row_blocks * zj, row_blocks)]
        for step in range(1, zs):
            remote(src, src, send_sem, recv_sem, i, 4 * ((zj + step) % zs) + xj).start()

    @pl.when(is_owner)
    def _():
        take(x_in, x_recv)
        rests = []
        for p in range(nx):
            v = x_in[p].astype(F32)
            x_own[:, MAIN * p:MAIN * (p + 1)] = v[:, 0:MAIN]
            rests.append(v[:, MAIN:2 * MAIN])
        for t, v in enumerate(rest_sum(rests)):
            x_own[:, MAIN * (nx + t):MAIN * (nx + t + 1)] = v
        row_all[my_block] = x_own[...].astype(BF16)
        spread(row_all, row_a_send, row_a_recv)

    for load in loads[5:9]:
        load.wait()
    own_f = wf_all.at[c, y]
    own_f[OUT_AT:OUT_REST_AT, :] = wo_vm[:, 0:MAIN]
    v = jnp.concatenate([wo_vm[:, MAIN:].astype(F32), jnp.zeros((64, MAIN - REST), F32)], axis=1)
    v = jnp.concatenate([v, jnp.zeros((64, MAIN), F32)], axis=0).T
    own_f[OUT_REST_AT:GATE_AT, :] = v[0:REST].astype(BF16)
    for n in range(2):
        at = slice(MAIN * n, MAIN * (n + 1))
        own_f[GATE_AT + 144 * n:GATE_AT + 144 * (n + 1), :] = wg_vm[:, at]
        own_f[GATE_AT + 144 * (n + 2):GATE_AT + 144 * (n + 3), :] = wu_vm[:, at]
        own_f[DOWN_AT + 144 * n:DOWN_AT + 144 * (n + 1), :] = wd_vm[:, at]
    v = [w[:, 256:288].astype(F32) for w in (wg_vm, wu_vm, wd_vm)] + [jnp.zeros((144, 32), F32)]
    own_f[NARROW_AT:DOWN_AT, :] = jnp.concatenate(v, axis=1).astype(BF16)
    ring_start(1)
    to_sibling(y)

    spread_in(row_all, row_a_recv)
    spread_out(row_all, row_b_send, row_b_recv)

    take(wa_all.at[c, pl.ds(0, ys - 1)], wa_recv)
    remote(wa_all.at[c], wa_all.at[c], wa_core_send, wa_core_recv, sibling, j).start()
    take(wa_all.at[1 - c], wa_core_recv)
    rests = []
    for p in range(nx):
        v = wa_all[p // ys, p % ys, QKV_ROWS:A_ROWS, :].astype(F32)
        v = v[0:8] + v[8:16]
        gain_main[p] = v
        rests.append(v)
    for t, v in enumerate(rest_sum(rests)):
        gain_rest[t] = v

    def gain(which, t):
        if t < nx:
            return gain_main[t, which:which + 1, :]
        return gain_rest[t - nx, 4 + which:5 + which, :]

    take(row_all.at[pl.ds(0, blocks - row_blocks)], row_b_recv)

    def chunk_tile(ref, t):
        at = slice(MAIN * t, MAIN * (t + 1))
        return jnp.concatenate([ref[k, :, at].astype(F32) for k in range(blocks)], axis=0)

    total = None
    for t in range(tiles):
        v = chunk_tile(row_all, t)
        total = v * v if total is None else total + v * v
    scale = lax.rsqrt(jnp.sum(total, axis=1, keepdims=True) / width + EPSILON)
    for t in range(tiles):
        v = chunk_tile(row_all, t)
        norm_in[:, MAIN * t:MAIN * (t + 1)] = (v * scale * gain(0, t)).astype(BF16)
    main_w = wa_all[:, :, 0:MAIN, :].reshape(nx * MAIN, 128)
    rest_w = wa_all[:, :, MAIN:QKV_ROWS, :].reshape(nx * REST, 128)
    qkv = dot(norm_in[:, 0:nx * MAIN], main_w) + dot(norm_in[:, nx * MAIN:nx * MAIN + nx * REST], rest_w)
    qkv = qkv.astype(BF16)
    qkv_out[0] = qkv[0:ROWS]
    qkv_out[1] = qkv[ROWS:2 * ROWS]

    for part in range(2):
        group = group_of(part)

        @pl.loop(0, nx)
        def _(step):
            put(qkv_out.at[part], qkv_in.at[j], qkv_send, qkv_recv, (i + step) % nx, group)

    if last_step > 1:
        ring_take(1)

    row = lax.broadcasted_iota(jnp.int32, (ROWS, 1), 0)
    row_step, row_beam = row & 3, jnp.right_shift(row, 2)
    for load in loads[9:12]:
        load.wait()
    length = jnp.full((1, 1), length_ref[0], jnp.int32)
    first_page = jnp.right_shift(jnp.maximum(length - (WINDOW - 1), 0), 7).astype(F32)
    length_wide = length.astype(F32)
    page_iota = lax.broadcasted_iota(jnp.int32, table_vm.shape, 1).astype(F32)
    lane = lax.broadcasted_iota(jnp.int32, (ROWS, PAGE), 1)
    lane_wide = lane.astype(F32)
    lowest = row_step.astype(F32) - (WINDOW - 1)
    masks = []
    for slot in range(4):
        match = table_vm[...] == i * 4 + slot
        page = jnp.sum(jnp.where(match, page_iota, 0.0), axis=1, keepdims=True)
        used = jnp.sum(jnp.where(match, 1.0, 0.0), axis=1, keepdims=True)
        start = jnp.where(used > 0.5, (first_page + page) * PAGE - length_wide, 1.0)
        place = start + lane_wide
        mask = jnp.where((place < 0.0) & (place >= lowest), 1.0, 0.0)
        masks.append(jnp.concatenate([mask, mask], axis=0) > 0.5)
    key_lane = lax.broadcasted_iota(jnp.int32, (ROWS, ROWS), 1)
    key_step, key_beam = key_lane & 3, jnp.right_shift(key_lane, 2)
    beam_lane = lax.broadcasted_iota(jnp.int32, (ROWS, BEAM), 1)
    current = row_beam
    tail = jnp.zeros((ROWS, ROWS), F32)
    for at in range(STEPS - 1, -1, -1):
        hit = (key_step == at) & (row_step >= at) & (key_beam == current)
        tail = jnp.where(hit, 1.0, tail)
        if at:
            chosen = jnp.where(beam_lane == current, parents_vm[at - 1:at, :].astype(F32), 0.0)
            parent = jnp.sum(chosen, axis=1, keepdims=True).astype(jnp.int32)
            current = jnp.where(row_step >= at, parent, current)
    tail = jnp.where(i == 0, tail, 0.0)
    tail_mask = jnp.concatenate([tail, tail], axis=0) > 0.5

    cosine, sine = trig_ref[0], trig_ref[1]
    take(qkv_in, qkv_recv)

    def quarter(source, at, parts):
        span = 128 // parts
        total = None
        for m in range(parts):
            v = qkv_in[source + m].astype(F32)
            shift = (span * m - at) % 128
            v = pltpu.roll(v, shift, 1) if shift else v
            total = v if total is None else jnp.where(lane >= span * m, v, total)
        return total

    def rotated(u, w):
        return u * cosine - w * sine, w * cosine + u * sine

    def wide(u, w):
        return jnp.concatenate([u, w], axis=1)

    for h in range(kv_heads):
        qs = []
        for g in range(2):
            base = 4 * (2 * h + g)
            u, w = rotated(quarter(base, 0, 2), quarter(base + 2, 0, 2))
            qs.append(wide(u, w) * HEAD_DIM ** -0.5)
        query = jnp.concatenate(qs, axis=0).astype(BF16)
        key = wide(*rotated(quarter(8 * h, 64, 4), quarter(8 * h + 4, 64, 4))).astype(BF16)
        value = wide(quarter(8 * h, 96, 4), quarter(8 * h + 4, 96, 4)).astype(BF16)
        weights = jnp.where(tail_mask, capped(dot_nt(query, key)), 0.0)
        den = jnp.sum(weights, axis=1, keepdims=True)
        num = dot(weights.astype(BF16), value)
        for slot in range(4):
            at = slice(HEAD_DIM * h, HEAD_DIM * (h + 1))
            weights = jnp.where(masks[slot], capped(dot_nt(query, cache[0, slot, :, at])), 0.0)
            den = den + jnp.sum(weights, axis=1, keepdims=True)
            num = num + dot(weights.astype(BF16), cache[1, slot, :, at])
        den_high = den.astype(BF16).astype(F32)
        den_low = den - den_high
        for g in range(2):
            rows = slice(ROWS * g, ROWS * (g + 1))
            both = jnp.where(lane == row, den_high[rows], 0.0) + jnp.where(lane == row + ROWS, den_low[rows], 0.0)
            both = jnp.broadcast_to(jnp.sum(both, axis=0, keepdims=True), (8, 128))
            for t in range(2):
                v = jnp.concatenate([num[rows, 128 * t:128 * (t + 1)], both], axis=0)
                num_out[2 * (2 * h + g) + t] = v.astype(BF16)

    @pl.loop(1, nx)
    def _(step):
        to = (i + step) % nx
        remote(num_out.at[to], num_in.at[i], num_send, num_recv, to, j).start()

    pltpu.make_async_copy(num_out.at[i], num_in.at[i], num_recv).start()
    if last_step > 2:
        ring_take(2)
    take(num_in, num_recv)
    total = None
    for p in range(nx):
        v = num_in[p].astype(F32)
        total = v if total is None else total + v
    both = jnp.where((lane == row) | (lane == row + ROWS), total[ROWS:ROWS + 1], 0.0)
    total = total[0:ROWS] / jnp.sum(both, axis=1, keepdims=True)
    att_out[0] = total.astype(BF16)
    for k in range(2):
        put(att_out.at[0], att_in.at[half], att_send, att_recv, chunk, 2 * i + k)
    for step in range(3, last_step):
        ring_take(step)

    take(att_in, att_recv)
    attended = []
    for part in range(2):
        v = att_in[part].astype(F32)
        attended.append(jnp.where(j % 2 == 1, pltpu.roll(v, 64, 1), v)[:, 0:64])
    attended = jnp.concatenate(attended, axis=0).astype(BF16)
    ring_take(last_step)
    take(wf_all.at[1 - c], wf_core_recv)

    def put_partial(which, t, v):
        for k in range(blocks):
            part_out[which, k, :, MAIN * t:MAIN * (t + 1)] = v[8 * k:8 * (k + 1)].astype(BF16)

    def put_rest(which, v):
        if v.shape[1] < 128:
            v = jnp.concatenate([v, jnp.zeros((v.shape[0], 128 - v.shape[1]), F32)], axis=1)
        for t in range(rest_tiles):
            put_partial(which, nx + t, v[:, 128 * t:128 * (t + 1)])

    for p in range(nx):
        put_partial(0, p, dot(attended, wf_all[p // ys, p % ys, OUT_AT:OUT_REST_AT, :]))
    rest_w = wf_all[:, :, OUT_REST_AT:GATE_AT, :].reshape(nx * REST, 128)
    put_rest(0, dot_nt(attended, rest_w[:, 0:64]))

    def send_partial(which, dst_all, send_sem, recv_sem):
        @pl.loop(0, blocks)
        def _(k):
            put(part_out.at[which, k], dst_all.at[j], send_sem, recv_sem, i, owner_of(c, k))

    def add_up(ref, t):
        total = None
        for s in range(ny):
            v = ref[s, :, MAIN * t:MAIN * (t + 1)].astype(F32)
            total = v if total is None else total + v
        return total

    def add_rows(ref):
        square = None
        for t in range(tiles):
            v = add_up(ref, t)
            sums[:, MAIN * t:MAIN * (t + 1)] = v
            square = v * v if square is None else square + v * v
        return lax.rsqrt(jnp.sum(square, axis=1, keepdims=True) / width + EPSILON)

    send_partial(0, part_in, part_send, part_recv)

    @pl.when(is_owner)
    def _():
        take(part_in, part_recv)
        scale = add_rows(part_in)
        square = None
        for t in range(tiles):
            at = slice(MAIN * t, MAIN * (t + 1))
            v = x_own[:, at] + sums[:, at] * scale * gain(1, t)
            mixed[:, at] = v
            square = v * v if square is None else square + v * v
        scale = lax.rsqrt(jnp.sum(square, axis=1, keepdims=True) / width + EPSILON)
        for t in range(tiles):
            at = slice(MAIN * t, MAIN * (t + 1))
            sums[:, at] = mixed[:, at] * scale * gain(2, t)
        ff_all[my_block] = sums[...].astype(BF16)
        spread(ff_all, ff_a_send, ff_a_recv)

    spread_in(ff_all, ff_a_recv)
    spread_out(ff_all, ff_b_send, ff_b_recv)

    take(ff_all.at[pl.ds(0, blocks - row_blocks)], ff_b_recv)
    for t in range(tiles):
        norm_in[:, MAIN * t:MAIN * (t + 1)] = chunk_tile(ff_all, t).astype(BF16)
    main_x = norm_in[:, 0:nx * MAIN]
    rest_x = norm_in[:, nx * MAIN:nx * MAIN + nx * REST]

    def ff_part(n):
        at = GATE_AT + 144 * n
        main_w = wf_all[:, :, at:at + MAIN, :].reshape(nx * MAIN, 128)
        rest_w = wf_all[:, :, at + MAIN:at + 144, :].reshape(nx * REST, 128)
        return dot(main_x, main_w) + dot(rest_x, rest_w)

    hidden = [(gelu(ff_part(n)) * ff_part(n + 2)).astype(BF16) for n in range(2)]
    both = ff_part(4)
    narrow = gelu(both) * pltpu.roll(both, 96, 1)
    lane_chunk = lax.broadcasted_iota(jnp.int32, narrow.shape, 1)
    narrow = pltpu.roll(jnp.where(lane_chunk < 32, narrow, 0.0), 64, 1)
    hidden.append(narrow.astype(BF16))
    places = [DOWN_AT, DOWN_AT + 144, NARROW_AT]
    for p in range(nx):
        v = None
        for h, at in zip(hidden, places):
            term = dot_nt(h, wf_all[p // ys, p % ys, at:at + MAIN, :])
            v = term if v is None else v + term
        put_partial(1, p, v)
    v = None
    for h, at in zip(hidden, places):
        rest_w = wf_all[:, :, at + MAIN:at + 144, :].reshape(nx * REST, 128)
        term = dot_nt(h, rest_w)
        v = term if v is None else v + term
    put_rest(1, v)
    send_partial(1, down_in, down_send, down_recv)

    @pl.when(is_owner)
    def _():
        take(down_in, down_recv)
        scale = add_rows(down_in)

        def result(t):
            at = slice(MAIN * t, MAIN * (t + 1))
            return mixed[:, at] + sums[:, at] * scale * gain(3, t)

        for p in range(nx):
            v = result(nx + p // 8)
            shift = (128 - REST * (p % 8)) % 128
            v = pltpu.roll(v, shift, 1) if shift else v
            last_out[p] = jnp.concatenate([result(p), v], axis=1).astype(BF16)
        group = group_of(my_block // 4)

        @pl.loop(0, nx)
        def _(p):
            to = 2 * (p % ys) + p // ys
            put(last_out.at[p], last_in.at[my_block % 4], last_send, last_recv, to, group)

    take(last_in, last_recv)
    out_ref[...] = last_in[...]

    take_sent(x_in, 4, x_send, own_rows)
    take(wa_all.at[c, pl.ds(0, ys - 1)], wa_send)
    take(wa_all.at[c], wa_core_send)
    for step in range(1, last_step + 1):
        for side in range(2):
            rows = pl.ds(0, F_ROWS) if step < last_step else pl.ds(CUT * side, F_ROWS - CUT if side else CUT)
            take(wf_all.at[0, 0, rows], ring_send.at[2 * step - 2 + side])
    take(wf_all.at[c], wf_core_send)
    take_sent(qkv_in, ny, qkv_send, home)
    take(num_out.at[pl.ds(0, nx - 1)], num_send)
    take_sent(att_in, 2, att_send, home & (j // 2 == i))
    take_sent(row_all, blocks, part_send, is_owner)
    take_sent(ff_all, blocks, down_send, is_owner)
    take(row_all.at[pl.ds(0, (zs - 1) * row_blocks)], row_b_send)
    take(ff_all.at[pl.ds(0, (zs - 1) * row_blocks)], ff_b_send)

    @pl.when(is_owner)
    def _():
        take(row_all.at[pl.ds(0, 3)], row_a_send)
        take(ff_all.at[pl.ds(0, 3)], ff_a_send)
        take_sent(x_in, nx, last_send, home & (my_block // 4 == half))


def body(
    inputs, cache_pool, lengths, block_table, parents, norm_gains,
    w_query, w_key, w_value, w_out, w_gate, w_up, w_down, *, nx, ny,
):
    columns = inputs.shape[2]
    tiles = nx + max(nx // 8, 1)
    rest_tiles = tiles - nx
    span = tiles * MAIN
    ys = nx // 2
    last_step = ys // 2

    frequency = ROPE_BASE ** (-jnp.arange(128, dtype=F32) * 2.0 / HEAD_DIM)
    positions = lengths[0] + jnp.arange(STEPS, dtype=jnp.int32)
    angles = positions[:, None].astype(F32) * frequency
    trig = jnp.tile(jnp.stack([jnp.cos(angles), jnp.sin(angles)]), (1, BEAM, 1))

    arrays = (
        inputs, cache_pool, lengths, block_table, parents, norm_gains,
        w_query.T, w_key.T, w_value.T, w_out, w_gate, w_up, w_down.T, trig,
    )
    vmem = pl.BlockSpec(memory_space=pltpu.VMEM)
    specs = [pl.BlockSpec(memory_space=pltpu.HBM) for _ in arrays]
    specs[2] = pl.BlockSpec(memory_space=pltpu.SMEM)
    specs[13] = vmem
    dma = pltpu.SemaphoreType.DMA

    def held(*shape, dtype=BF16):
        return pltpu.VMEM(shape, dtype)

    out = pl.pallas_call(
        functools.partial(layer_kernel, nx, ny, nx * columns),
        name="layer",
        out_shape=jax.ShapeDtypeStruct((4, 8, 256), BF16),
        in_specs=specs,
        out_specs=vmem,
        scratch_shapes=[pltpu.VMEM(arrays[k].shape, arrays[k].dtype) for k in (0, 1, 3, 4, 5, 6, 7, 8, 9, 10, 11, 12)]
        + [
            held(2, ys, A_ROWS, 128),
            held(2, ys, F_ROWS, 128),
            held(nx, 8, 128, dtype=F32),
            held(rest_tiles, 8, 128, dtype=F32),
            held(4, 8, 256),
            held(nx, 8, 256),
            held(8, span, dtype=F32),
            held(8, 8, span),
            held(8, 8, span),
            held(64, span),
            held(2, ROWS, 128),
            held(ny, ROWS, 128),
            held(nx, DEN_ROWS, 128),
            held(nx, DEN_ROWS, 128),
            held(1, ROWS, 128),
            held(2, ROWS, 128),
            held(2, 8, 8, span),
            held(ny, 8, span),
            held(ny, 8, span),
            held(nx, 8, 256),
            held(4, 8, 256),
            held(8, span, dtype=F32),
            held(8, span, dtype=F32),
        ]
        + [dma((12,))] + [dma(())] * 4
        + [dma((2 * last_step,)), dma((2 * last_step,))]
        + [dma(())] * 24,
        compiler_params=pltpu.CompilerParams(collective_id=0, has_side_effects=True, vmem_limit_bytes=60 << 20),
    )(*arrays)
    return out[:, :, 0:columns].reshape(inputs.shape)


def solution(mesh):
    return jax.shard_map(
        functools.partial(body, nx=mesh.shape["gx"], ny=mesh.shape["gy"]),
        mesh=mesh,
        in_specs=(
            P("gy", None, "gx"),
            P(None, "gx", "gy", None),
            P("gy"),
            P("gy", None),
            P(None, "gy"),
            P(None, "gx"),
            P("gx", "gy"),
            P("gx", "gy"),
            P("gx", "gy"),
            P("gy", "gx"),
            P("gx", "gy"),
            P("gx", "gy"),
            P("gy", "gx"),
        ),
        out_specs=P("gy", None, "gx"),
        check_vma=False,
    )
```

```python
import functools
import math

import jax
import jax.numpy as jnp
from jax import lax
from jax.experimental import pallas as pl
from jax.experimental.pallas import tpu as pltpu
from jax.sharding import PartitionSpec as P

MESH = pl.DeviceIdType.MESH
F32 = jnp.float32
BF16 = jnp.bfloat16

HEAD_DIM = 256
WINDOW = 4096
PAGE = 128
BEAM = 8
STEPS = 4
ROWS = BEAM * STEPS
EPSILON = 1e-06
SOFT_CAP = 50.0
ROPE_BASE = 10000.0
MAIN = 128
REST = 16

QKV_ROWS = 144
A_ROWS = 160
OUT_AT = 0
OUT_REST_AT = 64
B_ROWS = 80
GATE_AT = 0
NARROW_AT = 576
DOWN_AT = 720
F_ROWS = 1008
CUT = 512
DEN_ROWS = 40


def capped(scores):
    return jnp.exp(SOFT_CAP * jnp.tanh(scores * (1.0 / SOFT_CAP)))


def gelu(v):
    return 0.5 * v * (1.0 + jnp.tanh(math.sqrt(2.0 / math.pi) * (v + 0.044715 * (v * v * v))))


def dot(a, b):
    return jnp.dot(a, b, preferred_element_type=F32)


def dot_nt(a, b):
    return lax.dot_general(a, b, (((1,), (1,)), ((), ())), preferred_element_type=F32)


def layer_kernel(
    nx, ny, width,
    inputs_ref, cache_ref, length_ref, table_ref, parents_ref, gains_ref,
    wq_ref, wk_ref, wv_ref, wo_ref, wg_ref, wu_ref, wd_ref, trig_ref,
    out_ref,
    inputs_vm, cache, table_vm, parents_vm, gains_vm,
    wq_vm, wk_vm, wv_vm, wo_vm, wg_vm, wu_vm, wd_vm,
    wa_all, wb_all, wf_all, gain_main, gain_rest, x_out, x_in, x_own, row_all, ff_all, norm_in,
    q_out, kv_out, q_in, kv_in, tail_num, tail_den, num_out, num_in, att_out, att_in, part_out,
    part_z, down_z, sum_out, part_x, down_x, last_out, last_in, mixed, sums,
    load_sem, wa_send, wa_recv, wa_core_send, wa_core_recv, ring_send, ring_recv, wf_core_send, wf_core_recv,
    wb_send, wb_recv, wb_core_send, wb_core_recv,
    x_send, x_recv, row_send, row_recv, q_send, q_recv, kv_send, kv_recv, num_send, num_recv,
    att_send, att_recv, part_send, part_recv, part_x_send, part_x_recv, ff_send, ff_recv,
    down_send, down_recv, down_x_send, down_x_recv, last_send, last_recv,
):
    ys = nx // 2
    zs = ny // 4
    kv_heads = ny // 8
    tiles = nx + nx // 8 if nx >= 8 else nx + 1
    rest_tiles = tiles - nx
    blocks = 8
    row_blocks = blocks // zs
    i = lax.axis_index("gx")
    j = lax.axis_index("gy")
    y, c = i // 2, i % 2
    sibling = i + 1 - 2 * c
    piece = c * ys + y
    zj, xj = j // 4, j % 4
    chunk = 2 * ((zj + 2 * xj) % ys) + xj % 2
    half = xj // 2

    def group_of(part):
        x_r = 2 * part + c
        return ((y + 8 * ys - 2 * x_r) % ys) * 4 + x_r

    first_block = row_blocks * zj
    my_part = first_block // 4
    home = chunk == i
    own_rows = home & (my_part == half)
    tail_stride = nx // kv_heads

    def remote(src, dst, send_sem, recv_sem, tx, ty):
        return pltpu.make_async_remote_copy(
            src_ref=src, dst_ref=dst, send_sem=send_sem, recv_sem=recv_sem,
            device_id=(tx, ty), device_id_type=MESH,
        )

    def put(src, dst, send_sem, recv_sem, tx, ty):
        own = (tx == i) & (ty == j)

        @pl.when(jnp.logical_not(own))
        def _():
            remote(src, dst, send_sem, recv_sem, tx, ty).start()

        @pl.when(own)
        def _():
            pltpu.make_async_copy(src, dst, recv_sem).start()

    def take(ref, sem):
        pltpu.make_async_copy(ref, ref, sem).wait()

    def take_sent(ref, count, sem, own, fewer=1):
        @pl.when(own)
        def _():
            take(ref.at[pl.ds(0, count - fewer)], sem)

        @pl.when(jnp.logical_not(own))
        def _():
            take(ref.at[pl.ds(0, count)], sem)

    loads = [
        pltpu.make_async_copy(src, dst, load_sem.at[k])
        for k, (src, dst) in enumerate([
            (inputs_ref, inputs_vm), (wq_ref, wq_vm), (wk_ref, wk_vm), (wv_ref, wv_vm), (gains_ref, gains_vm),
            (wo_ref, wo_vm), (wg_ref, wg_vm), (wu_ref, wu_vm), (wd_ref, wd_vm),
            (table_ref, table_vm), (parents_ref, parents_vm), (cache_ref, cache),
        ])
    ]
    for load in loads:
        load.start()

    barrier = pltpu.get_barrier_semaphore()

    def hello(tx, ty):
        pl.semaphore_signal(barrier, inc=1, device_id=(tx, ty), device_id_type=MESH)

    for step in range(1, ys):
        hello(2 * ((y + step) % ys) + c, j)
    hello(sibling, j)
    for step in range(1, zs):
        hello(i, 4 * ((zj + step) % zs) + xj)
    group = group_of(my_part)

    @pl.loop(0, nx)
    def _(to):
        @pl.when(jnp.logical_not((to == i) & (group == j)))
        def _():
            hello(to, group)

    waits = ys + (zs - 1) + 16 // row_blocks - jnp.where(own_rows, 1, 0)

    loads[0].wait()
    for q in range(4):
        v = jnp.concatenate([inputs_vm[2 * q].astype(F32), inputs_vm[2 * q + 1].astype(F32)], axis=0)
        v = jnp.concatenate([v, jnp.zeros((8, MAIN - REST), F32)], axis=1)
        x_out[q] = v.astype(BF16)
    pl.semaphore_wait(barrier, waits)
    for q in range(4):
        block = half * 4 + q
        for step in range(4):
            put(
                x_out.at[q], x_in.at[block % row_blocks, piece], x_send, x_recv,
                chunk, 4 * (block // row_blocks) + (xj + step) % 4,
            )
    for load in loads[1:5]:
        load.wait()
    v = jnp.concatenate([wq_vm[...].astype(F32), wk_vm[...].astype(F32), wv_vm[...].astype(F32)], axis=0)
    wa_all[c, y, 0:MAIN, :] = v[:, 0:MAIN].T.astype(BF16)
    v = jnp.concatenate([v[:, MAIN:], jnp.zeros((128, MAIN - REST), F32)], axis=1).T
    wa_all[c, y, MAIN:QKV_ROWS, :] = v[0:REST].astype(BF16)
    v = 1.0 + gains_vm[...]
    v = jnp.concatenate([v, jnp.zeros((4, MAIN - REST), F32)], axis=1)
    v = jnp.concatenate([v[:, 0:MAIN], v[:, MAIN:]], axis=0)
    high = v.astype(BF16).astype(F32)
    wa_all[c, y, QKV_ROWS:A_ROWS, :] = jnp.concatenate([high, v - high], axis=0).astype(BF16)
    for step in range(1, ys):
        remote(wa_all.at[c, y], wa_all.at[c, y], wa_send, wa_recv, 2 * ((y + step) % ys) + c, j).start()

    right = 2 * ((y + 1) % ys) + c
    left = 2 * ((y + ys - 1) % ys) + c
    last_step = ys // 2

    def ring_refs(step):
        from_left = (y + ys - (step - 1)) % ys
        from_right = (y + (step - 1)) % ys
        return from_left, from_right

    def ring_start(step):
        a, b = ring_refs(step)
        src_a, src_b = wf_all.at[c, a], wf_all.at[c, b]
        if step == last_step:
            src_a, src_b = src_a.at[pl.ds(0, CUT)], src_b.at[pl.ds(CUT, F_ROWS - CUT)]
        remote(src_a, src_a, ring_send.at[2 * step - 2], ring_recv.at[2 * step - 2], right, j).start()
        remote(src_b, src_b, ring_send.at[2 * step - 1], ring_recv.at[2 * step - 1], left, j).start()

    def to_sibling(k):
        remote(wf_all.at[c, k], wf_all.at[c, k], wf_core_send, wf_core_recv, sibling, j).start()

    def ring_take(step):
        a = (y + ys - step) % ys
        b = (y + step) % ys
        ref_a, ref_b = wf_all.at[c, a], wf_all.at[c, b]
        if step == last_step:
            take(ref_a.at[pl.ds(0, CUT)], ring_recv.at[2 * step - 2])
            take(ref_b.at[pl.ds(CUT, F_ROWS - CUT)], ring_recv.at[2 * step - 1])
            to_sibling(a)
        else:
            take(ref_a, ring_recv.at[2 * step - 2])
            take(ref_b, ring_recv.at[2 * step - 1])
            ring_start(step + 1)
            to_sibling(a)
            to_sibling(b)

    def rest_sum(pieces):
        out = []
        for t in range(rest_tiles):
            total = None
            for k in range(min(8, nx)):
                v = pieces[8 * t + k]
                v = pltpu.roll(v, REST * k, 1) if k else v
                total = v if total is None else total + v
            out.append(total)
        return out

    def spread(ref, send_sem, recv_sem):
        src = ref.at[pl.ds(first_block, row_blocks)]
        for step in range(1, zs):
            remote(src, src, send_sem, recv_sem, i, 4 * ((zj + step) % zs) + xj).start()

    take(x_in, x_recv)
    for b in range(row_blocks):
        rests = []
        for p in range(nx):
            v = x_in[b, p].astype(F32)
            x_own[b, :, MAIN * p:MAIN * (p + 1)] = v[:, 0:MAIN]
            rests.append(v[:, MAIN:2 * MAIN])
        for t, v in enumerate(rest_sum(rests)):
            x_own[b, :, MAIN * (nx + t):MAIN * (nx + t + 1)] = v
        row_all[first_block + b] = x_own[b].astype(BF16)
    spread(row_all, row_send, row_recv)

    for load in loads[5:9]:
        load.wait()
    own_b = wb_all.at[c, y]
    own_b[OUT_AT:OUT_REST_AT, :] = wo_vm[:, 0:MAIN]
    v = jnp.concatenate([wo_vm[:, MAIN:].astype(F32), jnp.zeros((64, MAIN - REST), F32)], axis=1)
    v = jnp.concatenate([v, jnp.zeros((64, MAIN), F32)], axis=0).T
    own_b[OUT_REST_AT:B_ROWS, :] = v[0:REST].astype(BF16)
    for step in range(1, ys):
        remote(own_b, own_b, wb_send, wb_recv, 2 * ((y + step) % ys) + c, j).start()
    own_f = wf_all.at[c, y]
    for n in range(2):
        at = slice(MAIN * n, MAIN * (n + 1))
        own_f[GATE_AT + 144 * n:GATE_AT + 144 * (n + 1), :] = wg_vm[:, at]
        own_f[GATE_AT + 144 * (n + 2):GATE_AT + 144 * (n + 3), :] = wu_vm[:, at]
        own_f[DOWN_AT + 144 * n:DOWN_AT + 144 * (n + 1), :] = wd_vm[:, at]
    v = [w[:, 256:288].astype(F32) for w in (wg_vm, wu_vm, wd_vm)] + [jnp.zeros((144, 32), F32)]
    own_f[NARROW_AT:DOWN_AT, :] = jnp.concatenate(v, axis=1).astype(BF16)
    ring_start(1)
    to_sibling(y)

    take(wa_all.at[c, pl.ds(0, ys - 1)], wa_recv)
    remote(wa_all.at[c], wa_all.at[c], wa_core_send, wa_core_recv, sibling, j).start()
    take(wa_all.at[1 - c], wa_core_recv)
    rests = []
    for p in range(nx):
        v = wa_all[p // ys, p % ys, QKV_ROWS:A_ROWS, :].astype(F32)
        v = v[0:8] + v[8:16]
        gain_main[p] = v
        rests.append(v)
    for t, v in enumerate(rest_sum(rests)):
        gain_rest[t] = v

    def gain(which, t):
        if t < nx:
            return gain_main[t, which:which + 1, :]
        return gain_rest[t - nx, 4 + which:5 + which, :]

    take(row_all.at[pl.ds(0, blocks - row_blocks)], row_recv)

    def chunk_tile(ref, t):
        at = slice(MAIN * t, MAIN * (t + 1))
        return jnp.concatenate([ref[k, :, at].astype(F32) for k in range(blocks)], axis=0)

    total = None
    for t in range(tiles):
        v = chunk_tile(row_all, t)
        total = v * v if total is None else total + v * v
    scale = lax.rsqrt(jnp.sum(total, axis=1, keepdims=True) / width + EPSILON)
    for t in range(tiles):
        v = chunk_tile(row_all, t)
        norm_in[:, MAIN * t:MAIN * (t + 1)] = (v * scale * gain(0, t)).astype(BF16)
    main_w = wa_all[:, :, 0:MAIN, :].reshape(nx * MAIN, 128)
    rest_w = wa_all[:, :, MAIN:QKV_ROWS, :].reshape(nx * REST, 128)
    qkv = dot(norm_in[:, 0:nx * MAIN], main_w) + dot(norm_in[:, nx * MAIN:nx * MAIN + nx * REST], rest_w)
    lane_half = lax.broadcasted_iota(jnp.int32, (ROWS // 2, 128), 1) < 64
    for part in range(2):
        first, second = qkv[ROWS * part:ROWS * part + 16], qkv[ROWS * part + 16:ROWS * (part + 1)]
        q_out[part] = jnp.where(lane_half, first, pltpu.roll(second, 64, 1)).astype(BF16)
        kv_out[part] = jnp.where(lane_half, pltpu.roll(first, 64, 1), second).astype(BF16)
    for part in range(2):
        put(kv_out.at[part], kv_in.at[j % 8], kv_send, kv_recv, tail_stride * (j // 8), group_of(part))
    for part in range(2):
        group = group_of(part)

        @pl.loop(0, nx)
        def _(step):
            put(q_out.at[part], q_in.at[j], q_send, q_recv, (i + step) % nx, group)

    take(wb_all.at[c, pl.ds(0, ys - 1)], wb_recv)
    remote(wb_all.at[c], wb_all.at[c], wb_core_send, wb_core_recv, sibling, j).start()
    if last_step > 1:
        ring_take(1)

    row = lax.broadcasted_iota(jnp.int32, (ROWS, 1), 0)
    row_step, row_beam = row & 3, jnp.right_shift(row, 2)
    for load in loads[9:12]:
        load.wait()
    length = jnp.full((1, 1), length_ref[0], jnp.int32)
    first_page = jnp.right_shift(jnp.maximum(length - (WINDOW - 1), 0), 7).astype(F32)
    length_wide = length.astype(F32)
    page_iota = lax.broadcasted_iota(jnp.int32, table_vm.shape, 1).astype(F32)
    lane = lax.broadcasted_iota(jnp.int32, (ROWS, PAGE), 1)
    lane_wide = lane.astype(F32)
    lowest = row_step.astype(F32) - (WINDOW - 1)
    masks = []
    for slot in range(4):
        match = table_vm[...] == i * 4 + slot
        page = jnp.sum(jnp.where(match, page_iota, 0.0), axis=1, keepdims=True)
        used = jnp.sum(jnp.where(match, 1.0, 0.0), axis=1, keepdims=True)
        start = jnp.where(used > 0.5, (first_page + page) * PAGE - length_wide, 1.0)
        place = start + lane_wide
        mask = jnp.where((place < 0.0) & (place >= lowest), 1.0, 0.0)
        masks.append(jnp.concatenate([mask, mask], axis=0) > 0.5)
    key_lane = lax.broadcasted_iota(jnp.int32, (ROWS, ROWS), 1)
    key_step, key_beam = key_lane & 3, jnp.right_shift(key_lane, 2)
    beam_lane = lax.broadcasted_iota(jnp.int32, (ROWS, BEAM), 1)
    current = row_beam
    tail = jnp.zeros((ROWS, ROWS), F32)
    for at in range(STEPS - 1, -1, -1):
        hit = (key_step == at) & (row_step >= at) & (key_beam == current)
        tail = jnp.where(hit, 1.0, tail)
        if at:
            chosen = jnp.where(beam_lane == current, parents_vm[at - 1:at, :].astype(F32), 0.0)
            parent = jnp.sum(chosen, axis=1, keepdims=True).astype(jnp.int32)
            current = jnp.where(row_step >= at, parent, current)
    tail_mask = jnp.concatenate([tail, tail], axis=0) > 0.5

    cosine, sine = trig_ref[0], trig_ref[1]
    take(q_in, q_recv)

    def query_tile(at):
        first, second = q_in[at].astype(F32), q_in[at + 1].astype(F32)
        upper = jnp.where(lane_half, first, pltpu.roll(second, 64, 1))
        lower = jnp.where(lane_half, pltpu.roll(first, 64, 1), second)
        return jnp.concatenate([upper, lower], axis=0)

    def kv_tile(source, at):
        total = None
        for m in range(4):
            v = kv_in[source + m].astype(F32)
            v = jnp.concatenate([v, pltpu.roll(v, 64, 1)], axis=0)
            shift = (32 * m - at) % 128
            v = pltpu.roll(v, shift, 1) if shift else v
            total = v if total is None else jnp.where(lane >= 32 * m, v, total)
        return total

    def rotated(u, w):
        return u * cosine - w * sine, w * cosine + u * sine

    def wide(u, w):
        return jnp.concatenate([u, w], axis=1)

    def query_of(h):
        qs = []
        for g in range(2):
            base = 4 * (2 * h + g)
            qs.append(wide(*rotated(query_tile(base), query_tile(base + 2))) * HEAD_DIM ** -0.5)
        return jnp.concatenate(qs, axis=0).astype(BF16)

    tail_num[...] = jnp.zeros(tail_num.shape, F32)
    tail_den[...] = jnp.zeros(tail_den.shape, F32)

    @pl.when(i % tail_stride == 0)
    def _():
        h = i // tail_stride
        take(kv_in, kv_recv)
        key = wide(*rotated(kv_tile(0, 0), kv_tile(4, 0))).astype(BF16)
        value = wide(kv_tile(0, 32), kv_tile(4, 32)).astype(BF16)
        weights = jnp.where(tail_mask, capped(dot_nt(query_of(h), key)), 0.0)
        tail_den[h] = jnp.broadcast_to(jnp.sum(weights, axis=1, keepdims=True), (2 * ROWS, 128))
        tail_num[h] = dot(weights.astype(BF16), value)

    for h in range(kv_heads):
        query = query_of(h)
        den = tail_den[h, :, 0:1]
        num = tail_num[h]
        for slot in range(4):
            at = slice(HEAD_DIM * h, HEAD_DIM * (h + 1))
            weights = jnp.where(masks[slot], capped(dot_nt(query, cache[0, slot, :, at])), 0.0)
            den = den + jnp.sum(weights, axis=1, keepdims=True)
            num = num + dot(weights.astype(BF16), cache[1, slot, :, at])
        den_high = den.astype(BF16).astype(F32)
        den_low = den - den_high
        for g in range(2):
            rows = slice(ROWS * g, ROWS * (g + 1))
            both = jnp.where(lane == row, den_high[rows], 0.0) + jnp.where(lane == row + ROWS, den_low[rows], 0.0)
            both = jnp.broadcast_to(jnp.sum(both, axis=0, keepdims=True), (8, 128))
            for t in range(2):
                v = jnp.concatenate([num[rows, 128 * t:128 * (t + 1)], both], axis=0)
                num_out[2 * (2 * h + g) + t] = v.astype(BF16)

    @pl.loop(1, nx)
    def _(step):
        to = (i + step) % nx
        remote(num_out.at[to], num_in.at[i], num_send, num_recv, to, j).start()

    pltpu.make_async_copy(num_out.at[i], num_in.at[i], num_recv).start()
    if last_step > 2:
        ring_take(2)
    take(num_in, num_recv)
    total = None
    for p in range(nx):
        v = num_in[p].astype(F32)
        total = v if total is None else total + v
    both = jnp.where((lane == row) | (lane == row + ROWS), total[ROWS:ROWS + 1], 0.0)
    total = total[0:ROWS] / jnp.sum(both, axis=1, keepdims=True)
    att_out[0] = total.astype(BF16)
    for k in range(2):
        put(att_out.at[0], att_in.at[half], att_send, att_recv, chunk, 2 * i + k)

    take(att_in, att_recv)
    attended = []
    for part in range(2):
        v = att_in[part].astype(F32)
        attended.append(jnp.where(j % 2 == 1, pltpu.roll(v, 64, 1), v)[:, 0:64])
    attended = jnp.concatenate(attended, axis=0).astype(BF16)
    take(wb_all.at[1 - c], wb_core_recv)

    def put_partial(which, t, v):
        for k in range(blocks):
            part_out[which, k, :, MAIN * t:MAIN * (t + 1)] = v[8 * k:8 * (k + 1)].astype(BF16)

    def put_rest(which, v):
        if v.shape[1] < 128:
            v = jnp.concatenate([v, jnp.zeros((v.shape[0], 128 - v.shape[1]), F32)], axis=1)
        for t in range(rest_tiles):
            put_partial(which, nx + t, v[:, 128 * t:128 * (t + 1)])

    for p in range(nx):
        put_partial(0, p, dot(attended, wb_all[p // ys, p % ys, OUT_AT:OUT_REST_AT, :]))
    rest_w = wb_all[:, :, OUT_REST_AT:B_ROWS, :].reshape(nx * REST, 128)
    put_rest(0, dot_nt(attended, rest_w[:, 0:64]))

    def send_partial(which, dst_all, send_sem, recv_sem):
        for step in range(1, zs):
            to = (zj + step) % zs
            src = part_out.at[which, pl.ds(row_blocks * to, row_blocks)]
            remote(src, dst_all.at[step - 1], send_sem, recv_sem, i, 4 * to + xj).start()

    def add_z(which, ref, dst_all, send_sem, recv_sem):
        for b in range(row_blocks):
            for t in range(tiles):
                at = slice(MAIN * t, MAIN * (t + 1))
                total = part_out[which, first_block + b, :, at].astype(F32)
                for s in range(zs - 1):
                    total = total + ref[s, b, :, at].astype(F32)
                sums[b, :, at] = total
            sum_out[which, b] = sums[b].astype(BF16)
        for step in range(1, 4):
            remote(
                sum_out.at[which], dst_all.at[step - 1], send_sem, recv_sem, i, 4 * zj + (xj + step) % 4
            ).start()

    def add_x(ref, b):
        square = None
        for t in range(tiles):
            at = slice(MAIN * t, MAIN * (t + 1))
            v = sums[b, :, at]
            for s in range(3):
                v = v + ref[s, b, :, at].astype(F32)
            sums[b, :, at] = v
            square = v * v if square is None else square + v * v
        return lax.rsqrt(jnp.sum(square, axis=1, keepdims=True) / width + EPSILON)

    send_partial(0, part_z, part_send, part_recv)
    take(part_z, part_recv)
    add_z(0, part_z, part_x, part_x_send, part_x_recv)
    for step in range(3, last_step):
        ring_take(step)
    take(part_x, part_x_recv)
    for b in range(row_blocks):
        scale = add_x(part_x, b)
        square = None
        for t in range(tiles):
            at = slice(MAIN * t, MAIN * (t + 1))
            v = x_own[b, :, at] + sums[b, :, at] * scale * gain(1, t)
            mixed[b, :, at] = v
            square = v * v if square is None else square + v * v
        scale = lax.rsqrt(jnp.sum(square, axis=1, keepdims=True) / width + EPSILON)
        for t in range(tiles):
            at = slice(MAIN * t, MAIN * (t + 1))
            sums[b, :, at] = mixed[b, :, at] * scale * gain(2, t)
        ff_all[first_block + b] = sums[b].astype(BF16)
    spread(ff_all, ff_send, ff_recv)
    ring_take(last_step)
    take(wf_all.at[1 - c], wf_core_recv)

    take(ff_all.at[pl.ds(0, blocks - row_blocks)], ff_recv)
    for t in range(tiles):
        norm_in[:, MAIN * t:MAIN * (t + 1)] = chunk_tile(ff_all, t).astype(BF16)
    main_x = norm_in[:, 0:nx * MAIN]
    rest_x = norm_in[:, nx * MAIN:nx * MAIN + nx * REST]

    def ff_part(n):
        at = GATE_AT + 144 * n
        main_w = wf_all[:, :, at:at + MAIN, :].reshape(nx * MAIN, 128)
        rest_w = wf_all[:, :, at + MAIN:at + 144, :].reshape(nx * REST, 128)
        return dot(main_x, main_w) + dot(rest_x, rest_w)

    hidden = [(gelu(ff_part(n)) * ff_part(n + 2)).astype(BF16) for n in range(2)]
    both = ff_part(4)
    narrow = gelu(both) * pltpu.roll(both, 96, 1)
    lane_chunk = lax.broadcasted_iota(jnp.int32, narrow.shape, 1)
    narrow = pltpu.roll(jnp.where(lane_chunk < 32, narrow, 0.0), 64, 1)
    hidden.append(narrow.astype(BF16))
    places = [DOWN_AT, DOWN_AT + 144, NARROW_AT]
    for p in range(nx):
        v = None
        for h, at in zip(hidden, places):
            term = dot_nt(h, wf_all[p // ys, p % ys, at:at + MAIN, :])
            v = term if v is None else v + term
        put_partial(1, p, v)
    v = None
    for h, at in zip(hidden, places):
        rest_w = wf_all[:, :, at + MAIN:at + 144, :].reshape(nx * REST, 128)
        term = dot_nt(h, rest_w)
        v = term if v is None else v + term
    put_rest(1, v)
    send_partial(1, down_z, down_send, down_recv)
    take(down_z, down_recv)
    add_z(1, down_z, down_x, down_x_send, down_x_recv)
    take(down_x, down_x_recv)

    share = nx // 4
    for b in range(row_blocks):
        scale = add_x(down_x, b)

        def result(t):
            at = slice(MAIN * t, MAIN * (t + 1))
            return mixed[b, :, at] + sums[b, :, at] * scale * gain(3, t)

        for p in range(nx):
            v = result(nx + p // 8)
            shift = (128 - REST * (p % 8)) % 128
            v = pltpu.roll(v, shift, 1) if shift else v
            last_out[b, p] = jnp.concatenate([result(p), v], axis=1).astype(BF16)
        for m in range(share):
            p = share * xj + m
            to = 2 * (p % ys) + p // ys
            put(
                last_out.at[b, p], last_in.at[(first_block + b) % 4], last_send, last_recv,
                to, group_of(my_part),
            )

    take(last_in, last_recv)
    out_ref[...] = last_in[...]

    x_sent = last_out.at[0]
    take_sent(x_sent, 16, x_send, own_rows, row_blocks)
    take(wa_all.at[c, pl.ds(0, ys - 1)], wa_send)
    take(wa_all.at[c], wa_core_send)
    take(wb_all.at[c, pl.ds(0, ys - 1)], wb_send)
    take(wb_all.at[c], wb_core_send)
    for step in range(1, last_step + 1):
        for side in range(2):
            rows = pl.ds(0, F_ROWS) if step < last_step else pl.ds(CUT * side, F_ROWS - CUT if side else CUT)
            take(wf_all.at[0, 0, rows], ring_send.at[2 * step - 2 + side])
    take(wf_all.at[c], wf_core_send)
    take_sent(q_in, ny, q_send, home)
    take_sent(kv_out, 2, kv_send, home & (i == tail_stride * (j // 8)))
    take(num_out.at[pl.ds(0, nx - 1)], num_send)
    take_sent(att_in, 2, att_send, home & (j // 2 == i))
    take(row_all.at[pl.ds(0, (zs - 1) * row_blocks)], row_send)
    take(ff_all.at[pl.ds(0, (zs - 1) * row_blocks)], ff_send)
    take(part_z, part_send)
    take(down_z, down_send)
    take(part_x, part_x_send)
    take(down_x, down_x_send)
    take_sent(x_sent, row_blocks * share, last_send, own_rows & (piece // share == xj), row_blocks)


def body(
    inputs, cache_pool, lengths, block_table, parents, norm_gains,
    w_query, w_key, w_value, w_out, w_gate, w_up, w_down, *, nx, ny,
):
    columns = inputs.shape[2]
    tiles = nx + max(nx // 8, 1)
    rest_tiles = tiles - nx
    span = tiles * MAIN
    ys = nx // 2
    last_step = ys // 2
    zs = ny // 4
    row_blocks = 8 // zs

    frequency = ROPE_BASE ** (-jnp.arange(128, dtype=F32) * 2.0 / HEAD_DIM)
    positions = lengths[0] + jnp.arange(STEPS, dtype=jnp.int32)
    angles = positions[:, None].astype(F32) * frequency
    trig = jnp.tile(jnp.stack([jnp.cos(angles), jnp.sin(angles)]), (1, BEAM, 1))

    arrays = (
        inputs, cache_pool, lengths, block_table, parents, norm_gains,
        w_query.T, w_key.T, w_value.T, w_out, w_gate, w_up, w_down.T, trig,
    )
    vmem = pl.BlockSpec(memory_space=pltpu.VMEM)
    specs = [pl.BlockSpec(memory_space=pltpu.HBM) for _ in arrays]
    specs[2] = pl.BlockSpec(memory_space=pltpu.SMEM)
    specs[13] = vmem
    dma = pltpu.SemaphoreType.DMA

    def held(*shape, dtype=BF16):
        return pltpu.VMEM(shape, dtype)

    out = pl.pallas_call(
        functools.partial(layer_kernel, nx, ny, nx * columns),
        name="layer",
        out_shape=jax.ShapeDtypeStruct((4, 8, 256), BF16),
        in_specs=specs,
        out_specs=vmem,
        scratch_shapes=[pltpu.VMEM(arrays[k].shape, arrays[k].dtype) for k in (0, 1, 3, 4, 5, 6, 7, 8, 9, 10, 11, 12)]
        + [
            held(2, ys, A_ROWS, 128),
            held(2, ys, B_ROWS, 128),
            held(2, ys, F_ROWS, 128),
            held(nx, 8, 128, dtype=F32),
            held(rest_tiles, 8, 128, dtype=F32),
            held(4, 8, 256),
            held(row_blocks, nx, 8, 256),
            held(row_blocks, 8, span, dtype=F32),
            held(8, 8, span),
            held(8, 8, span),
            held(64, span),
            held(2, ROWS // 2, 128),
            held(2, ROWS // 2, 128),
            held(ny, ROWS // 2, 128),
            held(8, ROWS // 2, 128),
            held(ny // 8, 2 * ROWS, HEAD_DIM, dtype=F32),
            held(ny // 8, 2 * ROWS, 128, dtype=F32),
            held(nx, DEN_ROWS, 128),
            held(nx, DEN_ROWS, 128),
            held(1, ROWS, 128),
            held(2, ROWS, 128),
            held(2, 8, 8, span),
            held(zs - 1, row_blocks, 8, span),
            held(zs - 1, row_blocks, 8, span),
            held(2, row_blocks, 8, span),
            held(3, row_blocks, 8, span),
            held(3, row_blocks, 8, span),
            held(row_blocks, 16, 8, 256),
            held(4, 8, 256),
            held(row_blocks, 8, span, dtype=F32),
            held(row_blocks, 8, span, dtype=F32),
        ]
        + [dma((12,))] + [dma(())] * 4
        + [dma((2 * last_step,)), dma((2 * last_step,))]
        + [dma(())] * 30,
        compiler_params=pltpu.CompilerParams(collective_id=0, has_side_effects=True, vmem_limit_bytes=60 << 20),
    )(*arrays)
    return out[:, :, 0:columns].reshape(inputs.shape)


def solution(mesh):
    return jax.shard_map(
        functools.partial(body, nx=mesh.shape["gx"], ny=mesh.shape["gy"]),
        mesh=mesh,
        in_specs=(
            P("gy", None, "gx"),
            P(None, "gx", "gy", None),
            P("gy"),
            P("gy", None),
            P(None, "gy"),
            P(None, "gx"),
            P("gx", "gy"),
            P("gx", "gy"),
            P("gx", "gy"),
            P("gy", "gx"),
            P("gx", "gy"),
            P("gx", "gy"),
            P("gy", "gx"),
        ),
        out_specs=P("gy", None, "gx"),
        check_vma=False,
    )
```

```python
import functools
import math

import jax
import jax.numpy as jnp
from jax import lax
from jax.experimental import pallas as pl
from jax.experimental.pallas import tpu as pltpu
from jax.sharding import PartitionSpec as P

MESH = pl.DeviceIdType.MESH
F32 = jnp.float32
BF16 = jnp.bfloat16

HEAD_DIM = 256
WINDOW = 4096
PAGE = 128
BEAM = 8
STEPS = 4
ROWS = BEAM * STEPS
EPSILON = 1e-06
SOFT_CAP = 50.0
ROPE_BASE = 10000.0
MAIN = 128
REST = 16

QKV_ROWS = 144
A_ROWS = 160
OUT_AT = 0
OUT_REST_AT = 64
B_ROWS = 80
GATE_AT = 0
NARROW_AT = 576
DOWN_AT = 720
F_ROWS = 1008
CUT = 512
DEN_ROWS = 40


def capped(scores):
    return jnp.exp(SOFT_CAP * jnp.tanh(scores * (1.0 / SOFT_CAP)))


def gelu(v):
    return 0.5 * v * (1.0 + jnp.tanh(math.sqrt(2.0 / math.pi) * (v + 0.044715 * (v * v * v))))


def dot(a, b):
    return jnp.dot(a, b, preferred_element_type=F32)


def dot_nt(a, b):
    return lax.dot_general(a, b, (((1,), (1,)), ((), ())), preferred_element_type=F32)


def layer_kernel(
    nx, ny, width,
    inputs_ref, cache_ref, length_ref, table_ref, parents_ref, gains_ref,
    wq_ref, wk_ref, wv_ref, wo_ref, wg_ref, wu_ref, wd_ref, trig_ref,
    out_ref,
    inputs_vm, cache, table_vm, parents_vm, gains_vm,
    wq_vm, wk_vm, wv_vm, wo_vm, wg_vm, wu_vm, wd_vm,
    wa_all, wb_all, wf_all, gain_main, gain_rest, x_out, x_in, x_own, row_all, ff_all, norm_in,
    q_out, kv_out, q_in, kv_in, tail_num, tail_den, num_out, num_in, att_out, att_in, part_out,
    part_z, down_z, sum_out, part_x, down_x, last_out, last_in, mixed, sums,
    load_sem, wa_send, wa_recv, wa_core_send, wa_core_recv, ring_send, ring_recv, wf_core_send, wf_core_recv,
    wb_send, wb_recv, wb_core_send, wb_core_recv,
    x_send, x_recv, x_row_send, x_row_recv, row_send, row_recv, q_send, q_recv, kv_send, kv_recv, num_send, num_recv,
    att_send, att_recv, part_send, part_recv, part_x_send, part_x_recv, ff_send, ff_recv,
    down_send, down_recv, down_x_send, down_x_recv, last_send, last_recv,
):
    ys = nx // 2
    zs = ny // 4
    kv_heads = ny // 8
    tiles = nx + nx // 8 if nx >= 8 else nx + 1
    rest_tiles = tiles - nx
    blocks = 8
    row_blocks = blocks // zs
    i = lax.axis_index("gx")
    j = lax.axis_index("gy")
    y, c = i // 2, i % 2
    sibling = i + 1 - 2 * c
    piece = c * ys + y
    zj, xj = j // 4, j % 4
    chunk = 2 * ((zj + 2 * xj) % ys) + xj % 2
    half = xj // 2

    def group_of(part):
        x_r = 2 * part + c
        return ((y + 8 * ys - 2 * x_r) % ys) * 4 + x_r

    shift = (y + 8 * ys - 2 * c - 1) % ys if zs == 8 else 0
    first_block = row_blocks * ((zj + zs - shift) % zs)
    share = nx // 4
    my_part = first_block // 4
    home = chunk == i
    own_rows = home & (my_part == half) & (piece // share == xj)
    tail_stride = nx // kv_heads

    def row_of(block):
        there = (chunk // 2 + 8 * ys - 2 * (chunk % 2) - 1) % ys if zs == 8 else 0
        return (block + there) % zs

    def remote(src, dst, send_sem, recv_sem, tx, ty):
        return pltpu.make_async_remote_copy(
            src_ref=src, dst_ref=dst, send_sem=send_sem, recv_sem=recv_sem,
            device_id=(tx, ty), device_id_type=MESH,
        )

    def put(src, dst, send_sem, recv_sem, tx, ty):
        own = (tx == i) & (ty == j)

        @pl.when(jnp.logical_not(own))
        def _():
            remote(src, dst, send_sem, recv_sem, tx, ty).start()

        @pl.when(own)
        def _():
            pltpu.make_async_copy(src, dst, recv_sem).start()

    def take(ref, sem):
        pltpu.make_async_copy(ref, ref, sem).wait()

    def take_sent(ref, count, sem, own, fewer=1):
        @pl.when(own)
        def _():
            take(ref.at[pl.ds(0, count - fewer)], sem)

        @pl.when(jnp.logical_not(own))
        def _():
            take(ref.at[pl.ds(0, count)], sem)

    loads = [
        pltpu.make_async_copy(src, dst, load_sem.at[k])
        for k, (src, dst) in enumerate([
            (inputs_ref, inputs_vm), (wq_ref, wq_vm), (wk_ref, wk_vm), (wv_ref, wv_vm), (gains_ref, gains_vm),
            (wo_ref, wo_vm), (wg_ref, wg_vm), (wu_ref, wu_vm), (wd_ref, wd_vm),
            (table_ref, table_vm), (parents_ref, parents_vm), (cache_ref, cache),
        ])
    ]
    for load in loads:
        load.start()

    barrier = pltpu.get_barrier_semaphore()

    def hello(tx, ty):
        pl.semaphore_signal(barrier, inc=1, device_id=(tx, ty), device_id_type=MESH)

    for step in range(1, ys):
        hello(2 * ((y + step) % ys) + c, j)
    hello(sibling, j)
    for step in range(1, zs):
        hello(i, 4 * ((zj + step) % zs) + xj)
    group = group_of(my_part)

    for m in range(share):
        p = share * xj + m
        to = 2 * (p % ys) + p // ys

        @pl.when(jnp.logical_not((to == i) & (group == j)))
        def _():
            hello(to, group)

    for step in range(1, 4):
        hello(i, 4 * zj + (xj + step) % 4)
    waits = ys + (zs - 1) + 3 + 4 // row_blocks - jnp.where(own_rows, 1, 0)

    loads[0].wait()
    for q in range(4):
        v = jnp.concatenate([inputs_vm[2 * q].astype(F32), inputs_vm[2 * q + 1].astype(F32)], axis=0)
        v = jnp.concatenate([v, jnp.zeros((8, MAIN - REST), F32)], axis=1)
        x_out[q] = v.astype(BF16)
    pl.semaphore_wait(barrier, waits)
    for q in range(4):
        block = half * 4 + q
        put(
            x_out.at[q], x_in.at[piece, block % row_blocks], x_send, x_recv,
            chunk, 4 * row_of(block // row_blocks) + piece // share,
        )
    for load in loads[1:5]:
        load.wait()
    v = jnp.concatenate([wq_vm[...].astype(F32), wk_vm[...].astype(F32), wv_vm[...].astype(F32)], axis=0)
    wa_all[c, y, 0:MAIN, :] = v[:, 0:MAIN].T.astype(BF16)
    v = jnp.concatenate([v[:, MAIN:], jnp.zeros((128, MAIN - REST), F32)], axis=1).T
    wa_all[c, y, MAIN:QKV_ROWS, :] = v[0:REST].astype(BF16)
    v = 1.0 + gains_vm[...]
    v = jnp.concatenate([v, jnp.zeros((4, MAIN - REST), F32)], axis=1)
    v = jnp.concatenate([v[:, 0:MAIN], v[:, MAIN:]], axis=0)
    high = v.astype(BF16).astype(F32)
    wa_all[c, y, QKV_ROWS:A_ROWS, :] = jnp.concatenate([high, v - high], axis=0).astype(BF16)
    for step in range(1, ys):
        remote(wa_all.at[c, y], wa_all.at[c, y], wa_send, wa_recv, 2 * ((y + step) % ys) + c, j).start()

    right = 2 * ((y + 1) % ys) + c
    left = 2 * ((y + ys - 1) % ys) + c
    last_step = ys // 2

    def ring_refs(step):
        from_left = (y + ys - (step - 1)) % ys
        from_right = (y + (step - 1)) % ys
        return from_left, from_right

    def ring_start(step):
        a, b = ring_refs(step)
        src_a, src_b = wf_all.at[c, a], wf_all.at[c, b]
        if step == last_step:
            src_a, src_b = src_a.at[pl.ds(0, CUT)], src_b.at[pl.ds(CUT, F_ROWS - CUT)]
        remote(src_a, src_a, ring_send.at[2 * step - 2], ring_recv.at[2 * step - 2], right, j).start()
        remote(src_b, src_b, ring_send.at[2 * step - 1], ring_recv.at[2 * step - 1], left, j).start()

    def to_sibling(k):
        remote(wf_all.at[c, k], wf_all.at[c, k], wf_core_send, wf_core_recv, sibling, j).start()

    def ring_take(step):
        a = (y + ys - step) % ys
        b = (y + step) % ys
        ref_a, ref_b = wf_all.at[c, a], wf_all.at[c, b]
        if step == last_step:
            take(ref_a.at[pl.ds(0, CUT)], ring_recv.at[2 * step - 2])
            take(ref_b.at[pl.ds(CUT, F_ROWS - CUT)], ring_recv.at[2 * step - 1])
            to_sibling(a)
        else:
            take(ref_a, ring_recv.at[2 * step - 2])
            take(ref_b, ring_recv.at[2 * step - 1])
            ring_start(step + 1)
            to_sibling(a)
            to_sibling(b)

    def rest_sum(pieces):
        out = []
        for t in range(rest_tiles):
            total = None
            for k in range(min(8, nx)):
                v = pieces[8 * t + k]
                v = pltpu.roll(v, REST * k, 1) if k else v
                total = v if total is None else total + v
            out.append(total)
        return out

    def spread(ref, send_sem, recv_sem):
        src = ref.at[pl.ds(first_block, row_blocks)]
        for step in range(1, zs):
            remote(src, src, send_sem, recv_sem, i, 4 * ((zj + step) % zs) + xj).start()

    quarter = x_in.at[pl.ds(share * xj, share)]
    take(quarter, x_recv)
    for step in range(1, 4):
        remote(quarter, quarter, x_row_send, x_row_recv, i, 4 * zj + (xj + step) % 4).start()
    take(x_in.at[pl.ds(0, 3 * share)], x_row_recv)
    for b in range(row_blocks):
        rests = []
        for p in range(nx):
            v = x_in[p, b].astype(F32)
            x_own[b, :, MAIN * p:MAIN * (p + 1)] = v[:, 0:MAIN]
            rests.append(v[:, MAIN:2 * MAIN])
        for t, v in enumerate(rest_sum(rests)):
            x_own[b, :, MAIN * (nx + t):MAIN * (nx + t + 1)] = v
        row_all[first_block + b] = x_own[b].astype(BF16)
    spread(row_all, row_send, row_recv)

    for load in loads[5:9]:
        load.wait()
    own_b = wb_all.at[c, y]
    own_b[OUT_AT:OUT_REST_AT, :] = wo_vm[:, 0:MAIN]
    v = jnp.concatenate([wo_vm[:, MAIN:].astype(F32), jnp.zeros((64, MAIN - REST), F32)], axis=1)
    v = jnp.concatenate([v, jnp.zeros((64, MAIN), F32)], axis=0).T
    own_b[OUT_REST_AT:B_ROWS, :] = v[0:REST].astype(BF16)
    for step in range(1, ys):
        remote(own_b, own_b, wb_send, wb_recv, 2 * ((y + step) % ys) + c, j).start()
    own_f = wf_all.at[c, y]
    for n in range(2):
        at = slice(MAIN * n, MAIN * (n + 1))
        own_f[GATE_AT + 144 * n:GATE_AT + 144 * (n + 1), :] = wg_vm[:, at]
        own_f[GATE_AT + 144 * (n + 2):GATE_AT + 144 * (n + 3), :] = wu_vm[:, at]
        own_f[DOWN_AT + 144 * n:DOWN_AT + 144 * (n + 1), :] = wd_vm[:, at]
    v = [w[:, 256:288].astype(F32) for w in (wg_vm, wu_vm, wd_vm)] + [jnp.zeros((144, 32), F32)]
    own_f[NARROW_AT:DOWN_AT, :] = jnp.concatenate(v, axis=1).astype(BF16)
    ring_start(1)
    to_sibling(y)

    take(wa_all.at[c, pl.ds(0, ys - 1)], wa_recv)
    remote(wa_all.at[c], wa_all.at[c], wa_core_send, wa_core_recv, sibling, j).start()
    take(wa_all.at[1 - c], wa_core_recv)
    rests = []
    for p in range(nx):
        v = wa_all[p // ys, p % ys, QKV_ROWS:A_ROWS, :].astype(F32)
        v = v[0:8] + v[8:16]
        gain_main[p] = v
        rests.append(v)
    for t, v in enumerate(rest_sum(rests)):
        gain_rest[t] = v

    def gain(which, t):
        if t < nx:
            return gain_main[t, which:which + 1, :]
        return gain_rest[t - nx, 4 + which:5 + which, :]

    take(row_all.at[pl.ds(0, blocks - row_blocks)], row_recv)

    def chunk_tile(ref, t):
        at = slice(MAIN * t, MAIN * (t + 1))
        return jnp.concatenate([ref[k, :, at].astype(F32) for k in range(blocks)], axis=0)

    total = None
    for t in range(tiles):
        v = chunk_tile(row_all, t)
        total = v * v if total is None else total + v * v
    scale = lax.rsqrt(jnp.sum(total, axis=1, keepdims=True) / width + EPSILON)
    for t in range(tiles):
        v = chunk_tile(row_all, t)
        norm_in[:, MAIN * t:MAIN * (t + 1)] = (v * scale * gain(0, t)).astype(BF16)
    main_w = wa_all[:, :, 0:MAIN, :].reshape(nx * MAIN, 128)
    rest_w = wa_all[:, :, MAIN:QKV_ROWS, :].reshape(nx * REST, 128)
    qkv = dot(norm_in[:, 0:nx * MAIN], main_w) + dot(norm_in[:, nx * MAIN:nx * MAIN + nx * REST], rest_w)
    lane_half = lax.broadcasted_iota(jnp.int32, (ROWS // 2, 128), 1) < 64
    for part in range(2):
        first, second = qkv[ROWS * part:ROWS * part + 16], qkv[ROWS * part + 16:ROWS * (part + 1)]
        q_out[part] = jnp.where(lane_half, first, pltpu.roll(second, 64, 1)).astype(BF16)
        kv_out[part] = jnp.where(lane_half, pltpu.roll(first, 64, 1), second).astype(BF16)
    for part in range(2):
        put(kv_out.at[part], kv_in.at[j % 8], kv_send, kv_recv, tail_stride * (j // 8), group_of(part))
    for part in range(2):
        group = group_of(part)

        @pl.loop(0, nx)
        def _(step):
            put(q_out.at[part], q_in.at[j], q_send, q_recv, (i + step) % nx, group)

    take(wb_all.at[c, pl.ds(0, ys - 1)], wb_recv)
    remote(wb_all.at[c], wb_all.at[c], wb_core_send, wb_core_recv, sibling, j).start()
    row = lax.broadcasted_iota(jnp.int32, (ROWS, 1), 0)
    row_step, row_beam = row & 3, jnp.right_shift(row, 2)
    for load in loads[9:12]:
        load.wait()
    length = jnp.full((1, 1), length_ref[0], jnp.int32)
    first_page = jnp.right_shift(jnp.maximum(length - (WINDOW - 1), 0), 7).astype(F32)
    length_wide = length.astype(F32)
    page_iota = lax.broadcasted_iota(jnp.int32, table_vm.shape, 1).astype(F32)
    lane = lax.broadcasted_iota(jnp.int32, (ROWS, PAGE), 1)
    lane_wide = lane.astype(F32)
    lowest = row_step.astype(F32) - (WINDOW - 1)
    masks = []
    for slot in range(4):
        match = table_vm[...] == i * 4 + slot
        page = jnp.sum(jnp.where(match, page_iota, 0.0), axis=1, keepdims=True)
        used = jnp.sum(jnp.where(match, 1.0, 0.0), axis=1, keepdims=True)
        start = jnp.where(used > 0.5, (first_page + page) * PAGE - length_wide, 1.0)
        place = start + lane_wide
        mask = jnp.where((place < 0.0) & (place >= lowest), 1.0, 0.0)
        masks.append(jnp.concatenate([mask, mask], axis=0) > 0.5)
    key_lane = lax.broadcasted_iota(jnp.int32, (ROWS, ROWS), 1)
    key_step, key_beam = key_lane & 3, jnp.right_shift(key_lane, 2)
    beam_lane = lax.broadcasted_iota(jnp.int32, (ROWS, BEAM), 1)
    current = row_beam
    tail = jnp.zeros((ROWS, ROWS), F32)
    for at in range(STEPS - 1, -1, -1):
        hit = (key_step == at) & (row_step >= at) & (key_beam == current)
        tail = jnp.where(hit, 1.0, tail)
        if at:
            chosen = jnp.where(beam_lane == current, parents_vm[at - 1:at, :].astype(F32), 0.0)
            parent = jnp.sum(chosen, axis=1, keepdims=True).astype(jnp.int32)
            current = jnp.where(row_step >= at, parent, current)
    tail_mask = jnp.concatenate([tail, tail], axis=0) > 0.5

    cosine, sine = trig_ref[0], trig_ref[1]
    take(q_in, q_recv)

    def query_tile(at):
        first, second = q_in[at].astype(F32), q_in[at + 1].astype(F32)
        upper = jnp.where(lane_half, first, pltpu.roll(second, 64, 1))
        lower = jnp.where(lane_half, pltpu.roll(first, 64, 1), second)
        return jnp.concatenate([upper, lower], axis=0)

    def kv_tile(source, at):
        total = None
        for m in range(4):
            v = kv_in[source + m].astype(F32)
            v = jnp.concatenate([v, pltpu.roll(v, 64, 1)], axis=0)
            shift = (32 * m - at) % 128
            v = pltpu.roll(v, shift, 1) if shift else v
            total = v if total is None else jnp.where(lane >= 32 * m, v, total)
        return total

    def rotated(u, w):
        return u * cosine - w * sine, w * cosine + u * sine

    def wide(u, w):
        return jnp.concatenate([u, w], axis=1)

    def query_of(h):
        qs = []
        for g in range(2):
            base = 4 * (2 * h + g)
            qs.append(wide(*rotated(query_tile(base), query_tile(base + 2))) * HEAD_DIM ** -0.5)
        return jnp.concatenate(qs, axis=0).astype(BF16)

    tail_num[...] = jnp.zeros(tail_num.shape, F32)
    tail_den[...] = jnp.zeros(tail_den.shape, F32)

    @pl.when(i % tail_stride == 0)
    def _():
        h = i // tail_stride
        take(kv_in, kv_recv)
        key = wide(*rotated(kv_tile(0, 0), kv_tile(4, 0))).astype(BF16)
        value = wide(kv_tile(0, 32), kv_tile(4, 32)).astype(BF16)
        weights = jnp.where(tail_mask, capped(dot_nt(query_of(h), key)), 0.0)
        tail_den[h] = jnp.broadcast_to(jnp.sum(weights, axis=1, keepdims=True), (2 * ROWS, 128))
        tail_num[h] = dot(weights.astype(BF16), value)

    for h in range(kv_heads):
        query = query_of(h)
        den = tail_den[h, :, 0:1]
        num = tail_num[h]
        for slot in range(4):
            at = slice(HEAD_DIM * h, HEAD_DIM * (h + 1))
            weights = jnp.where(masks[slot], capped(dot_nt(query, cache[0, slot, :, at])), 0.0)
            den = den + jnp.sum(weights, axis=1, keepdims=True)
            num = num + dot(weights.astype(BF16), cache[1, slot, :, at])
        den_high = den.astype(BF16).astype(F32)
        den_low = den - den_high
        for g in range(2):
            rows = slice(ROWS * g, ROWS * (g + 1))
            both = jnp.where(lane == row, den_high[rows], 0.0) + jnp.where(lane == row + ROWS, den_low[rows], 0.0)
            both = jnp.broadcast_to(jnp.sum(both, axis=0, keepdims=True), (8, 128))
            for t in range(2):
                v = jnp.concatenate([num[rows, 128 * t:128 * (t + 1)], both], axis=0)
                num_out[2 * (2 * h + g) + t] = v.astype(BF16)

    @pl.loop(1, nx)
    def _(step):
        to = (i + step) % nx
        remote(num_out.at[to], num_in.at[i], num_send, num_recv, to, j).start()

    pltpu.make_async_copy(num_out.at[i], num_in.at[i], num_recv).start()
    take(num_in, num_recv)
    total = None
    for p in range(nx):
        v = num_in[p].astype(F32)
        total = v if total is None else total + v
    both = jnp.where((lane == row) | (lane == row + ROWS), total[ROWS:ROWS + 1], 0.0)
    total = total[0:ROWS] / jnp.sum(both, axis=1, keepdims=True)
    att_out[0] = total.astype(BF16)
    for k in range(2):
        put(att_out.at[0], att_in.at[half], att_send, att_recv, chunk, 2 * i + k)
    if last_step > 1:
        ring_take(1)

    take(att_in, att_recv)
    attended = []
    for part in range(2):
        v = att_in[part].astype(F32)
        attended.append(jnp.where(j % 2 == 1, pltpu.roll(v, 64, 1), v)[:, 0:64])
    attended = jnp.concatenate(attended, axis=0).astype(BF16)
    take(wb_all.at[1 - c], wb_core_recv)

    def put_partial(which, t, v):
        for k in range(blocks):
            part_out[which, k, :, MAIN * t:MAIN * (t + 1)] = v[8 * k:8 * (k + 1)].astype(BF16)

    def put_rest(which, v):
        if v.shape[1] < 128:
            v = jnp.concatenate([v, jnp.zeros((v.shape[0], 128 - v.shape[1]), F32)], axis=1)
        for t in range(rest_tiles):
            put_partial(which, nx + t, v[:, 128 * t:128 * (t + 1)])

    for p in range(nx):
        put_partial(0, p, dot(attended, wb_all[p // ys, p % ys, OUT_AT:OUT_REST_AT, :]))
    rest_w = wb_all[:, :, OUT_REST_AT:B_ROWS, :].reshape(nx * REST, 128)
    put_rest(0, dot_nt(attended, rest_w[:, 0:64]))

    def send_partial(which, dst_all, send_sem, recv_sem):
        for step in range(1, zs):
            to = (zj + step) % zs
            src = part_out.at[which, pl.ds(row_blocks * ((to + zs - shift) % zs), row_blocks)]
            remote(src, dst_all.at[step - 1], send_sem, recv_sem, i, 4 * to + xj).start()

    def add_z(which, ref, dst_all, send_sem, recv_sem):
        for b in range(row_blocks):
            for t in range(tiles):
                at = slice(MAIN * t, MAIN * (t + 1))
                total = part_out[which, first_block + b, :, at].astype(F32)
                for s in range(zs - 1):
                    total = total + ref[s, b, :, at].astype(F32)
                sums[b, :, at] = total
            sum_out[which, b] = sums[b].astype(BF16)
        for step in range(1, 4):
            remote(
                sum_out.at[which], dst_all.at[step - 1], send_sem, recv_sem, i, 4 * zj + (xj + step) % 4
            ).start()

    def add_x(ref, b):
        square = None
        for t in range(tiles):
            at = slice(MAIN * t, MAIN * (t + 1))
            v = sums[b, :, at]
            for s in range(3):
                v = v + ref[s, b, :, at].astype(F32)
            sums[b, :, at] = v
            square = v * v if square is None else square + v * v
        return lax.rsqrt(jnp.sum(square, axis=1, keepdims=True) / width + EPSILON)

    send_partial(0, part_z, part_send, part_recv)
    if last_step > 2:
        ring_take(2)
    take(part_z, part_recv)
    add_z(0, part_z, part_x, part_x_send, part_x_recv)
    for step in range(3, last_step):
        ring_take(step)
    take(part_x, part_x_recv)
    for b in range(row_blocks):
        scale = add_x(part_x, b)
        square = None
        for t in range(tiles):
            at = slice(MAIN * t, MAIN * (t + 1))
            v = x_own[b, :, at] + sums[b, :, at] * scale * gain(1, t)
            mixed[b, :, at] = v
            square = v * v if square is None else square + v * v
        scale = lax.rsqrt(jnp.sum(square, axis=1, keepdims=True) / width + EPSILON)
        for t in range(tiles):
            at = slice(MAIN * t, MAIN * (t + 1))
            sums[b, :, at] = mixed[b, :, at] * scale * gain(2, t)
        ff_all[first_block + b] = sums[b].astype(BF16)
    spread(ff_all, ff_send, ff_recv)
    ring_take(last_step)
    take(wf_all.at[1 - c], wf_core_recv)

    take(ff_all.at[pl.ds(0, blocks - row_blocks)], ff_recv)
    for t in range(tiles):
        norm_in[:, MAIN * t:MAIN * (t + 1)] = chunk_tile(ff_all, t).astype(BF16)
    main_x = norm_in[:, 0:nx * MAIN]
    rest_x = norm_in[:, nx * MAIN:nx * MAIN + nx * REST]

    def ff_part(n):
        at = GATE_AT + 144 * n
        main_w = wf_all[:, :, at:at + MAIN, :].reshape(nx * MAIN, 128)
        rest_w = wf_all[:, :, at + MAIN:at + 144, :].reshape(nx * REST, 128)
        return dot(main_x, main_w) + dot(rest_x, rest_w)

    hidden = [(gelu(ff_part(n)) * ff_part(n + 2)).astype(BF16) for n in range(2)]
    both = ff_part(4)
    narrow = gelu(both) * pltpu.roll(both, 96, 1)
    lane_chunk = lax.broadcasted_iota(jnp.int32, narrow.shape, 1)
    narrow = pltpu.roll(jnp.where(lane_chunk < 32, narrow, 0.0), 64, 1)
    hidden.append(narrow.astype(BF16))
    places = [DOWN_AT, DOWN_AT + 144, NARROW_AT]
    for p in range(nx):
        v = None
        for h, at in zip(hidden, places):
            term = dot_nt(h, wf_all[p // ys, p % ys, at:at + MAIN, :])
            v = term if v is None else v + term
        put_partial(1, p, v)
    v = None
    for h, at in zip(hidden, places):
        rest_w = wf_all[:, :, at + MAIN:at + 144, :].reshape(nx * REST, 128)
        term = dot_nt(h, rest_w)
        v = term if v is None else v + term
    put_rest(1, v)
    send_partial(1, down_z, down_send, down_recv)
    take(down_z, down_recv)
    add_z(1, down_z, down_x, down_x_send, down_x_recv)
    take(down_x, down_x_recv)

    for b in range(row_blocks):
        scale = add_x(down_x, b)

        def result(t):
            at = slice(MAIN * t, MAIN * (t + 1))
            return mixed[b, :, at] + sums[b, :, at] * scale * gain(3, t)

        for p in range(nx):
            v = result(nx + p // 8)
            shift = (128 - REST * (p % 8)) % 128
            v = pltpu.roll(v, shift, 1) if shift else v
            last_out[b, p] = jnp.concatenate([result(p), v], axis=1).astype(BF16)
        for m in range(share):
            p = share * xj + m
            to = 2 * (p % ys) + p // ys
            put(
                last_out.at[b, p], last_in.at[(first_block + b) % 4], last_send, last_recv,
                to, group_of(my_part),
            )

    take(last_in, last_recv)
    out_ref[...] = last_in[...]

    x_sent = last_out.at[0]
    take_sent(x_sent, 4, x_send, own_rows, row_blocks)
    take(x_in.at[pl.ds(0, 3 * share)], x_row_send)
    take(wa_all.at[c, pl.ds(0, ys - 1)], wa_send)
    take(wa_all.at[c], wa_core_send)
    take(wb_all.at[c, pl.ds(0, ys - 1)], wb_send)
    take(wb_all.at[c], wb_core_send)
    for step in range(1, last_step + 1):
        for side in range(2):
            rows = pl.ds(0, F_ROWS) if step < last_step else pl.ds(CUT * side, F_ROWS - CUT if side else CUT)
            take(wf_all.at[0, 0, rows], ring_send.at[2 * step - 2 + side])
    take(wf_all.at[c], wf_core_send)
    take_sent(q_in, ny, q_send, home)
    take_sent(kv_out, 2, kv_send, home & (i == tail_stride * (j // 8)))
    take(num_out.at[pl.ds(0, nx - 1)], num_send)
    take_sent(att_in, 2, att_send, home & (j // 2 == i))
    take(row_all.at[pl.ds(0, (zs - 1) * row_blocks)], row_send)
    take(ff_all.at[pl.ds(0, (zs - 1) * row_blocks)], ff_send)
    take(part_z, part_send)
    take(down_z, down_send)
    take(part_x, part_x_send)
    take(down_x, down_x_send)
    take_sent(x_sent, row_blocks * share, last_send, own_rows, row_blocks)


def body(
    inputs, cache_pool, lengths, block_table, parents, norm_gains,
    w_query, w_key, w_value, w_out, w_gate, w_up, w_down, *, nx, ny,
):
    columns = inputs.shape[2]
    tiles = nx + max(nx // 8, 1)
    rest_tiles = tiles - nx
    span = tiles * MAIN
    ys = nx // 2
    last_step = ys // 2
    zs = ny // 4
    row_blocks = 8 // zs

    frequency = ROPE_BASE ** (-jnp.arange(128, dtype=F32) * 2.0 / HEAD_DIM)
    positions = lengths[0] + jnp.arange(STEPS, dtype=jnp.int32)
    angles = positions[:, None].astype(F32) * frequency
    trig = jnp.tile(jnp.stack([jnp.cos(angles), jnp.sin(angles)]), (1, BEAM, 1))

    arrays = (
        inputs, cache_pool, lengths, block_table, parents, norm_gains,
        w_query.T, w_key.T, w_value.T, w_out, w_gate, w_up, w_down.T, trig,
    )
    vmem = pl.BlockSpec(memory_space=pltpu.VMEM)
    specs = [pl.BlockSpec(memory_space=pltpu.HBM) for _ in arrays]
    specs[2] = pl.BlockSpec(memory_space=pltpu.SMEM)
    specs[13] = vmem
    dma = pltpu.SemaphoreType.DMA

    def held(*shape, dtype=BF16):
        return pltpu.VMEM(shape, dtype)

    out = pl.pallas_call(
        functools.partial(layer_kernel, nx, ny, nx * columns),
        name="layer",
        out_shape=jax.ShapeDtypeStruct((4, 8, 256), BF16),
        in_specs=specs,
        out_specs=vmem,
        scratch_shapes=[pltpu.VMEM(arrays[k].shape, arrays[k].dtype) for k in (0, 1, 3, 4, 5, 6, 7, 8, 9, 10, 11, 12)]
        + [
            held(2, ys, A_ROWS, 128),
            held(2, ys, B_ROWS, 128),
            held(2, ys, F_ROWS, 128),
            held(nx, 8, 128, dtype=F32),
            held(rest_tiles, 8, 128, dtype=F32),
            held(4, 8, 256),
            held(nx, row_blocks, 8, 256),
            held(row_blocks, 8, span, dtype=F32),
            held(8, 8, span),
            held(8, 8, span),
            held(64, span),
            held(2, ROWS // 2, 128),
            held(2, ROWS // 2, 128),
            held(ny, ROWS // 2, 128),
            held(8, ROWS // 2, 128),
            held(ny // 8, 2 * ROWS, HEAD_DIM, dtype=F32),
            held(ny // 8, 2 * ROWS, 128, dtype=F32),
            held(nx, DEN_ROWS, 128),
            held(nx, DEN_ROWS, 128),
            held(1, ROWS, 128),
            held(2, ROWS, 128),
            held(2, 8, 8, span),
            held(zs - 1, row_blocks, 8, span),
            held(zs - 1, row_blocks, 8, span),
            held(2, row_blocks, 8, span),
            held(3, row_blocks, 8, span),
            held(3, row_blocks, 8, span),
            held(row_blocks, 16, 8, 256),
            held(4, 8, 256),
            held(row_blocks, 8, span, dtype=F32),
            held(row_blocks, 8, span, dtype=F32),
        ]
        + [dma((12,))] + [dma(())] * 4
        + [dma((2 * last_step,)), dma((2 * last_step,))]
        + [dma(())] * 32,
        compiler_params=pltpu.CompilerParams(collective_id=0, has_side_effects=True, vmem_limit_bytes=60 << 20),
    )(*arrays)
    return out[:, :, 0:columns].reshape(inputs.shape)


def solution(mesh):
    return jax.shard_map(
        functools.partial(body, nx=mesh.shape["gx"], ny=mesh.shape["gy"]),
        mesh=mesh,
        in_specs=(
            P("gy", None, "gx"),
            P(None, "gx", "gy", None),
            P("gy"),
            P("gy", None),
            P(None, "gy"),
            P(None, "gx"),
            P("gx", "gy"),
            P("gx", "gy"),
            P("gx", "gy"),
            P("gy", "gx"),
            P("gx", "gy"),
            P("gx", "gy"),
            P("gy", "gx"),
        ),
        out_specs=P("gy", None, "gx"),
        check_vma=False,
    )
```

```python
import functools
import math

import jax
import jax.numpy as jnp
from jax import lax
from jax.experimental import pallas as pl
from jax.experimental.pallas import tpu as pltpu
from jax.sharding import PartitionSpec as P

MESH = pl.DeviceIdType.MESH
F32 = jnp.float32
BF16 = jnp.bfloat16

HEAD_DIM = 256
WINDOW = 4096
PAGE = 128
BEAM = 8
STEPS = 4
ROWS = BEAM * STEPS
EPSILON = 1e-06
SOFT_CAP = 50.0
ROPE_BASE = 10000.0
MAIN = 128
REST = 16

QKV_ROWS = 144
A_ROWS = 160
OUT_AT = 0
OUT_REST_AT = 64
B_ROWS = 80
GATE_AT = 0
NARROW_AT = 576
DOWN_AT = 720
F_ROWS = 1008
CUT = 512
DEN_ROWS = 40


def capped(scores):
    return jnp.exp(SOFT_CAP * jnp.tanh(scores * (1.0 / SOFT_CAP)))


def gelu(v):
    return 0.5 * v * (1.0 + jnp.tanh(math.sqrt(2.0 / math.pi) * (v + 0.044715 * (v * v * v))))


def dot(a, b):
    return jnp.dot(a, b, preferred_element_type=F32)


def dot_nt(a, b):
    return lax.dot_general(a, b, (((1,), (1,)), ((), ())), preferred_element_type=F32)


def layer_kernel(
    nx, ny, width,
    inputs_ref, cache_ref, length_ref, table_ref, parents_ref, gains_ref,
    wq_ref, wk_ref, wv_ref, wo_ref, wg_ref, wu_ref, wd_ref, cosine_ref, sine_ref,
    out_ref,
    inputs_vm, cache, table_vm, parents_vm, gains_vm,
    wq_vm, wk_vm, wv_vm, wo_vm, wg_vm, wu_vm, wd_vm,
    wa_all, wb_all, wf_all, gain_main, gain_rest, x_out, x_in, x_own, row_all, ff_all, norm_in,
    q_out, kv_out, q_in, kv_in, tail_num, tail_den, num_out, num_in, att_out, att_in, part_out,
    part_z, down_z, sum_out, part_x, down_x, last_out, last_in, mixed, sums,
    load_sem, wa_send, wa_recv, wa_core_send, wa_core_recv, ring_send, ring_recv, wf_core_send, wf_core_recv,
    wb_send, wb_recv, wb_core_send, wb_core_recv,
    x_send, x_recv, x_row_send, x_row_recv, row_send, row_recv, q_send, q_recv, kv_send, kv_recv, num_send, num_recv,
    att_send, att_recv, part_send, part_recv, part_x_send, part_x_recv, ff_send, ff_recv,
    down_send, down_recv, down_x_send, down_x_recv, last_send, last_recv,
):
    ys = nx // 2
    zs = ny // 4
    kv_heads = ny // 8
    tiles = nx + nx // 8 if nx >= 8 else nx + 1
    rest_tiles = tiles - nx
    blocks = 8
    row_blocks = blocks // zs
    z_steps = sorted(range(1, zs), key=lambda d: -min(d, zs - d))
    y_steps = sorted(range(1, ys), key=lambda d: -min(d, ys - d))
    i = lax.axis_index("gx")
    j = lax.axis_index("gy")
    y, c = i // 2, i % 2
    sibling = i + 1 - 2 * c
    piece = c * ys + y
    zj, xj = j // 4, j % 4
    chunk = 2 * ((zj + 2 * xj) % ys) + xj % 2
    half = xj // 2

    def group_of(part):
        x_r = 2 * part + c
        return ((y + 8 * ys - 2 * x_r) % ys) * 4 + x_r

    shift = (y + 8 * ys - 2 * c - 1) % ys if zs == 8 else 0
    first_block = row_blocks * ((zj + zs - shift) % zs)
    share = nx // 4
    my_part = first_block // 4
    home = chunk == i
    own_rows = home & (my_part == half) & (piece // share == xj)
    tail_stride = nx // kv_heads

    def row_of(block):
        there = (chunk // 2 + 8 * ys - 2 * (chunk % 2) - 1) % ys if zs == 8 else 0
        return (block + there) % zs

    def remote(src, dst, send_sem, recv_sem, tx, ty):
        return pltpu.make_async_remote_copy(
            src_ref=src, dst_ref=dst, send_sem=send_sem, recv_sem=recv_sem,
            device_id=(tx, ty), device_id_type=MESH,
        )

    def put(src, dst, send_sem, recv_sem, tx, ty):
        own = (tx == i) & (ty == j)

        @pl.when(jnp.logical_not(own))
        def _():
            remote(src, dst, send_sem, recv_sem, tx, ty).start()

        @pl.when(own)
        def _():
            pltpu.make_async_copy(src, dst, recv_sem).start()

    def take(ref, sem):
        pltpu.make_async_copy(ref, ref, sem).wait()

    def take_sent(ref, count, sem, own, fewer=1):
        @pl.when(own)
        def _():
            take(ref.at[pl.ds(0, count - fewer)], sem)

        @pl.when(jnp.logical_not(own))
        def _():
            take(ref.at[pl.ds(0, count)], sem)

    loads = [
        pltpu.make_async_copy(src, dst, load_sem.at[k])
        for k, (src, dst) in enumerate([
            (inputs_ref, inputs_vm), (wq_ref, wq_vm), (wk_ref, wk_vm), (wv_ref, wv_vm), (gains_ref, gains_vm),
            (wo_ref, wo_vm), (wg_ref, wg_vm), (wu_ref, wu_vm), (wd_ref, wd_vm),
            (table_ref, table_vm), (parents_ref, parents_vm), (cache_ref, cache),
        ])
    ]
    for load in loads:
        load.start()

    barrier = pltpu.get_barrier_semaphore()

    def hello(tx, ty):
        pl.semaphore_signal(barrier, inc=1, device_id=(tx, ty), device_id_type=MESH)

    for step in range(1, ys):
        hello(2 * ((y + step) % ys) + c, j)
    hello(sibling, j)
    for step in range(1, zs):
        hello(i, 4 * ((zj + step) % zs) + xj)
    group = group_of(my_part)

    for m in range(share):
        p = share * xj + m
        to = 2 * (p % ys) + p // ys

        @pl.when(jnp.logical_not((to == i) & (group == j)))
        def _():
            hello(to, group)

    for step in range(1, 4):
        hello(i, 4 * zj + (xj + step) % 4)
    waits = ys + (zs - 1) + 3 + 4 // row_blocks - jnp.where(own_rows, 1, 0)

    loads[0].wait()
    for q in range(4):
        v = jnp.concatenate([inputs_vm[2 * q].astype(F32), inputs_vm[2 * q + 1].astype(F32)], axis=0)
        v = jnp.concatenate([v, jnp.zeros((8, MAIN - REST), F32)], axis=1)
        x_out[q] = v.astype(BF16)
    pl.semaphore_wait(barrier, waits)
    for q in range(4):
        block = half * 4 + q
        put(
            x_out.at[q], x_in.at[piece, block % row_blocks], x_send, x_recv,
            chunk, 4 * row_of(block // row_blocks) + piece // share,
        )
    for load in loads[1:5]:
        load.wait()
    v = jnp.concatenate([wq_vm[...].astype(F32), wk_vm[...].astype(F32), wv_vm[...].astype(F32)], axis=0)
    wa_all[c, y, 0:MAIN, :] = v[:, 0:MAIN].T.astype(BF16)
    v = jnp.concatenate([v[:, MAIN:], jnp.zeros((128, MAIN - REST), F32)], axis=1).T
    wa_all[c, y, MAIN:QKV_ROWS, :] = v[0:REST].astype(BF16)
    v = 1.0 + gains_vm[...]
    v = jnp.concatenate([v, jnp.zeros((4, MAIN - REST), F32)], axis=1)
    v = jnp.concatenate([v[:, 0:MAIN], v[:, MAIN:]], axis=0)
    high = v.astype(BF16).astype(F32)
    wa_all[c, y, QKV_ROWS:A_ROWS, :] = jnp.concatenate([high, v - high], axis=0).astype(BF16)
    for step in y_steps:
        remote(wa_all.at[c, y], wa_all.at[c, y], wa_send, wa_recv, 2 * ((y + step) % ys) + c, j).start()

    right = 2 * ((y + 1) % ys) + c
    left = 2 * ((y + ys - 1) % ys) + c
    last_step = ys // 2

    def ring_refs(step):
        from_left = (y + ys - (step - 1)) % ys
        from_right = (y + (step - 1)) % ys
        return from_left, from_right

    def ring_start(step):
        a, b = ring_refs(step)
        src_a, src_b = wf_all.at[c, a], wf_all.at[c, b]
        if step == last_step:
            src_a, src_b = src_a.at[pl.ds(0, CUT)], src_b.at[pl.ds(CUT, F_ROWS - CUT)]
        remote(src_a, src_a, ring_send.at[2 * step - 2], ring_recv.at[2 * step - 2], right, j).start()
        remote(src_b, src_b, ring_send.at[2 * step - 1], ring_recv.at[2 * step - 1], left, j).start()

    def to_sibling(k):
        remote(wf_all.at[c, k], wf_all.at[c, k], wf_core_send, wf_core_recv, sibling, j).start()

    def ring_take(step):
        a = (y + ys - step) % ys
        b = (y + step) % ys
        ref_a, ref_b = wf_all.at[c, a], wf_all.at[c, b]
        if step == last_step:
            take(ref_a.at[pl.ds(0, CUT)], ring_recv.at[2 * step - 2])
            take(ref_b.at[pl.ds(CUT, F_ROWS - CUT)], ring_recv.at[2 * step - 1])
            to_sibling(a)
        else:
            take(ref_a, ring_recv.at[2 * step - 2])
            take(ref_b, ring_recv.at[2 * step - 1])
            ring_start(step + 1)
            to_sibling(a)
            to_sibling(b)

    def rest_sum(pieces):
        out = []
        for t in range(rest_tiles):
            total = None
            for k in range(min(8, nx)):
                v = pieces[8 * t + k]
                v = pltpu.roll(v, REST * k, 1) if k else v
                total = v if total is None else total + v
            out.append(total)
        return out

    def spread(ref, send_sem, recv_sem):
        src = ref.at[pl.ds(first_block, row_blocks)]
        for step in z_steps:
            remote(src, src, send_sem, recv_sem, i, 4 * ((zj + step) % zs) + xj).start()

    quarter = x_in.at[pl.ds(share * xj, share)]
    take(quarter, x_recv)
    for step in range(1, 4):
        remote(quarter, quarter, x_row_send, x_row_recv, i, 4 * zj + (xj + step) % 4).start()
    take(x_in.at[pl.ds(0, 3 * share)], x_row_recv)
    for b in range(row_blocks):
        rests = []
        for p in range(nx):
            v = x_in[p, b].astype(F32)
            x_own[b, :, MAIN * p:MAIN * (p + 1)] = v[:, 0:MAIN]
            rests.append(v[:, MAIN:2 * MAIN])
        for t, v in enumerate(rest_sum(rests)):
            x_own[b, :, MAIN * (nx + t):MAIN * (nx + t + 1)] = v
        row_all[first_block + b] = x_own[b].astype(BF16)
    spread(row_all, row_send, row_recv)

    for load in loads[5:9]:
        load.wait()
    own_b = wb_all.at[c, y]
    own_b[OUT_AT:OUT_REST_AT, :] = wo_vm[:, 0:MAIN]
    v = jnp.concatenate([wo_vm[:, MAIN:].astype(F32), jnp.zeros((64, MAIN - REST), F32)], axis=1)
    v = jnp.concatenate([v, jnp.zeros((64, MAIN), F32)], axis=0).T
    own_b[OUT_REST_AT:B_ROWS, :] = v[0:REST].astype(BF16)
    for step in y_steps:
        remote(own_b, own_b, wb_send, wb_recv, 2 * ((y + step) % ys) + c, j).start()
    own_f = wf_all.at[c, y]
    for n in range(2):
        at = slice(MAIN * n, MAIN * (n + 1))
        own_f[GATE_AT + 144 * n:GATE_AT + 144 * (n + 1), :] = wg_vm[:, at]
        own_f[GATE_AT + 144 * (n + 2):GATE_AT + 144 * (n + 3), :] = wu_vm[:, at]
        own_f[DOWN_AT + 144 * n:DOWN_AT + 144 * (n + 1), :] = wd_vm[:, at]
    v = [w[:, 256:288].astype(F32) for w in (wg_vm, wu_vm, wd_vm)] + [jnp.zeros((144, 32), F32)]
    own_f[NARROW_AT:DOWN_AT, :] = jnp.concatenate(v, axis=1).astype(BF16)
    ring_start(1)
    to_sibling(y)

    take(wa_all.at[c, pl.ds(0, ys - 1)], wa_recv)
    remote(wa_all.at[c], wa_all.at[c], wa_core_send, wa_core_recv, sibling, j).start()
    take(wa_all.at[1 - c], wa_core_recv)
    rests = []
    for p in range(nx):
        v = wa_all[p // ys, p % ys, QKV_ROWS:A_ROWS, :].astype(F32)
        v = v[0:8] + v[8:16]
        gain_main[p] = v
        rests.append(v)
    for t, v in enumerate(rest_sum(rests)):
        gain_rest[t] = v

    def gain(which, t):
        if t < nx:
            return gain_main[t, which:which + 1, :]
        return gain_rest[t - nx, 4 + which:5 + which, :]

    take(row_all.at[pl.ds(0, blocks - row_blocks)], row_recv)

    def chunk_tile(ref, t):
        at = slice(MAIN * t, MAIN * (t + 1))
        return jnp.concatenate([ref[k, :, at].astype(F32) for k in range(blocks)], axis=0)

    total = None
    for t in range(tiles):
        v = chunk_tile(row_all, t)
        total = v * v if total is None else total + v * v
    scale = lax.rsqrt(jnp.sum(total, axis=1, keepdims=True) / width + EPSILON)
    for t in range(tiles):
        v = chunk_tile(row_all, t)
        norm_in[:, MAIN * t:MAIN * (t + 1)] = (v * scale * gain(0, t)).astype(BF16)
    main_w = wa_all[:, :, 0:MAIN, :].reshape(nx * MAIN, 128)
    rest_w = wa_all[:, :, MAIN:QKV_ROWS, :].reshape(nx * REST, 128)
    qkv = dot(norm_in[:, 0:nx * MAIN], main_w) + dot(norm_in[:, nx * MAIN:nx * MAIN + nx * REST], rest_w)
    lane_half = lax.broadcasted_iota(jnp.int32, (ROWS // 2, 128), 1) < 64
    for part in range(2):
        first, second = qkv[ROWS * part:ROWS * part + 16], qkv[ROWS * part + 16:ROWS * (part + 1)]
        q_out[part] = jnp.where(lane_half, first, pltpu.roll(second, 64, 1)).astype(BF16)
        kv_out[part] = jnp.where(lane_half, pltpu.roll(first, 64, 1), second).astype(BF16)
    for part in range(2):
        put(kv_out.at[part], kv_in.at[j % 8], kv_send, kv_recv, tail_stride * (j // 8), group_of(part))
    for part in range(2):
        group = group_of(part)

        @pl.loop(0, nx)
        def _(step):
            put(q_out.at[part], q_in.at[j], q_send, q_recv, (i + 2 * j + step) % nx, group)

    take(wb_all.at[c, pl.ds(0, ys - 1)], wb_recv)
    remote(wb_all.at[c], wb_all.at[c], wb_core_send, wb_core_recv, sibling, j).start()
    row = lax.broadcasted_iota(jnp.int32, (ROWS, 1), 0)
    row_step, row_beam = row & 3, jnp.right_shift(row, 2)
    for load in loads[9:12]:
        load.wait()
    length = jnp.full((1, 1), length_ref[0], jnp.int32)
    first_page = jnp.right_shift(jnp.maximum(length - (WINDOW - 1), 0), 7).astype(F32)
    length_wide = length.astype(F32)
    page_iota = lax.broadcasted_iota(jnp.int32, table_vm.shape, 1).astype(F32)
    lane = lax.broadcasted_iota(jnp.int32, (ROWS, PAGE), 1)
    lane_wide = lane.astype(F32)
    lowest = row_step.astype(F32) - (WINDOW - 1)
    masks = []
    for slot in range(4):
        match = table_vm[...] == i * 4 + slot
        page = jnp.sum(jnp.where(match, page_iota, 0.0), axis=1, keepdims=True)
        used = jnp.sum(jnp.where(match, 1.0, 0.0), axis=1, keepdims=True)
        start = jnp.where(used > 0.5, (first_page + page) * PAGE - length_wide, 1.0)
        place = start + lane_wide
        mask = jnp.where((place < 0.0) & (place >= lowest), 1.0, 0.0)
        masks.append(jnp.concatenate([mask, mask], axis=0) > 0.5)
    key_lane = lax.broadcasted_iota(jnp.int32, (ROWS, ROWS), 1)
    key_step, key_beam = key_lane & 3, jnp.right_shift(key_lane, 2)
    beam_lane = lax.broadcasted_iota(jnp.int32, (ROWS, BEAM), 1)
    current = row_beam
    tail = jnp.zeros((ROWS, ROWS), F32)
    for at in range(STEPS - 1, -1, -1):
        hit = (key_step == at) & (row_step >= at) & (key_beam == current)
        tail = jnp.where(hit, 1.0, tail)
        if at:
            chosen = jnp.where(beam_lane == current, parents_vm[at - 1:at, :].astype(F32), 0.0)
            parent = jnp.sum(chosen, axis=1, keepdims=True).astype(jnp.int32)
            current = jnp.where(row_step >= at, parent, current)
    tail_mask = jnp.concatenate([tail, tail], axis=0) > 0.5

    cosine = jnp.concatenate([cosine_ref[...]] * BEAM, axis=0)
    sine = jnp.concatenate([sine_ref[...]] * BEAM, axis=0)
    take(q_in, q_recv)

    def query_tile(at):
        first, second = q_in[at].astype(F32), q_in[at + 1].astype(F32)
        upper = jnp.where(lane_half, first, pltpu.roll(second, 64, 1))
        lower = jnp.where(lane_half, pltpu.roll(first, 64, 1), second)
        return jnp.concatenate([upper, lower], axis=0)

    def kv_tile(source, at):
        total = None
        for m in range(4):
            v = kv_in[source + m].astype(F32)
            v = jnp.concatenate([v, pltpu.roll(v, 64, 1)], axis=0)
            shift = (32 * m - at) % 128
            v = pltpu.roll(v, shift, 1) if shift else v
            total = v if total is None else jnp.where(lane >= 32 * m, v, total)
        return total

    def rotated(u, w):
        return u * cosine - w * sine, w * cosine + u * sine

    def wide(u, w):
        return jnp.concatenate([u, w], axis=1)

    def query_of(h):
        qs = []
        for g in range(2):
            base = 4 * (2 * h + g)
            qs.append(wide(*rotated(query_tile(base), query_tile(base + 2))) * HEAD_DIM ** -0.5)
        return jnp.concatenate(qs, axis=0).astype(BF16)

    tail_num[...] = jnp.zeros(tail_num.shape, F32)
    tail_den[...] = jnp.zeros(tail_den.shape, F32)

    @pl.when(i % tail_stride == 0)
    def _():
        h = i // tail_stride
        take(kv_in, kv_recv)
        key = wide(*rotated(kv_tile(0, 0), kv_tile(4, 0))).astype(BF16)
        value = wide(kv_tile(0, 32), kv_tile(4, 32)).astype(BF16)
        weights = jnp.where(tail_mask, capped(dot_nt(query_of(h), key)), 0.0)
        tail_den[h] = jnp.broadcast_to(jnp.sum(weights, axis=1, keepdims=True), (2 * ROWS, 128))
        tail_num[h] = dot(weights.astype(BF16), value)

    for h in range(kv_heads):
        query = query_of(h)
        den = tail_den[h, :, 0:1]
        num = tail_num[h]
        for slot in range(4):
            at = slice(HEAD_DIM * h, HEAD_DIM * (h + 1))
            weights = jnp.where(masks[slot], capped(dot_nt(query, cache[0, slot, :, at])), 0.0)
            den = den + jnp.sum(weights, axis=1, keepdims=True)
            num = num + dot(weights.astype(BF16), cache[1, slot, :, at])
        den_high = den.astype(BF16).astype(F32)
        den_low = den - den_high
        for g in range(2):
            rows = slice(ROWS * g, ROWS * (g + 1))
            both = jnp.where(lane == row, den_high[rows], 0.0) + jnp.where(lane == row + ROWS, den_low[rows], 0.0)
            both = jnp.broadcast_to(jnp.sum(both, axis=0, keepdims=True), (8, 128))
            for t in range(2):
                v = jnp.concatenate([num[rows, 128 * t:128 * (t + 1)], both], axis=0)
                num_out[2 * (2 * h + g) + t] = v.astype(BF16)

    for step in y_steps + [0]:
        for core in range(2):
            to = 2 * ((y + step) % ys) + (c + core) % 2
            if step or core:
                remote(num_out.at[to], num_in.at[i], num_send, num_recv, to, j).start()

    pltpu.make_async_copy(num_out.at[i], num_in.at[i], num_recv).start()
    take(num_in, num_recv)
    total = None
    for p in range(nx):
        v = num_in[p].astype(F32)
        total = v if total is None else total + v
    both = jnp.where((lane == row) | (lane == row + ROWS), total[ROWS:ROWS + 1], 0.0)
    total = total[0:ROWS] / jnp.sum(both, axis=1, keepdims=True)
    att_out[0] = total.astype(BF16)
    for k in range(2):
        put(att_out.at[0], att_in.at[half], att_send, att_recv, chunk, 2 * i + k)
    if last_step > 1:
        ring_take(1)

    take(att_in, att_recv)
    attended = []
    for part in range(2):
        v = att_in[part].astype(F32)
        attended.append(jnp.where(j % 2 == 1, pltpu.roll(v, 64, 1), v)[:, 0:64])
    attended = jnp.concatenate(attended, axis=0).astype(BF16)
    take(wb_all.at[1 - c], wb_core_recv)

    def put_partial(which, t, v):
        for k in range(blocks):
            part_out[which, k, :, MAIN * t:MAIN * (t + 1)] = v[8 * k:8 * (k + 1)].astype(BF16)

    def put_rest(which, v):
        if v.shape[1] < 128:
            v = jnp.concatenate([v, jnp.zeros((v.shape[0], 128 - v.shape[1]), F32)], axis=1)
        for t in range(rest_tiles):
            put_partial(which, nx + t, v[:, 128 * t:128 * (t + 1)])

    for p in range(nx):
        put_partial(0, p, dot(attended, wb_all[p // ys, p % ys, OUT_AT:OUT_REST_AT, :]))
    rest_w = wb_all[:, :, OUT_REST_AT:B_ROWS, :].reshape(nx * REST, 128)
    put_rest(0, dot_nt(attended, rest_w[:, 0:64]))

    def send_partial(which, dst_all, send_sem, recv_sem):
        for step in z_steps:
            to = (zj + step) % zs
            src = part_out.at[which, pl.ds(row_blocks * ((to + zs - shift) % zs), row_blocks)]
            remote(src, dst_all.at[step - 1], send_sem, recv_sem, i, 4 * to + xj).start()

    def add_z(which, ref, dst_all, send_sem, recv_sem):
        for b in range(row_blocks):
            for t in range(tiles):
                at = slice(MAIN * t, MAIN * (t + 1))
                total = part_out[which, first_block + b, :, at].astype(F32)
                for s in range(zs - 1):
                    total = total + ref[s, b, :, at].astype(F32)
                sums[b, :, at] = total
            sum_out[which, b] = sums[b].astype(BF16)
        for step in range(1, 4):
            remote(
                sum_out.at[which], dst_all.at[step - 1], send_sem, recv_sem, i, 4 * zj + (xj + step) % 4
            ).start()

    def add_x(ref, b):
        square = None
        for t in range(tiles):
            at = slice(MAIN * t, MAIN * (t + 1))
            v = sums[b, :, at]
            for s in range(3):
                v = v + ref[s, b, :, at].astype(F32)
            sums[b, :, at] = v
            square = v * v if square is None else square + v * v
        return lax.rsqrt(jnp.sum(square, axis=1, keepdims=True) / width + EPSILON)

    send_partial(0, part_z, part_send, part_recv)
    if last_step > 2:
        ring_take(2)
    take(part_z, part_recv)
    add_z(0, part_z, part_x, part_x_send, part_x_recv)
    for step in range(3, last_step):
        ring_take(step)
    take(part_x, part_x_recv)
    for b in range(row_blocks):
        scale = add_x(part_x, b)
        square = None
        for t in range(tiles):
            at = slice(MAIN * t, MAIN * (t + 1))
            v = x_own[b, :, at] + sums[b, :, at] * scale * gain(1, t)
            mixed[b, :, at] = v
            square = v * v if square is None else square + v * v
        scale = lax.rsqrt(jnp.sum(square, axis=1, keepdims=True) / width + EPSILON)
        for t in range(tiles):
            at = slice(MAIN * t, MAIN * (t + 1))
            sums[b, :, at] = mixed[b, :, at] * scale * gain(2, t)
        ff_all[first_block + b] = sums[b].astype(BF16)
    spread(ff_all, ff_send, ff_recv)
    ring_take(last_step)
    take(wf_all.at[1 - c], wf_core_recv)

    take(ff_all.at[pl.ds(0, blocks - row_blocks)], ff_recv)
    for t in range(tiles):
        norm_in[:, MAIN * t:MAIN * (t + 1)] = chunk_tile(ff_all, t).astype(BF16)
    main_x = norm_in[:, 0:nx * MAIN]
    rest_x = norm_in[:, nx * MAIN:nx * MAIN + nx * REST]

    def ff_part(n):
        at = GATE_AT + 144 * n
        main_w = wf_all[:, :, at:at + MAIN, :].reshape(nx * MAIN, 128)
        rest_w = wf_all[:, :, at + MAIN:at + 144, :].reshape(nx * REST, 128)
        return dot(main_x, main_w) + dot(rest_x, rest_w)

    hidden = [(gelu(ff_part(n)) * ff_part(n + 2)).astype(BF16) for n in range(2)]
    both = ff_part(4)
    narrow = gelu(both) * pltpu.roll(both, 96, 1)
    lane_chunk = lax.broadcasted_iota(jnp.int32, narrow.shape, 1)
    narrow = pltpu.roll(jnp.where(lane_chunk < 32, narrow, 0.0), 64, 1)
    hidden.append(narrow.astype(BF16))
    places = [DOWN_AT, DOWN_AT + 144, NARROW_AT]
    for p in range(nx):
        v = None
        for h, at in zip(hidden, places):
            term = dot_nt(h, wf_all[p // ys, p % ys, at:at + MAIN, :])
            v = term if v is None else v + term
        put_partial(1, p, v)
    v = None
    for h, at in zip(hidden, places):
        rest_w = wf_all[:, :, at + MAIN:at + 144, :].reshape(nx * REST, 128)
        term = dot_nt(h, rest_w)
        v = term if v is None else v + term
    put_rest(1, v)
    send_partial(1, down_z, down_send, down_recv)
    take(down_z, down_recv)
    add_z(1, down_z, down_x, down_x_send, down_x_recv)
    take(down_x, down_x_recv)

    for b in range(row_blocks):
        scale = add_x(down_x, b)

        def result(t):
            at = slice(MAIN * t, MAIN * (t + 1))
            return mixed[b, :, at] + sums[b, :, at] * scale * gain(3, t)

        for p in range(nx):
            v = result(nx + p // 8)
            shift = (128 - REST * (p % 8)) % 128
            v = pltpu.roll(v, shift, 1) if shift else v
            last_out[b, p] = jnp.concatenate([result(p), v], axis=1).astype(BF16)
        for m in range(share):
            p = share * xj + m
            to = 2 * (p % ys) + p // ys
            put(
                last_out.at[b, p], last_in.at[(first_block + b) % 4], last_send, last_recv,
                to, group_of(my_part),
            )

    take(last_in, last_recv)
    for q in range(4):
        v = last_in[q].astype(F32)
        out_ref[2 * q] = v[0:STEPS, 0:144].astype(BF16)
        out_ref[2 * q + 1] = v[STEPS:8, 0:144].astype(BF16)

    x_sent = last_out.at[0]
    take_sent(x_sent, 4, x_send, own_rows, row_blocks)
    take(x_in.at[pl.ds(0, 3 * share)], x_row_send)
    take(wa_all.at[c, pl.ds(0, ys - 1)], wa_send)
    take(wa_all.at[c], wa_core_send)
    take(wb_all.at[c, pl.ds(0, ys - 1)], wb_send)
    take(wb_all.at[c], wb_core_send)
    for step in range(1, last_step + 1):
        for side in range(2):
            rows = pl.ds(0, F_ROWS) if step < last_step else pl.ds(CUT * side, F_ROWS - CUT if side else CUT)
            take(wf_all.at[0, 0, rows], ring_send.at[2 * step - 2 + side])
    take(wf_all.at[c], wf_core_send)
    take_sent(q_in, ny, q_send, home)
    take_sent(kv_out, 2, kv_send, home & (i == tail_stride * (j // 8)))
    take(num_out.at[pl.ds(0, nx - 1)], num_send)
    take_sent(att_in, 2, att_send, home & (j // 2 == i))
    take(row_all.at[pl.ds(0, (zs - 1) * row_blocks)], row_send)
    take(ff_all.at[pl.ds(0, (zs - 1) * row_blocks)], ff_send)
    take(part_z, part_send)
    take(down_z, down_send)
    take(part_x, part_x_send)
    take(down_x, down_x_send)
    take_sent(x_sent, row_blocks * share, last_send, own_rows, row_blocks)


def body(
    inputs, cache_pool, lengths, block_table, parents, norm_gains,
    w_query, w_key, w_value, w_out, w_gate, w_up, w_down, *, nx, ny,
):
    columns = inputs.shape[2]
    tiles = nx + max(nx // 8, 1)
    rest_tiles = tiles - nx
    span = tiles * MAIN
    ys = nx // 2
    last_step = ys // 2
    zs = ny // 4
    row_blocks = 8 // zs

    frequency = ROPE_BASE ** (-jnp.arange(128, dtype=F32) * 2.0 / HEAD_DIM)
    positions = lengths[0] + jnp.arange(STEPS, dtype=jnp.int32)
    angles = positions[:, None].astype(F32) * frequency

    arrays = (
        inputs, cache_pool, lengths, block_table, parents, norm_gains,
        w_query.T, w_key.T, w_value.T, w_out, w_gate, w_up, w_down.T, jnp.cos(angles), jnp.sin(angles),
    )
    vmem = pl.BlockSpec(memory_space=pltpu.VMEM)
    specs = [pl.BlockSpec(memory_space=pltpu.HBM) for _ in arrays]
    specs[2] = pl.BlockSpec(memory_space=pltpu.SMEM)
    specs[13:15] = [vmem, vmem]
    dma = pltpu.SemaphoreType.DMA

    def held(*shape, dtype=BF16):
        return pltpu.VMEM(shape, dtype)

    out = pl.pallas_call(
        functools.partial(layer_kernel, nx, ny, nx * columns),
        name="layer",
        out_shape=jax.ShapeDtypeStruct(inputs.shape, BF16),
        in_specs=specs,
        out_specs=vmem,
        scratch_shapes=[pltpu.VMEM(arrays[k].shape, arrays[k].dtype) for k in (0, 1, 3, 4, 5, 6, 7, 8, 9, 10, 11, 12)]
        + [
            held(2, ys, A_ROWS, 128),
            held(2, ys, B_ROWS, 128),
            held(2, ys, F_ROWS, 128),
            held(nx, 8, 128, dtype=F32),
            held(rest_tiles, 8, 128, dtype=F32),
            held(4, 8, 256),
            held(nx, row_blocks, 8, 256),
            held(row_blocks, 8, span, dtype=F32),
            held(8, 8, span),
            held(8, 8, span),
            held(64, span),
            held(2, ROWS // 2, 128),
            held(2, ROWS // 2, 128),
            held(ny, ROWS // 2, 128),
            held(8, ROWS // 2, 128),
            held(ny // 8, 2 * ROWS, HEAD_DIM, dtype=F32),
            held(ny // 8, 2 * ROWS, 128, dtype=F32),
            held(nx, DEN_ROWS, 128),
            held(nx, DEN_ROWS, 128),
            held(1, ROWS, 128),
            held(2, ROWS, 128),
            held(2, 8, 8, span),
            held(zs - 1, row_blocks, 8, span),
            held(zs - 1, row_blocks, 8, span),
            held(2, row_blocks, 8, span),
            held(3, row_blocks, 8, span),
            held(3, row_blocks, 8, span),
            held(row_blocks, 16, 8, 256),
            held(4, 8, 256),
            held(row_blocks, 8, span, dtype=F32),
            held(row_blocks, 8, span, dtype=F32),
        ]
        + [dma((12,))] + [dma(())] * 4
        + [dma((2 * last_step,)), dma((2 * last_step,))]
        + [dma(())] * 32,
        compiler_params=pltpu.CompilerParams(collective_id=0, has_side_effects=True, vmem_limit_bytes=60 << 20),
    )(*arrays)
    return out


def solution(mesh):
    return jax.shard_map(
        functools.partial(body, nx=mesh.shape["gx"], ny=mesh.shape["gy"]),
        mesh=mesh,
        in_specs=(
            P("gy", None, "gx"),
            P(None, "gx", "gy", None),
            P("gy"),
            P("gy", None),
            P(None, "gy"),
            P(None, "gx"),
            P("gx", "gy"),
            P("gx", "gy"),
            P("gx", "gy"),
            P("gy", "gx"),
            P("gx", "gy"),
            P("gx", "gy"),
            P("gy", "gx"),
        ),
        out_specs=P("gy", None, "gx"),
        check_vma=False,
    )
```

```python
import functools
import math

import jax
import jax.numpy as jnp
from jax import lax
from jax.experimental import pallas as pl
from jax.experimental.pallas import tpu as pltpu
from jax.sharding import PartitionSpec as P

MESH = pl.DeviceIdType.MESH
F32 = jnp.float32
BF16 = jnp.bfloat16

HEAD_DIM = 256
WINDOW = 4096
PAGE = 128
BEAM = 8
STEPS = 4
ROWS = BEAM * STEPS
EPSILON = 1e-06
SOFT_CAP = 50.0
ROPE_BASE = 10000.0
MAIN = 128
REST = 16

QKV_ROWS = 144
A_ROWS = 160
OUT_AT = 0
OUT_REST_AT = 64
B_ROWS = 80
GATE_AT = 0
NARROW_AT = 576
DOWN_AT = 720
F_ROWS = 1008
CUT = 512
DEN_ROWS = 40


def capped(scores):
    return jnp.exp(SOFT_CAP * jnp.tanh(scores * (1.0 / SOFT_CAP)))


def gelu(v):
    return 0.5 * v * (1.0 + jnp.tanh(math.sqrt(2.0 / math.pi) * (v + 0.044715 * (v * v * v))))


def dot(a, b):
    return jnp.dot(a, b, preferred_element_type=F32)


def dot_nt(a, b):
    return lax.dot_general(a, b, (((1,), (1,)), ((), ())), preferred_element_type=F32)


def layer_kernel(
    nx, ny, width,
    inputs_ref, cache_ref, length_ref, table_ref, parents_ref, gains_ref,
    wq_ref, wk_ref, wv_ref, wo_ref, wg_ref, wu_ref, wd_ref, cosine_ref, sine_ref,
    out_ref,
    inputs_vm, cache, table_vm, parents_vm, gains_vm,
    wq_vm, wk_vm, wv_vm, wo_vm, wg_vm, wu_vm, wd_vm,
    wa_all, wb_all, wf_all, gain_main, gain_rest, x_out, x_in, x_own, row_all, ff_all, norm_in,
    q_out, kv_out, q_in, kv_in, tail_num, tail_den, num_out, num_in, att_out, att_in, part_out,
    part_z, down_z, sum_out, part_x, down_x, last_out, last_in, mixed, sums,
    load_sem, wa_send, wa_recv, wa_core_send, wa_core_recv, ring_send, ring_recv, wf_core_send, wf_core_recv,
    wb_send, wb_recv, wb_core_send, wb_core_recv,
    x_send, x_recv, x_row_send, x_row_recv, row_send, row_recv, q_send, q_recv, kv_send, kv_recv, num_send, num_recv,
    att_send, att_recv, part_send, part_recv, part_x_send, part_x_recv, ff_send, ff_recv,
    down_send, down_recv, down_x_send, down_x_recv, last_send, last_recv,
):
    ys = nx // 2
    zs = ny // 4
    kv_heads = ny // 8
    tiles = nx + nx // 8 if nx >= 8 else nx + 1
    rest_tiles = tiles - nx
    blocks = 8
    row_blocks = blocks // zs
    z_steps = sorted(range(1, zs), key=lambda d: -min(d, zs - d))
    y_steps = sorted(range(1, ys), key=lambda d: -min(d, ys - d))
    i = lax.axis_index("gx")
    j = lax.axis_index("gy")
    y, c = i // 2, i % 2
    sibling = i + 1 - 2 * c
    piece = c * ys + y
    zj, xj = j // 4, j % 4
    chunk = 2 * ((zj + 2 * xj) % ys) + xj % 2
    half = xj // 2

    def group_of(part):
        x_r = 2 * part + c
        return ((y + 8 * ys - 2 * x_r) % ys) * 4 + x_r

    shift = (y + 8 * ys - 2 * c - 1) % ys if zs == 8 else 0
    first_block = row_blocks * ((zj + zs - shift) % zs)
    share = nx // 4
    my_part = first_block // 4
    home = chunk == i
    own_rows = home & (my_part == half) & (piece // share == xj)
    tail_stride = nx // kv_heads

    def row_of(block):
        there = (chunk // 2 + 8 * ys - 2 * (chunk % 2) - 1) % ys if zs == 8 else 0
        return (block + there) % zs

    def remote(src, dst, send_sem, recv_sem, tx, ty):
        return pltpu.make_async_remote_copy(
            src_ref=src, dst_ref=dst, send_sem=send_sem, recv_sem=recv_sem,
            device_id=(tx, ty), device_id_type=MESH,
        )

    def put(src, dst, send_sem, recv_sem, tx, ty):
        own = (tx == i) & (ty == j)

        @pl.when(jnp.logical_not(own))
        def _():
            remote(src, dst, send_sem, recv_sem, tx, ty).start()

        @pl.when(own)
        def _():
            pltpu.make_async_copy(src, dst, recv_sem).start()

    def take(ref, sem):
        pltpu.make_async_copy(ref, ref, sem).wait()

    def take_sent(ref, count, sem, own, fewer=1):
        @pl.when(own)
        def _():
            take(ref.at[pl.ds(0, count - fewer)], sem)

        @pl.when(jnp.logical_not(own))
        def _():
            take(ref.at[pl.ds(0, count)], sem)

    loads = [
        pltpu.make_async_copy(src, dst, load_sem.at[k])
        for k, (src, dst) in enumerate([
            (inputs_ref, inputs_vm), (wq_ref, wq_vm), (wk_ref, wk_vm), (wv_ref, wv_vm), (gains_ref, gains_vm),
            (wo_ref, wo_vm), (wg_ref, wg_vm), (wu_ref, wu_vm), (wd_ref, wd_vm),
            (table_ref, table_vm), (parents_ref, parents_vm), (cache_ref, cache),
        ])
    ]
    for load in loads:
        load.start()

    barrier = pltpu.get_barrier_semaphore()

    def hello(tx, ty):
        pl.semaphore_signal(barrier, inc=1, device_id=(tx, ty), device_id_type=MESH)

    for step in range(1, ys):
        hello(2 * ((y + step) % ys) + c, j)
    hello(sibling, j)
    for step in range(1, zs):
        hello(i, 4 * ((zj + step) % zs) + xj)
    group = group_of(my_part)

    for m in range(share):
        p = share * xj + m
        to = 2 * (p % ys) + p // ys

        @pl.when(jnp.logical_not((to == i) & (group == j)))
        def _():
            hello(to, group)

    for step in range(1, 4):
        hello(i, 4 * zj + (xj + step) % 4)
    waits = ys + (zs - 1) + 3 + 4 // row_blocks - jnp.where(own_rows, 1, 0)

    loads[0].wait()
    for q in range(4):
        v = jnp.concatenate([inputs_vm[2 * q].astype(F32), inputs_vm[2 * q + 1].astype(F32)], axis=0)
        v = jnp.concatenate([v, jnp.zeros((8, MAIN - REST), F32)], axis=1)
        x_out[q] = v.astype(BF16)
    pl.semaphore_wait(barrier, waits)
    for q in range(4):
        block = half * 4 + q
        put(
            x_out.at[q], x_in.at[piece, block % row_blocks], x_send, x_recv,
            chunk, 4 * row_of(block // row_blocks) + piece // share,
        )
    for load in loads[1:5]:
        load.wait()
    v = jnp.concatenate([wq_vm[...].astype(F32), wk_vm[...].astype(F32), wv_vm[...].astype(F32)], axis=0)
    wa_all[c, y, 0:MAIN, :] = v[:, 0:MAIN].T.astype(BF16)
    v = jnp.concatenate([v[:, MAIN:], jnp.zeros((128, MAIN - REST), F32)], axis=1).T
    wa_all[c, y, MAIN:QKV_ROWS, :] = v[0:REST].astype(BF16)
    v = 1.0 + gains_vm[...]
    v = jnp.concatenate([v, jnp.zeros((4, MAIN - REST), F32)], axis=1)
    v = jnp.concatenate([v[:, 0:MAIN], v[:, MAIN:]], axis=0)
    high = v.astype(BF16).astype(F32)
    wa_all[c, y, QKV_ROWS:A_ROWS, :] = jnp.concatenate([high, v - high], axis=0).astype(BF16)
    for step in y_steps:
        remote(wa_all.at[c, y], wa_all.at[c, y], wa_send, wa_recv, 2 * ((y + step) % ys) + c, j).start()

    right = 2 * ((y + 1) % ys) + c
    left = 2 * ((y + ys - 1) % ys) + c
    last_step = ys // 2

    def ring_refs(step):
        from_left = (y + ys - (step - 1)) % ys
        from_right = (y + (step - 1)) % ys
        return from_left, from_right

    def ring_start(step):
        a, b = ring_refs(step)
        src_a, src_b = wf_all.at[c, a], wf_all.at[c, b]
        if step == last_step:
            src_a, src_b = src_a.at[pl.ds(0, CUT)], src_b.at[pl.ds(CUT, F_ROWS - CUT)]
        remote(src_a, src_a, ring_send.at[2 * step - 2], ring_recv.at[2 * step - 2], right, j).start()
        remote(src_b, src_b, ring_send.at[2 * step - 1], ring_recv.at[2 * step - 1], left, j).start()

    def to_sibling(k):
        remote(wf_all.at[c, k], wf_all.at[c, k], wf_core_send, wf_core_recv, sibling, j).start()

    def ring_take(step):
        a = (y + ys - step) % ys
        b = (y + step) % ys
        ref_a, ref_b = wf_all.at[c, a], wf_all.at[c, b]
        if step == last_step:
            take(ref_a.at[pl.ds(0, CUT)], ring_recv.at[2 * step - 2])
            take(ref_b.at[pl.ds(CUT, F_ROWS - CUT)], ring_recv.at[2 * step - 1])
            to_sibling(a)
        else:
            take(ref_a, ring_recv.at[2 * step - 2])
            take(ref_b, ring_recv.at[2 * step - 1])
            ring_start(step + 1)
            to_sibling(a)
            to_sibling(b)

    def rest_sum(pieces):
        out = []
        for t in range(rest_tiles):
            total = None
            for k in range(min(8, nx)):
                v = pieces[8 * t + k]
                v = pltpu.roll(v, REST * k, 1) if k else v
                total = v if total is None else total + v
            out.append(total)
        return out

    for load in loads[5:9]:
        load.wait()
    own_b = wb_all.at[c, y]
    own_b[OUT_AT:OUT_REST_AT, :] = wo_vm[:, 0:MAIN]
    v = jnp.concatenate([wo_vm[:, MAIN:].astype(F32), jnp.zeros((64, MAIN - REST), F32)], axis=1)
    v = jnp.concatenate([v, jnp.zeros((64, MAIN), F32)], axis=0).T
    own_b[OUT_REST_AT:B_ROWS, :] = v[0:REST].astype(BF16)
    for step in y_steps:
        remote(own_b, own_b, wb_send, wb_recv, 2 * ((y + step) % ys) + c, j).start()
    own_f = wf_all.at[c, y]
    for n in range(2):
        at = slice(MAIN * n, MAIN * (n + 1))
        own_f[GATE_AT + 144 * n:GATE_AT + 144 * (n + 1), :] = wg_vm[:, at]
        own_f[GATE_AT + 144 * (n + 2):GATE_AT + 144 * (n + 3), :] = wu_vm[:, at]
        own_f[DOWN_AT + 144 * n:DOWN_AT + 144 * (n + 1), :] = wd_vm[:, at]
    v = [w[:, 256:288].astype(F32) for w in (wg_vm, wu_vm, wd_vm)] + [jnp.zeros((144, 32), F32)]
    own_f[NARROW_AT:DOWN_AT, :] = jnp.concatenate(v, axis=1).astype(BF16)
    ring_start(1)
    to_sibling(y)

    def spread(ref, send_sem, recv_sem):
        src = ref.at[pl.ds(first_block, row_blocks)]
        for step in z_steps:
            remote(src, src, send_sem, recv_sem, i, 4 * ((zj + step) % zs) + xj).start()

    quarter = x_in.at[pl.ds(share * xj, share)]
    take(quarter, x_recv)
    for step in range(1, 4):
        remote(quarter, quarter, x_row_send, x_row_recv, i, 4 * zj + (xj + step) % 4).start()
    take(x_in.at[pl.ds(0, 3 * share)], x_row_recv)
    for b in range(row_blocks):
        rests = []
        for p in range(nx):
            v = x_in[p, b].astype(F32)
            x_own[b, :, MAIN * p:MAIN * (p + 1)] = v[:, 0:MAIN]
            rests.append(v[:, MAIN:2 * MAIN])
        for t, v in enumerate(rest_sum(rests)):
            x_own[b, :, MAIN * (nx + t):MAIN * (nx + t + 1)] = v
        row_all[first_block + b] = x_own[b].astype(BF16)
    spread(row_all, row_send, row_recv)

    take(wa_all.at[c, pl.ds(0, ys - 1)], wa_recv)
    remote(wa_all.at[c], wa_all.at[c], wa_core_send, wa_core_recv, sibling, j).start()
    take(wa_all.at[1 - c], wa_core_recv)
    rests = []
    for p in range(nx):
        v = wa_all[p // ys, p % ys, QKV_ROWS:A_ROWS, :].astype(F32)
        v = v[0:8] + v[8:16]
        gain_main[p] = v
        rests.append(v)
    for t, v in enumerate(rest_sum(rests)):
        gain_rest[t] = v

    def gain(which, t):
        if t < nx:
            return gain_main[t, which:which + 1, :]
        return gain_rest[t - nx, 4 + which:5 + which, :]

    take(row_all.at[pl.ds(0, blocks - row_blocks)], row_recv)

    def chunk_tile(ref, t):
        at = slice(MAIN * t, MAIN * (t + 1))
        return jnp.concatenate([ref[k, :, at].astype(F32) for k in range(blocks)], axis=0)

    total = None
    for t in range(tiles):
        v = chunk_tile(row_all, t)
        total = v * v if total is None else total + v * v
    scale = lax.rsqrt(jnp.sum(total, axis=1, keepdims=True) / width + EPSILON)
    for t in range(tiles):
        v = chunk_tile(row_all, t)
        norm_in[:, MAIN * t:MAIN * (t + 1)] = (v * scale * gain(0, t)).astype(BF16)
    main_w = wa_all[:, :, 0:MAIN, :].reshape(nx * MAIN, 128)
    rest_w = wa_all[:, :, MAIN:QKV_ROWS, :].reshape(nx * REST, 128)
    qkv = dot(norm_in[:, 0:nx * MAIN], main_w) + dot(norm_in[:, nx * MAIN:nx * MAIN + nx * REST], rest_w)
    lane_half = lax.broadcasted_iota(jnp.int32, (ROWS // 2, 128), 1) < 64
    for part in range(2):
        first, second = qkv[ROWS * part:ROWS * part + 16], qkv[ROWS * part + 16:ROWS * (part + 1)]
        q_out[part] = jnp.where(lane_half, first, pltpu.roll(second, 64, 1)).astype(BF16)
        kv_out[part] = jnp.where(lane_half, pltpu.roll(first, 64, 1), second).astype(BF16)
    for part in range(2):
        put(kv_out.at[part], kv_in.at[j % 8], kv_send, kv_recv, tail_stride * (j // 8), group_of(part))
    for part in range(2):
        group = group_of(part)

        @pl.loop(0, nx)
        def _(step):
            put(q_out.at[part], q_in.at[j], q_send, q_recv, (i + 2 * j + step) % nx, group)

    take(wb_all.at[c, pl.ds(0, ys - 1)], wb_recv)
    remote(wb_all.at[c], wb_all.at[c], wb_core_send, wb_core_recv, sibling, j).start()
    row = lax.broadcasted_iota(jnp.int32, (ROWS, 1), 0)
    row_step, row_beam = row & 3, jnp.right_shift(row, 2)
    for load in loads[9:12]:
        load.wait()
    length = jnp.full((1, 1), length_ref[0], jnp.int32)
    first_page = jnp.right_shift(jnp.maximum(length - (WINDOW - 1), 0), 7).astype(F32)
    length_wide = length.astype(F32)
    page_iota = lax.broadcasted_iota(jnp.int32, table_vm.shape, 1).astype(F32)
    lane = lax.broadcasted_iota(jnp.int32, (ROWS, PAGE), 1)
    lane_wide = lane.astype(F32)
    lowest = row_step.astype(F32) - (WINDOW - 1)
    masks = []
    for slot in range(4):
        match = table_vm[...] == i * 4 + slot
        page = jnp.sum(jnp.where(match, page_iota, 0.0), axis=1, keepdims=True)
        used = jnp.sum(jnp.where(match, 1.0, 0.0), axis=1, keepdims=True)
        start = jnp.where(used > 0.5, (first_page + page) * PAGE - length_wide, 1.0)
        place = start + lane_wide
        mask = jnp.where((place < 0.0) & (place >= lowest), 1.0, 0.0)
        masks.append(jnp.concatenate([mask, mask], axis=0) > 0.5)
    key_lane = lax.broadcasted_iota(jnp.int32, (ROWS, ROWS), 1)
    key_step, key_beam = key_lane & 3, jnp.right_shift(key_lane, 2)
    beam_lane = lax.broadcasted_iota(jnp.int32, (ROWS, BEAM), 1)
    current = row_beam
    tail = jnp.zeros((ROWS, ROWS), F32)
    for at in range(STEPS - 1, -1, -1):
        hit = (key_step == at) & (row_step >= at) & (key_beam == current)
        tail = jnp.where(hit, 1.0, tail)
        if at:
            chosen = jnp.where(beam_lane == current, parents_vm[at - 1:at, :].astype(F32), 0.0)
            parent = jnp.sum(chosen, axis=1, keepdims=True).astype(jnp.int32)
            current = jnp.where(row_step >= at, parent, current)
    tail_mask = jnp.concatenate([tail, tail], axis=0) > 0.5

    cosine = jnp.concatenate([cosine_ref[...]] * BEAM, axis=0)
    sine = jnp.concatenate([sine_ref[...]] * BEAM, axis=0)
    take(q_in, q_recv)

    def query_tile(at):
        first, second = q_in[at].astype(F32), q_in[at + 1].astype(F32)
        upper = jnp.where(lane_half, first, pltpu.roll(second, 64, 1))
        lower = jnp.where(lane_half, pltpu.roll(first, 64, 1), second)
        return jnp.concatenate([upper, lower], axis=0)

    def kv_tile(source, at):
        total = None
        for m in range(4):
            v = kv_in[source + m].astype(F32)
            v = jnp.concatenate([v, pltpu.roll(v, 64, 1)], axis=0)
            shift = (32 * m - at) % 128
            v = pltpu.roll(v, shift, 1) if shift else v
            total = v if total is None else jnp.where(lane >= 32 * m, v, total)
        return total

    def rotated(u, w):
        return u * cosine - w * sine, w * cosine + u * sine

    def wide(u, w):
        return jnp.concatenate([u, w], axis=1)

    def query_of(h):
        qs = []
        for g in range(2):
            base = 4 * (2 * h + g)
            qs.append(wide(*rotated(query_tile(base), query_tile(base + 2))) * HEAD_DIM ** -0.5)
        return jnp.concatenate(qs, axis=0).astype(BF16)

    tail_num[...] = jnp.zeros(tail_num.shape, F32)
    tail_den[...] = jnp.zeros(tail_den.shape, F32)

    @pl.when(i % tail_stride == 0)
    def _():
        h = i // tail_stride
        take(kv_in, kv_recv)
        key = wide(*rotated(kv_tile(0, 0), kv_tile(4, 0))).astype(BF16)
        value = wide(kv_tile(0, 32), kv_tile(4, 32)).astype(BF16)
        weights = jnp.where(tail_mask, capped(dot_nt(query_of(h), key)), 0.0)
        tail_den[h] = jnp.broadcast_to(jnp.sum(weights, axis=1, keepdims=True), (2 * ROWS, 128))
        tail_num[h] = dot(weights.astype(BF16), value)

    for h in range(kv_heads):
        query = query_of(h)
        den = tail_den[h, :, 0:1]
        num = tail_num[h]
        for slot in range(4):
            at = slice(HEAD_DIM * h, HEAD_DIM * (h + 1))
            weights = jnp.where(masks[slot], capped(dot_nt(query, cache[0, slot, :, at])), 0.0)
            den = den + jnp.sum(weights, axis=1, keepdims=True)
            num = num + dot(weights.astype(BF16), cache[1, slot, :, at])
        den_high = den.astype(BF16).astype(F32)
        den_low = den - den_high
        for g in range(2):
            rows = slice(ROWS * g, ROWS * (g + 1))
            both = jnp.where(lane == row, den_high[rows], 0.0) + jnp.where(lane == row + ROWS, den_low[rows], 0.0)
            both = jnp.broadcast_to(jnp.sum(both, axis=0, keepdims=True), (8, 128))
            for t in range(2):
                v = jnp.concatenate([num[rows, 128 * t:128 * (t + 1)], both], axis=0)
                num_out[2 * (2 * h + g) + t] = v.astype(BF16)

    for step in y_steps + [0]:
        for core in range(2):
            to = 2 * ((y + step) % ys) + (c + core) % 2
            if step or core:
                remote(num_out.at[to], num_in.at[i], num_send, num_recv, to, j).start()

    pltpu.make_async_copy(num_out.at[i], num_in.at[i], num_recv).start()
    take(num_in, num_recv)
    total = None
    for p in range(nx):
        v = num_in[p].astype(F32)
        total = v if total is None else total + v
    both = jnp.where((lane == row) | (lane == row + ROWS), total[ROWS:ROWS + 1], 0.0)
    total = total[0:ROWS] / jnp.sum(both, axis=1, keepdims=True)
    att_out[0] = total.astype(BF16)
    for k in range(2):
        put(att_out.at[0], att_in.at[half], att_send, att_recv, chunk, 2 * i + k)
    if last_step > 1:
        ring_take(1)

    take(att_in, att_recv)
    attended = []
    for part in range(2):
        v = att_in[part].astype(F32)
        attended.append(jnp.where(j % 2 == 1, pltpu.roll(v, 64, 1), v)[:, 0:64])
    attended = jnp.concatenate(attended, axis=0).astype(BF16)
    take(wb_all.at[1 - c], wb_core_recv)

    def put_partial(which, t, v):
        for k in range(blocks):
            part_out[which, k, :, MAIN * t:MAIN * (t + 1)] = v[8 * k:8 * (k + 1)].astype(BF16)

    def put_rest(which, v):
        if v.shape[1] < 128:
            v = jnp.concatenate([v, jnp.zeros((v.shape[0], 128 - v.shape[1]), F32)], axis=1)
        for t in range(rest_tiles):
            put_partial(which, nx + t, v[:, 128 * t:128 * (t + 1)])

    for p in range(nx):
        put_partial(0, p, dot(attended, wb_all[p // ys, p % ys, OUT_AT:OUT_REST_AT, :]))
    rest_w = wb_all[:, :, OUT_REST_AT:B_ROWS, :].reshape(nx * REST, 128)
    put_rest(0, dot_nt(attended, rest_w[:, 0:64]))

    def send_partial(which, dst_all, send_sem, recv_sem):
        for step in z_steps:
            to = (zj + step) % zs
            src = part_out.at[which, pl.ds(row_blocks * ((to + zs - shift) % zs), row_blocks)]
            remote(src, dst_all.at[step - 1], send_sem, recv_sem, i, 4 * to + xj).start()

    def add_z(which, ref, dst_all, send_sem, recv_sem):
        for b in range(row_blocks):
            for t in range(tiles):
                at = slice(MAIN * t, MAIN * (t + 1))
                total = part_out[which, first_block + b, :, at].astype(F32)
                for s in range(zs - 1):
                    total = total + ref[s, b, :, at].astype(F32)
                sums[b, :, at] = total
            sum_out[which, b] = sums[b].astype(BF16)
        for step in range(1, 4):
            remote(
                sum_out.at[which], dst_all.at[step - 1], send_sem, recv_sem, i, 4 * zj + (xj + step) % 4
            ).start()

    def add_x(ref, b):
        square = None
        for t in range(tiles):
            at = slice(MAIN * t, MAIN * (t + 1))
            v = sums[b, :, at]
            for s in range(3):
                v = v + ref[s, b, :, at].astype(F32)
            sums[b, :, at] = v
            square = v * v if square is None else square + v * v
        return lax.rsqrt(jnp.sum(square, axis=1, keepdims=True) / width + EPSILON)

    send_partial(0, part_z, part_send, part_recv)
    if last_step > 2:
        ring_take(2)
    take(part_z, part_recv)
    add_z(0, part_z, part_x, part_x_send, part_x_recv)
    for step in range(3, last_step):
        ring_take(step)
    take(part_x, part_x_recv)
    for b in range(row_blocks):
        scale = add_x(part_x, b)
        square = None
        for t in range(tiles):
            at = slice(MAIN * t, MAIN * (t + 1))
            v = x_own[b, :, at] + sums[b, :, at] * scale * gain(1, t)
            mixed[b, :, at] = v
            square = v * v if square is None else square + v * v
        scale = lax.rsqrt(jnp.sum(square, axis=1, keepdims=True) / width + EPSILON)
        for t in range(tiles):
            at = slice(MAIN * t, MAIN * (t + 1))
            sums[b, :, at] = mixed[b, :, at] * scale * gain(2, t)
        ff_all[first_block + b] = sums[b].astype(BF16)
    spread(ff_all, ff_send, ff_recv)
    ring_take(last_step)
    take(wf_all.at[1 - c], wf_core_recv)

    take(ff_all.at[pl.ds(0, blocks - row_blocks)], ff_recv)
    for t in range(tiles):
        norm_in[:, MAIN * t:MAIN * (t + 1)] = chunk_tile(ff_all, t).astype(BF16)
    main_x = norm_in[:, 0:nx * MAIN]
    rest_x = norm_in[:, nx * MAIN:nx * MAIN + nx * REST]

    def ff_part(n):
        at = GATE_AT + 144 * n
        main_w = wf_all[:, :, at:at + MAIN, :].reshape(nx * MAIN, 128)
        rest_w = wf_all[:, :, at + MAIN:at + 144, :].reshape(nx * REST, 128)
        return dot(main_x, main_w) + dot(rest_x, rest_w)

    hidden = [(gelu(ff_part(n)) * ff_part(n + 2)).astype(BF16) for n in range(2)]
    both = ff_part(4)
    narrow = gelu(both) * pltpu.roll(both, 96, 1)
    lane_chunk = lax.broadcasted_iota(jnp.int32, narrow.shape, 1)
    narrow = pltpu.roll(jnp.where(lane_chunk < 32, narrow, 0.0), 64, 1)
    hidden.append(narrow.astype(BF16))
    places = [DOWN_AT, DOWN_AT + 144, NARROW_AT]
    for p in range(nx):
        v = None
        for h, at in zip(hidden, places):
            term = dot_nt(h, wf_all[p // ys, p % ys, at:at + MAIN, :])
            v = term if v is None else v + term
        put_partial(1, p, v)
    v = None
    for h, at in zip(hidden, places):
        rest_w = wf_all[:, :, at + MAIN:at + 144, :].reshape(nx * REST, 128)
        term = dot_nt(h, rest_w)
        v = term if v is None else v + term
    put_rest(1, v)
    send_partial(1, down_z, down_send, down_recv)
    take(down_z, down_recv)
    add_z(1, down_z, down_x, down_x_send, down_x_recv)
    take(down_x, down_x_recv)

    for b in range(row_blocks):
        scale = add_x(down_x, b)

        def result(t):
            at = slice(MAIN * t, MAIN * (t + 1))
            return mixed[b, :, at] + sums[b, :, at] * scale * gain(3, t)

        for p in range(nx):
            v = result(nx + p // 8)
            shift = (128 - REST * (p % 8)) % 128
            v = pltpu.roll(v, shift, 1) if shift else v
            last_out[b, p] = jnp.concatenate([result(p), v], axis=1).astype(BF16)
        for m in range(share):
            p = share * xj + m
            to = 2 * (p % ys) + p // ys
            put(
                last_out.at[b, p], last_in.at[(first_block + b) % 4], last_send, last_recv,
                to, group_of(my_part),
            )

    take(last_in, last_recv)
    for q in range(4):
        v = last_in[q].astype(F32)
        out_ref[2 * q] = v[0:STEPS, 0:144].astype(BF16)
        out_ref[2 * q + 1] = v[STEPS:8, 0:144].astype(BF16)

    x_sent = last_out.at[0]
    take_sent(x_sent, 4, x_send, own_rows, row_blocks)
    take(x_in.at[pl.ds(0, 3 * share)], x_row_send)
    take(wa_all.at[c, pl.ds(0, ys - 1)], wa_send)
    take(wa_all.at[c], wa_core_send)
    take(wb_all.at[c, pl.ds(0, ys - 1)], wb_send)
    take(wb_all.at[c], wb_core_send)
    for step in range(1, last_step + 1):
        for side in range(2):
            rows = pl.ds(0, F_ROWS) if step < last_step else pl.ds(CUT * side, F_ROWS - CUT if side else CUT)
            take(wf_all.at[0, 0, rows], ring_send.at[2 * step - 2 + side])
    take(wf_all.at[c], wf_core_send)
    take_sent(q_in, ny, q_send, home)
    take_sent(kv_out, 2, kv_send, home & (i == tail_stride * (j // 8)))
    take(num_out.at[pl.ds(0, nx - 1)], num_send)
    take_sent(att_in, 2, att_send, home & (j // 2 == i))
    take(row_all.at[pl.ds(0, (zs - 1) * row_blocks)], row_send)
    take(ff_all.at[pl.ds(0, (zs - 1) * row_blocks)], ff_send)
    take(part_z, part_send)
    take(down_z, down_send)
    take(part_x, part_x_send)
    take(down_x, down_x_send)
    take_sent(x_sent, row_blocks * share, last_send, own_rows, row_blocks)


def body(
    inputs, cache_pool, lengths, block_table, parents, norm_gains,
    w_query, w_key, w_value, w_out, w_gate, w_up, w_down, *, nx, ny,
):
    columns = inputs.shape[2]
    tiles = nx + max(nx // 8, 1)
    rest_tiles = tiles - nx
    span = tiles * MAIN
    ys = nx // 2
    last_step = ys // 2
    zs = ny // 4
    row_blocks = 8 // zs

    frequency = ROPE_BASE ** (-jnp.arange(128, dtype=F32) * 2.0 / HEAD_DIM)
    positions = lengths[0] + jnp.arange(STEPS, dtype=jnp.int32)
    angles = positions[:, None].astype(F32) * frequency

    arrays = (
        inputs, cache_pool, lengths, block_table, parents, norm_gains,
        w_query.T, w_key.T, w_value.T, w_out, w_gate, w_up, w_down.T, jnp.cos(angles), jnp.sin(angles),
    )
    vmem = pl.BlockSpec(memory_space=pltpu.VMEM)
    specs = [pl.BlockSpec(memory_space=pltpu.HBM) for _ in arrays]
    specs[2] = pl.BlockSpec(memory_space=pltpu.SMEM)
    specs[13:15] = [vmem, vmem]
    dma = pltpu.SemaphoreType.DMA

    def held(*shape, dtype=BF16):
        return pltpu.VMEM(shape, dtype)

    out = pl.pallas_call(
        functools.partial(layer_kernel, nx, ny, nx * columns),
        name="layer",
        out_shape=jax.ShapeDtypeStruct(inputs.shape, BF16),
        in_specs=specs,
        out_specs=vmem,
        scratch_shapes=[pltpu.VMEM(arrays[k].shape, arrays[k].dtype) for k in (0, 1, 3, 4, 5, 6, 7, 8, 9, 10, 11, 12)]
        + [
            held(2, ys, A_ROWS, 128),
            held(2, ys, B_ROWS, 128),
            held(2, ys, F_ROWS, 128),
            held(nx, 8, 128, dtype=F32),
            held(rest_tiles, 8, 128, dtype=F32),
            held(4, 8, 256),
            held(nx, row_blocks, 8, 256),
            held(row_blocks, 8, span, dtype=F32),
            held(8, 8, span),
            held(8, 8, span),
            held(64, span),
            held(2, ROWS // 2, 128),
            held(2, ROWS // 2, 128),
            held(ny, ROWS // 2, 128),
            held(8, ROWS // 2, 128),
            held(ny // 8, 2 * ROWS, HEAD_DIM, dtype=F32),
            held(ny // 8, 2 * ROWS, 128, dtype=F32),
            held(nx, DEN_ROWS, 128),
            held(nx, DEN_ROWS, 128),
            held(1, ROWS, 128),
            held(2, ROWS, 128),
            held(2, 8, 8, span),
            held(zs - 1, row_blocks, 8, span),
            held(zs - 1, row_blocks, 8, span),
            held(2, row_blocks, 8, span),
            held(3, row_blocks, 8, span),
            held(3, row_blocks, 8, span),
            held(row_blocks, 16, 8, 256),
            held(4, 8, 256),
            held(row_blocks, 8, span, dtype=F32),
            held(row_blocks, 8, span, dtype=F32),
        ]
        + [dma((12,))] + [dma(())] * 4
        + [dma((2 * last_step,)), dma((2 * last_step,))]
        + [dma(())] * 32,
        compiler_params=pltpu.CompilerParams(collective_id=0, has_side_effects=True, vmem_limit_bytes=60 << 20),
    )(*arrays)
    return out


def solution(mesh):
    return jax.shard_map(
        functools.partial(body, nx=mesh.shape["gx"], ny=mesh.shape["gy"]),
        mesh=mesh,
        in_specs=(
            P("gy", None, "gx"),
            P(None, "gx", "gy", None),
            P("gy"),
            P("gy", None),
            P(None, "gy"),
            P(None, "gx"),
            P("gx", "gy"),
            P("gx", "gy"),
            P("gx", "gy"),
            P("gy", "gx"),
            P("gx", "gy"),
            P("gx", "gy"),
            P("gy", "gx"),
        ),
        out_specs=P("gy", None, "gx"),
        check_vma=False,
    )
```

```python
import functools
import math

import jax
import jax.numpy as jnp
from jax import lax
from jax.experimental import pallas as pl
from jax.experimental.pallas import tpu as pltpu
from jax.sharding import PartitionSpec as P

MESH = pl.DeviceIdType.MESH
F32 = jnp.float32
BF16 = jnp.bfloat16

HEAD_DIM = 256
WINDOW = 4096
PAGE = 128
BEAM = 8
STEPS = 4
ROWS = BEAM * STEPS
EPSILON = 1e-06
SOFT_CAP = 50.0
ROPE_BASE = 10000.0
MAIN = 128
REST = 16

QKV_ROWS = 144
A_ROWS = 160
OUT_AT = 0
OUT_REST_AT = 64
B_ROWS = 80
GATE_AT = 0
NARROW_AT = 576
DOWN_AT = 720
F_ROWS = 1008
CUT = 512
DEN_ROWS = 40


def capped(scores):
    return jnp.exp(SOFT_CAP * jnp.tanh(scores * (1.0 / SOFT_CAP)))


def gelu(v):
    return 0.5 * v * (1.0 + jnp.tanh(math.sqrt(2.0 / math.pi) * (v + 0.044715 * (v * v * v))))


def dot(a, b):
    return jnp.dot(a, b, preferred_element_type=F32)


def dot_nt(a, b):
    return lax.dot_general(a, b, (((1,), (1,)), ((), ())), preferred_element_type=F32)


def layer_kernel(
    nx, ny, width,
    inputs_ref, cache_ref, length_ref, table_ref, parents_ref, gains_ref,
    wq_ref, wk_ref, wv_ref, wo_ref, wg_ref, wu_ref, wd_ref, cosine_ref, sine_ref,
    out_ref,
    inputs_vm, cache, table_vm, parents_vm, gains_vm,
    wq_vm, wk_vm, wv_vm, wo_vm, wg_vm, wu_vm, wd_vm,
    wa_all, wb_all, wf_all, gain_main, gain_rest, x_out, x_in, x_own, row_all, ff_all, norm_in,
    q_out, kv_out, q_in, kv_in, tail_num, tail_den, num_out, num_in, att_out, att_in, part_out,
    part_z, down_z, sum_out, part_x, down_x, last_out, last_in, mixed, sums,
    load_sem, wa_send, wa_recv, wa_core_send, wa_core_recv, ring_send, ring_recv, wf_core_send, wf_core_recv,
    wb_send, wb_recv, wb_core_send, wb_core_recv,
    x_send, x_recv, x_row_send, x_row_recv, row_send, row_recv, q_send, q_recv, kv_send, kv_recv, num_send, num_recv,
    att_send, att_recv, part_send, part_recv, part_x_send, part_x_recv, ff_send, ff_recv,
    down_send, down_recv, down_x_send, down_x_recv, last_send, last_recv,
):
    ys = nx // 2
    zs = ny // 4
    kv_heads = ny // 8
    tiles = nx + nx // 8 if nx >= 8 else nx + 1
    rest_tiles = tiles - nx
    blocks = 8
    row_blocks = blocks // zs
    z_steps = sorted(range(1, zs), key=lambda d: -min(d, zs - d))
    y_steps = sorted(range(1, ys), key=lambda d: -min(d, ys - d))
    i = lax.axis_index("gx")
    j = lax.axis_index("gy")
    y, c = i // 2, i % 2
    sibling = i + 1 - 2 * c
    piece = c * ys + y
    zj, xj = j // 4, j % 4
    chunk = 2 * ((zj + 2 * xj) % ys) + xj % 2
    half = xj // 2

    def group_of(part):
        x_r = 2 * part + c
        return ((y + 8 * ys - 2 * x_r) % ys) * 4 + x_r

    shift = (y + 8 * ys - 2 * c - 1) % ys if zs == 8 else 0
    first_block = row_blocks * ((zj + zs - shift) % zs)
    share = nx // 4
    my_part = first_block // 4
    home = chunk == i
    own_rows = home & (my_part == half) & (piece // share == xj)
    tail_stride = nx // kv_heads

    def row_of(block):
        there = (chunk // 2 + 8 * ys - 2 * (chunk % 2) - 1) % ys if zs == 8 else 0
        return (block + there) % zs

    def remote(src, dst, send_sem, recv_sem, tx, ty):
        return pltpu.make_async_remote_copy(
            src_ref=src, dst_ref=dst, send_sem=send_sem, recv_sem=recv_sem,
            device_id=(tx, ty), device_id_type=MESH,
        )

    def put(src, dst, send_sem, recv_sem, tx, ty):
        own = (tx == i) & (ty == j)

        @pl.when(jnp.logical_not(own))
        def _():
            remote(src, dst, send_sem, recv_sem, tx, ty).start()

        @pl.when(own)
        def _():
            pltpu.make_async_copy(src, dst, recv_sem).start()

    def take(ref, sem):
        pltpu.make_async_copy(ref, ref, sem).wait()

    def take_sent(ref, count, sem, own, fewer=1):
        @pl.when(own)
        def _():
            take(ref.at[pl.ds(0, count - fewer)], sem)

        @pl.when(jnp.logical_not(own))
        def _():
            take(ref.at[pl.ds(0, count)], sem)

    loads = [
        pltpu.make_async_copy(src, dst, load_sem.at[k])
        for k, (src, dst) in enumerate([
            (inputs_ref, inputs_vm), (wq_ref, wq_vm), (wk_ref, wk_vm), (wv_ref, wv_vm), (gains_ref, gains_vm),
            (wo_ref, wo_vm), (wg_ref, wg_vm), (wu_ref, wu_vm), (wd_ref, wd_vm),
            (table_ref, table_vm), (parents_ref, parents_vm), (cache_ref, cache),
        ])
    ]
    for load in loads:
        load.start()

    barrier = pltpu.get_barrier_semaphore()

    def hello(tx, ty):
        pl.semaphore_signal(barrier, inc=1, device_id=(tx, ty), device_id_type=MESH)

    group = group_of(my_part)

    for m in range(share):
        p = share * xj + m
        to = 2 * (p % ys) + p // ys

        @pl.when(jnp.logical_not((to == i) & (group == j)))
        def _():
            hello(to, group)

    for step in range(1, ys):
        hello(2 * ((y + step) % ys) + c, j)
    hello(sibling, j)
    for step in range(1, zs):
        hello(i, 4 * ((zj + step) % zs) + xj)
    for step in range(1, 4):
        hello(i, 4 * zj + (xj + step) % 4)
    waits = ys + (zs - 1) + 3 + 4 // row_blocks - jnp.where(own_rows, 1, 0)

    loads[0].wait()
    for q in range(4):
        v = jnp.concatenate([inputs_vm[2 * q].astype(F32), inputs_vm[2 * q + 1].astype(F32)], axis=0)
        v = jnp.concatenate([v, jnp.zeros((8, MAIN - REST), F32)], axis=1)
        x_out[q] = v.astype(BF16)
    pl.semaphore_wait(barrier, waits)
    for q in range(4):
        block = half * 4 + q
        put(
            x_out.at[q], x_in.at[piece, block % row_blocks], x_send, x_recv,
            chunk, 4 * row_of(block // row_blocks) + piece // share,
        )
    for load in loads[1:5]:
        load.wait()
    v = jnp.concatenate([wq_vm[...].astype(F32), wk_vm[...].astype(F32), wv_vm[...].astype(F32)], axis=0)
    wa_all[c, y, 0:MAIN, :] = v[:, 0:MAIN].T.astype(BF16)
    v = jnp.concatenate([v[:, MAIN:], jnp.zeros((128, MAIN - REST), F32)], axis=1).T
    wa_all[c, y, MAIN:QKV_ROWS, :] = v[0:REST].astype(BF16)
    v = 1.0 + gains_vm[...]
    v = jnp.concatenate([v, jnp.zeros((4, MAIN - REST), F32)], axis=1)
    v = jnp.concatenate([v[:, 0:MAIN], v[:, MAIN:]], axis=0)
    high = v.astype(BF16).astype(F32)
    wa_all[c, y, QKV_ROWS:A_ROWS, :] = jnp.concatenate([high, v - high], axis=0).astype(BF16)
    for step in y_steps:
        remote(wa_all.at[c, y], wa_all.at[c, y], wa_send, wa_recv, 2 * ((y + step) % ys) + c, j).start()

    right = 2 * ((y + 1) % ys) + c
    left = 2 * ((y + ys - 1) % ys) + c
    last_step = ys // 2

    def ring_refs(step):
        from_left = (y + ys - (step - 1)) % ys
        from_right = (y + (step - 1)) % ys
        return from_left, from_right

    def ring_start(step):
        a, b = ring_refs(step)
        src_a, src_b = wf_all.at[c, a], wf_all.at[c, b]
        if step == last_step:
            src_a, src_b = src_a.at[pl.ds(0, CUT)], src_b.at[pl.ds(CUT, F_ROWS - CUT)]
        remote(src_a, src_a, ring_send.at[2 * step - 2], ring_recv.at[2 * step - 2], right, j).start()
        remote(src_b, src_b, ring_send.at[2 * step - 1], ring_recv.at[2 * step - 1], left, j).start()

    def to_sibling(k):
        remote(wf_all.at[c, k], wf_all.at[c, k], wf_core_send, wf_core_recv, sibling, j).start()

    def ring_take(step):
        a = (y + ys - step) % ys
        b = (y + step) % ys
        ref_a, ref_b = wf_all.at[c, a], wf_all.at[c, b]
        if step == last_step:
            take(ref_a.at[pl.ds(0, CUT)], ring_recv.at[2 * step - 2])
            take(ref_b.at[pl.ds(CUT, F_ROWS - CUT)], ring_recv.at[2 * step - 1])
            to_sibling(a)
        else:
            take(ref_a, ring_recv.at[2 * step - 2])
            take(ref_b, ring_recv.at[2 * step - 1])
            ring_start(step + 1)
            to_sibling(a)
            to_sibling(b)

    def rest_sum(pieces):
        out = []
        for t in range(rest_tiles):
            total = None
            for k in range(min(8, nx)):
                v = pieces[8 * t + k]
                v = pltpu.roll(v, REST * k, 1) if k else v
                total = v if total is None else total + v
            out.append(total)
        return out

    for load in loads[5:9]:
        load.wait()
    own_b = wb_all.at[c, y]
    own_b[OUT_AT:OUT_REST_AT, :] = wo_vm[:, 0:MAIN]
    v = jnp.concatenate([wo_vm[:, MAIN:].astype(F32), jnp.zeros((64, MAIN - REST), F32)], axis=1)
    v = jnp.concatenate([v, jnp.zeros((64, MAIN), F32)], axis=0).T
    own_b[OUT_REST_AT:B_ROWS, :] = v[0:REST].astype(BF16)
    for step in y_steps:
        remote(own_b, own_b, wb_send, wb_recv, 2 * ((y + step) % ys) + c, j).start()
    own_f = wf_all.at[c, y]
    for n in range(2):
        at = slice(MAIN * n, MAIN * (n + 1))
        own_f[GATE_AT + 144 * n:GATE_AT + 144 * (n + 1), :] = wg_vm[:, at]
        own_f[GATE_AT + 144 * (n + 2):GATE_AT + 144 * (n + 3), :] = wu_vm[:, at]
        own_f[DOWN_AT + 144 * n:DOWN_AT + 144 * (n + 1), :] = wd_vm[:, at]
    v = [w[:, 256:288].astype(F32) for w in (wg_vm, wu_vm, wd_vm)] + [jnp.zeros((144, 32), F32)]
    own_f[NARROW_AT:DOWN_AT, :] = jnp.concatenate(v, axis=1).astype(BF16)
    ring_start(1)
    to_sibling(y)

    def spread(ref, send_sem, recv_sem):
        src = ref.at[pl.ds(first_block, row_blocks)]
        for step in z_steps:
            remote(src, src, send_sem, recv_sem, i, 4 * ((zj + step) % zs) + xj).start()

    quarter = x_in.at[pl.ds(share * xj, share)]
    take(quarter, x_recv)
    for step in range(1, 4):
        remote(quarter, quarter, x_row_send, x_row_recv, i, 4 * zj + (xj + step) % 4).start()
    take(x_in.at[pl.ds(0, 3 * share)], x_row_recv)
    for b in range(row_blocks):
        rests = []
        for p in range(nx):
            v = x_in[p, b].astype(F32)
            x_own[b, :, MAIN * p:MAIN * (p + 1)] = v[:, 0:MAIN]
            rests.append(v[:, MAIN:2 * MAIN])
        for t, v in enumerate(rest_sum(rests)):
            x_own[b, :, MAIN * (nx + t):MAIN * (nx + t + 1)] = v
        row_all[first_block + b] = x_own[b].astype(BF16)
    spread(row_all, row_send, row_recv)

    take(wa_all.at[c, pl.ds(0, ys - 1)], wa_recv)
    remote(wa_all.at[c], wa_all.at[c], wa_core_send, wa_core_recv, sibling, j).start()
    take(wa_all.at[1 - c], wa_core_recv)
    rests = []
    for p in range(nx):
        v = wa_all[p // ys, p % ys, QKV_ROWS:A_ROWS, :].astype(F32)
        v = v[0:8] + v[8:16]
        gain_main[p] = v
        rests.append(v)
    for t, v in enumerate(rest_sum(rests)):
        gain_rest[t] = v

    def gain(which, t):
        if t < nx:
            return gain_main[t, which:which + 1, :]
        return gain_rest[t - nx, 4 + which:5 + which, :]

    take(row_all.at[pl.ds(0, blocks - row_blocks)], row_recv)

    def chunk_tile(ref, t):
        at = slice(MAIN * t, MAIN * (t + 1))
        return jnp.concatenate([ref[k, :, at].astype(F32) for k in range(blocks)], axis=0)

    total = None
    for t in range(tiles):
        v = chunk_tile(row_all, t)
        total = v * v if total is None else total + v * v
    scale = lax.rsqrt(jnp.sum(total, axis=1, keepdims=True) / width + EPSILON)
    for t in range(tiles):
        v = chunk_tile(row_all, t)
        norm_in[:, MAIN * t:MAIN * (t + 1)] = (v * scale * gain(0, t)).astype(BF16)
    main_w = wa_all[:, :, 0:MAIN, :].reshape(nx * MAIN, 128)
    rest_w = wa_all[:, :, MAIN:QKV_ROWS, :].reshape(nx * REST, 128)
    qkv = dot(norm_in[:, 0:nx * MAIN], main_w) + dot(norm_in[:, nx * MAIN:nx * MAIN + nx * REST], rest_w)
    lane_half = lax.broadcasted_iota(jnp.int32, (ROWS // 2, 128), 1) < 64
    for part in range(2):
        first, second = qkv[ROWS * part:ROWS * part + 16], qkv[ROWS * part + 16:ROWS * (part + 1)]
        q_out[part] = jnp.where(lane_half, first, pltpu.roll(second, 64, 1)).astype(BF16)
        kv_out[part] = jnp.where(lane_half, pltpu.roll(first, 64, 1), second).astype(BF16)
    for part in range(2):
        put(kv_out.at[part], kv_in.at[j % 8], kv_send, kv_recv, tail_stride * (j // 8), group_of(part))
    for part in range(2):
        group = group_of(part)

        @pl.loop(0, nx)
        def _(step):
            put(q_out.at[part], q_in.at[j], q_send, q_recv, (i + 2 * j + step) % nx, group)

    take(wb_all.at[c, pl.ds(0, ys - 1)], wb_recv)
    remote(wb_all.at[c], wb_all.at[c], wb_core_send, wb_core_recv, sibling, j).start()
    row = lax.broadcasted_iota(jnp.int32, (ROWS, 1), 0)
    row_step, row_beam = row & 3, jnp.right_shift(row, 2)
    for load in loads[9:12]:
        load.wait()
    length = jnp.full((1, 1), length_ref[0], jnp.int32)
    first_page = jnp.right_shift(jnp.maximum(length - (WINDOW - 1), 0), 7).astype(F32)
    length_wide = length.astype(F32)
    page_iota = lax.broadcasted_iota(jnp.int32, table_vm.shape, 1).astype(F32)
    lane = lax.broadcasted_iota(jnp.int32, (ROWS, PAGE), 1)
    lane_wide = lane.astype(F32)
    lowest = row_step.astype(F32) - (WINDOW - 1)
    masks = []
    for slot in range(4):
        match = table_vm[...] == i * 4 + slot
        page = jnp.sum(jnp.where(match, page_iota, 0.0), axis=1, keepdims=True)
        used = jnp.sum(jnp.where(match, 1.0, 0.0), axis=1, keepdims=True)
        start = jnp.where(used > 0.5, (first_page + page) * PAGE - length_wide, 1.0)
        place = start + lane_wide
        mask = jnp.where((place < 0.0) & (place >= lowest), 1.0, 0.0)
        masks.append(jnp.concatenate([mask, mask], axis=0) > 0.5)
    key_lane = lax.broadcasted_iota(jnp.int32, (ROWS, ROWS), 1)
    key_step, key_beam = key_lane & 3, jnp.right_shift(key_lane, 2)
    beam_lane = lax.broadcasted_iota(jnp.int32, (ROWS, BEAM), 1)
    current = row_beam
    tail = jnp.zeros((ROWS, ROWS), F32)
    for at in range(STEPS - 1, -1, -1):
        hit = (key_step == at) & (row_step >= at) & (key_beam == current)
        tail = jnp.where(hit, 1.0, tail)
        if at:
            chosen = jnp.where(beam_lane == current, parents_vm[at - 1:at, :].astype(F32), 0.0)
            parent = jnp.sum(chosen, axis=1, keepdims=True).astype(jnp.int32)
            current = jnp.where(row_step >= at, parent, current)
    tail_mask = jnp.concatenate([tail, tail], axis=0) > 0.5

    cosine = jnp.concatenate([cosine_ref[...]] * BEAM, axis=0)
    sine = jnp.concatenate([sine_ref[...]] * BEAM, axis=0)
    take(q_in, q_recv)

    def query_tile(at):
        first, second = q_in[at].astype(F32), q_in[at + 1].astype(F32)
        upper = jnp.where(lane_half, first, pltpu.roll(second, 64, 1))
        lower = jnp.where(lane_half, pltpu.roll(first, 64, 1), second)
        return jnp.concatenate([upper, lower], axis=0)

    def kv_tile(source, at):
        total = None
        for m in range(4):
            v = kv_in[source + m].astype(F32)
            v = jnp.concatenate([v, pltpu.roll(v, 64, 1)], axis=0)
            shift = (32 * m - at) % 128
            v = pltpu.roll(v, shift, 1) if shift else v
            total = v if total is None else jnp.where(lane >= 32 * m, v, total)
        return total

    def rotated(u, w):
        return u * cosine - w * sine, w * cosine + u * sine

    def wide(u, w):
        return jnp.concatenate([u, w], axis=1)

    def query_of(h):
        qs = []
        for g in range(2):
            base = 4 * (2 * h + g)
            qs.append(wide(*rotated(query_tile(base), query_tile(base + 2))) * HEAD_DIM ** -0.5)
        return jnp.concatenate(qs, axis=0).astype(BF16)

    tail_num[...] = jnp.zeros(tail_num.shape, F32)
    tail_den[...] = jnp.zeros(tail_den.shape, F32)

    @pl.when(i % tail_stride == 0)
    def _():
        h = i // tail_stride
        take(kv_in, kv_recv)
        key = wide(*rotated(kv_tile(0, 0), kv_tile(4, 0))).astype(BF16)
        value = wide(kv_tile(0, 32), kv_tile(4, 32)).astype(BF16)
        weights = jnp.where(tail_mask, capped(dot_nt(query_of(h), key)), 0.0)
        tail_den[h] = jnp.broadcast_to(jnp.sum(weights, axis=1, keepdims=True), (2 * ROWS, 128))
        tail_num[h] = dot(weights.astype(BF16), value)

    for h in range(kv_heads):
        query = query_of(h)
        den = tail_den[h, :, 0:1]
        num = tail_num[h]
        for slot in range(4):
            at = slice(HEAD_DIM * h, HEAD_DIM * (h + 1))
            weights = jnp.where(masks[slot], capped(dot_nt(query, cache[0, slot, :, at])), 0.0)
            den = den + jnp.sum(weights, axis=1, keepdims=True)
            num = num + dot(weights.astype(BF16), cache[1, slot, :, at])
        den_high = den.astype(BF16).astype(F32)
        den_low = den - den_high
        for g in range(2):
            rows = slice(ROWS * g, ROWS * (g + 1))
            both = jnp.where(lane == row, den_high[rows], 0.0) + jnp.where(lane == row + ROWS, den_low[rows], 0.0)
            both = jnp.broadcast_to(jnp.sum(both, axis=0, keepdims=True), (8, 128))
            for t in range(2):
                v = jnp.concatenate([num[rows, 128 * t:128 * (t + 1)], both], axis=0)
                num_out[2 * (2 * h + g) + t] = v.astype(BF16)

    for step in y_steps + [0]:
        for core in range(2):
            to = 2 * ((y + step) % ys) + (c + core) % 2
            if step or core:
                remote(num_out.at[to], num_in.at[i], num_send, num_recv, to, j).start()

    pltpu.make_async_copy(num_out.at[i], num_in.at[i], num_recv).start()
    take(num_in, num_recv)
    total = None
    for p in range(nx):
        v = num_in[p].astype(F32)
        total = v if total is None else total + v
    both = jnp.where((lane == row) | (lane == row + ROWS), total[ROWS:ROWS + 1], 0.0)
    total = total[0:ROWS] / jnp.sum(both, axis=1, keepdims=True)
    att_out[0] = total.astype(BF16)
    for k in range(2):
        put(att_out.at[0], att_in.at[half], att_send, att_recv, chunk, 2 * i + k)
    if last_step > 1:
        ring_take(1)

    take(att_in, att_recv)
    attended = []
    for part in range(2):
        v = att_in[part].astype(F32)
        attended.append(jnp.where(j % 2 == 1, pltpu.roll(v, 64, 1), v)[:, 0:64])
    attended = jnp.concatenate(attended, axis=0).astype(BF16)
    take(wb_all.at[1 - c], wb_core_recv)

    def put_partial(which, t, v):
        for k in range(blocks):
            part_out[which, k, :, MAIN * t:MAIN * (t + 1)] = v[8 * k:8 * (k + 1)].astype(BF16)

    def put_rest(which, v):
        if v.shape[1] < 128:
            v = jnp.concatenate([v, jnp.zeros((v.shape[0], 128 - v.shape[1]), F32)], axis=1)
        for t in range(rest_tiles):
            put_partial(which, nx + t, v[:, 128 * t:128 * (t + 1)])

    for p in range(nx):
        put_partial(0, p, dot(attended, wb_all[p // ys, p % ys, OUT_AT:OUT_REST_AT, :]))
    rest_w = wb_all[:, :, OUT_REST_AT:B_ROWS, :].reshape(nx * REST, 128)
    put_rest(0, dot_nt(attended, rest_w[:, 0:64]))

    def send_partial(which, dst_all, send_sem, recv_sem):
        for step in z_steps:
            to = (zj + step) % zs
            src = part_out.at[which, pl.ds(row_blocks * ((to + zs - shift) % zs), row_blocks)]
            remote(src, dst_all.at[step - 1], send_sem, recv_sem, i, 4 * to + xj).start()

    def add_z(which, ref, dst_all, send_sem, recv_sem):
        for b in range(row_blocks):
            for t in range(tiles):
                at = slice(MAIN * t, MAIN * (t + 1))
                total = part_out[which, first_block + b, :, at].astype(F32)
                for s in range(zs - 1):
                    total = total + ref[s, b, :, at].astype(F32)
                sums[b, :, at] = total
            sum_out[which, b] = sums[b].astype(BF16)
        for step in range(1, 4):
            remote(
                sum_out.at[which], dst_all.at[step - 1], send_sem, recv_sem, i, 4 * zj + (xj + step) % 4
            ).start()

    def add_x(ref, b):
        square = None
        for t in range(tiles):
            at = slice(MAIN * t, MAIN * (t + 1))
            v = sums[b, :, at]
            for s in range(3):
                v = v + ref[s, b, :, at].astype(F32)
            sums[b, :, at] = v
            square = v * v if square is None else square + v * v
        return lax.rsqrt(jnp.sum(square, axis=1, keepdims=True) / width + EPSILON)

    send_partial(0, part_z, part_send, part_recv)
    if last_step > 2:
        ring_take(2)
    take(part_z, part_recv)
    add_z(0, part_z, part_x, part_x_send, part_x_recv)
    for step in range(3, last_step):
        ring_take(step)
    take(part_x, part_x_recv)
    for b in range(row_blocks):
        scale = add_x(part_x, b)
        square = None
        for t in range(tiles):
            at = slice(MAIN * t, MAIN * (t + 1))
            v = x_own[b, :, at] + sums[b, :, at] * scale * gain(1, t)
            mixed[b, :, at] = v
            square = v * v if square is None else square + v * v
        scale = lax.rsqrt(jnp.sum(square, axis=1, keepdims=True) / width + EPSILON)
        for t in range(tiles):
            at = slice(MAIN * t, MAIN * (t + 1))
            sums[b, :, at] = mixed[b, :, at] * scale * gain(2, t)
        ff_all[first_block + b] = sums[b].astype(BF16)
    spread(ff_all, ff_send, ff_recv)
    ring_take(last_step)
    take(wf_all.at[1 - c], wf_core_recv)

    take(ff_all.at[pl.ds(0, blocks - row_blocks)], ff_recv)
    for t in range(tiles):
        norm_in[:, MAIN * t:MAIN * (t + 1)] = chunk_tile(ff_all, t).astype(BF16)
    main_x = norm_in[:, 0:nx * MAIN]
    rest_x = norm_in[:, nx * MAIN:nx * MAIN + nx * REST]

    def ff_part(n):
        at = GATE_AT + 144 * n
        main_w = wf_all[:, :, at:at + MAIN, :].reshape(nx * MAIN, 128)
        rest_w = wf_all[:, :, at + MAIN:at + 144, :].reshape(nx * REST, 128)
        return dot(main_x, main_w) + dot(rest_x, rest_w)

    hidden = [(gelu(ff_part(n)) * ff_part(n + 2)).astype(BF16) for n in range(2)]
    both = ff_part(4)
    narrow = gelu(both) * pltpu.roll(both, 96, 1)
    lane_chunk = lax.broadcasted_iota(jnp.int32, narrow.shape, 1)
    narrow = pltpu.roll(jnp.where(lane_chunk < 32, narrow, 0.0), 64, 1)
    hidden.append(narrow.astype(BF16))
    places = [DOWN_AT, DOWN_AT + 144, NARROW_AT]
    for p in range(nx):
        v = None
        for h, at in zip(hidden, places):
            term = dot_nt(h, wf_all[p // ys, p % ys, at:at + MAIN, :])
            v = term if v is None else v + term
        put_partial(1, p, v)
    v = None
    for h, at in zip(hidden, places):
        rest_w = wf_all[:, :, at + MAIN:at + 144, :].reshape(nx * REST, 128)
        term = dot_nt(h, rest_w)
        v = term if v is None else v + term
    put_rest(1, v)
    send_partial(1, down_z, down_send, down_recv)
    take(down_z, down_recv)
    add_z(1, down_z, down_x, down_x_send, down_x_recv)
    take(down_x, down_x_recv)

    for b in range(row_blocks):
        scale = add_x(down_x, b)

        def result(t):
            at = slice(MAIN * t, MAIN * (t + 1))
            return mixed[b, :, at] + sums[b, :, at] * scale * gain(3, t)

        for p in range(nx):
            v = result(nx + p // 8)
            shift = (128 - REST * (p % 8)) % 128
            v = pltpu.roll(v, shift, 1) if shift else v
            last_out[b, p] = jnp.concatenate([result(p), v], axis=1).astype(BF16)
        for m in range(share):
            p = share * xj + m
            to = 2 * (p % ys) + p // ys
            put(
                last_out.at[b, p], last_in.at[(first_block + b) % 4], last_send, last_recv,
                to, group_of(my_part),
            )

    take(last_in, last_recv)
    for q in range(4):
        v = last_in[q].astype(F32)
        out_ref[2 * q] = v[0:STEPS, 0:144].astype(BF16)
        out_ref[2 * q + 1] = v[STEPS:8, 0:144].astype(BF16)

    x_sent = last_out.at[0]
    take_sent(x_sent, 4, x_send, own_rows, row_blocks)
    take(x_in.at[pl.ds(0, 3 * share)], x_row_send)
    take(wa_all.at[c, pl.ds(0, ys - 1)], wa_send)
    take(wa_all.at[c], wa_core_send)
    take(wb_all.at[c, pl.ds(0, ys - 1)], wb_send)
    take(wb_all.at[c], wb_core_send)
    for step in range(1, last_step + 1):
        for side in range(2):
            rows = pl.ds(0, F_ROWS) if step < last_step else pl.ds(CUT * side, F_ROWS - CUT if side else CUT)
            take(wf_all.at[0, 0, rows], ring_send.at[2 * step - 2 + side])
    take(wf_all.at[c], wf_core_send)
    take_sent(q_in, ny, q_send, home)
    take_sent(kv_out, 2, kv_send, home & (i == tail_stride * (j // 8)))
    take(num_out.at[pl.ds(0, nx - 1)], num_send)
    take_sent(att_in, 2, att_send, home & (j // 2 == i))
    take(row_all.at[pl.ds(0, (zs - 1) * row_blocks)], row_send)
    take(ff_all.at[pl.ds(0, (zs - 1) * row_blocks)], ff_send)
    take(part_z, part_send)
    take(down_z, down_send)
    take(part_x, part_x_send)
    take(down_x, down_x_send)
    take_sent(x_sent, row_blocks * share, last_send, own_rows, row_blocks)


def body(
    inputs, cache_pool, lengths, block_table, parents, norm_gains,
    w_query, w_key, w_value, w_out, w_gate, w_up, w_down, *, nx, ny,
):
    columns = inputs.shape[2]
    tiles = nx + max(nx // 8, 1)
    rest_tiles = tiles - nx
    span = tiles * MAIN
    ys = nx // 2
    last_step = ys // 2
    zs = ny // 4
    row_blocks = 8 // zs

    frequency = ROPE_BASE ** (-jnp.arange(128, dtype=F32) * 2.0 / HEAD_DIM)
    positions = lengths[0] + jnp.arange(STEPS, dtype=jnp.int32)
    angles = positions[:, None].astype(F32) * frequency

    arrays = (
        inputs, cache_pool, lengths, block_table, parents, norm_gains,
        w_query.T, w_key.T, w_value.T, w_out, w_gate, w_up, w_down.T, jnp.cos(angles), jnp.sin(angles),
    )
    vmem = pl.BlockSpec(memory_space=pltpu.VMEM)
    specs = [pl.BlockSpec(memory_space=pltpu.HBM) for _ in arrays]
    specs[2] = pl.BlockSpec(memory_space=pltpu.SMEM)
    specs[13:15] = [vmem, vmem]
    dma = pltpu.SemaphoreType.DMA

    def held(*shape, dtype=BF16):
        return pltpu.VMEM(shape, dtype)

    out = pl.pallas_call(
        functools.partial(layer_kernel, nx, ny, nx * columns),
        name="layer",
        out_shape=jax.ShapeDtypeStruct(inputs.shape, BF16),
        in_specs=specs,
        out_specs=vmem,
        scratch_shapes=[pltpu.VMEM(arrays[k].shape, arrays[k].dtype) for k in (0, 1, 3, 4, 5, 6, 7, 8, 9, 10, 11, 12)]
        + [
            held(2, ys, A_ROWS, 128),
            held(2, ys, B_ROWS, 128),
            held(2, ys, F_ROWS, 128),
            held(nx, 8, 128, dtype=F32),
            held(rest_tiles, 8, 128, dtype=F32),
            held(4, 8, 256),
            held(nx, row_blocks, 8, 256),
            held(row_blocks, 8, span, dtype=F32),
            held(8, 8, span),
            held(8, 8, span),
            held(64, span),
            held(2, ROWS // 2, 128),
            held(2, ROWS // 2, 128),
            held(ny, ROWS // 2, 128),
            held(8, ROWS // 2, 128),
            held(ny // 8, 2 * ROWS, HEAD_DIM, dtype=F32),
            held(ny // 8, 2 * ROWS, 128, dtype=F32),
            held(nx, DEN_ROWS, 128),
            held(nx, DEN_ROWS, 128),
            held(1, ROWS, 128),
            held(2, ROWS, 128),
            held(2, 8, 8, span),
            held(zs - 1, row_blocks, 8, span),
            held(zs - 1, row_blocks, 8, span),
            held(2, row_blocks, 8, span),
            held(3, row_blocks, 8, span),
            held(3, row_blocks, 8, span),
            held(row_blocks, 16, 8, 256),
            held(4, 8, 256),
            held(row_blocks, 8, span, dtype=F32),
            held(row_blocks, 8, span, dtype=F32),
        ]
        + [dma((12,))] + [dma(())] * 4
        + [dma((2 * last_step,)), dma((2 * last_step,))]
        + [dma(())] * 32,
        compiler_params=pltpu.CompilerParams(collective_id=0, has_side_effects=True, vmem_limit_bytes=60 << 20),
    )(*arrays)
    return out


def solution(mesh):
    return jax.shard_map(
        functools.partial(body, nx=mesh.shape["gx"], ny=mesh.shape["gy"]),
        mesh=mesh,
        in_specs=(
            P("gy", None, "gx"),
            P(None, "gx", "gy", None),
            P("gy"),
            P("gy", None),
            P(None, "gy"),
            P(None, "gx"),
            P("gx", "gy"),
            P("gx", "gy"),
            P("gx", "gy"),
            P("gy", "gx"),
            P("gx", "gy"),
            P("gx", "gy"),
            P("gy", "gx"),
        ),
        out_specs=P("gy", None, "gx"),
        check_vma=False,
    )
```
